256 devices in a mesh: group: 32 (over x, y, core), mp: 8 (over z).
Axes of the slice: x: 4, y: 4, z: 8, core: 2. Of those that a mesh axis runs over, the one named last changes fastest.
Arguments:
- hidden: bfloat16 [16384, 1792], P('group')
- norm_gain: float32 [1792], replicated, may hold values from 0.1 to 1.9
- qkv_weight: bfloat16 [1792, 2304], P(None, 'mp'), may hold values from -0.125 to 0.125
- out_weight: bfloat16 [1792, 1792], P('mp'), may hold values from -0.125 to 0.125
- adapter_down: bfloat16 [1792, 1024], P(None, 'mp'), may hold values from -0.125 to 0.125
- adapter_up: bfloat16 [1024, 1792], P('mp'), may hold values from -1.5 to 1.5
- vocab_rows: bfloat16 [4096, 1792], P(('group', 'mp')), may hold values from -0.125 to 0.125
- segments: int32 [16384], P('group'), may hold values from 0 to 127, never falling along the last dimension, each value on 1 to 512 neighbouring positions
- request_adapter: int32 [128], replicated, may hold values from 0 to 63
- adapter_slot: int32 [64], replicated, may hold values from 0 to 63, each once
- page_table: int32 [2048], replicated, may hold values from 0 to 2047, as said below
Outputs:
- layer_update: bfloat16 [16384, 1792], P('group', 'mp')
- state_norms: float32 [16, 16384], P('mp', 'group')
- max_logits: float32 [16384], P(('group', 'mp'))
The draws below stay inside these ranges and needn't reach their ends.
Inputs may be any that keep to these rules, and one draw needn't show every extreme that they name: A permutation of all pages. Logical page k of group g (entry g * 64 + k) lies in group page_table[g * 64 + k] // 64, and every group holds exactly two of the logical pages of every group. `segments`: every request's tokens stand together and in order; no request has more than 512 tokens. `adapter_slot`: A permutation.
All inputs are finite; a program needn't handle non-finite values.
Results may differ from the reference program's by a relative error of at most 0.013.
Values may be sent and summed in bfloat16 or wider, within the bound.
A program may use at most 64 MiB of HBM per device.

```python
import math
import jax
import jax.numpy as jnp
import numpy as np
from jax import lax

D = 1792
HEADS = 16
FEAT = 16
HD = 112
PHI = 273
RANK = 16
ADAPT_DEV = 8
ADAPTERS = 64
ROWS = 512
REQS = 128
TOKENS = 16384
PAGES_DEV = 64
PAGE = 8
ALL_PAGES = 2048
VOCAB = 4096
N_MP = 8


def draw_hidden(key, part):
    key_rows, key_cols, key_base = jax.random.split(key, 3)
    row_scale = jnp.exp(jax.random.uniform(key_rows, (TOKENS, 1), jnp.float32, -1.15, 1.15))
    col_scale = jnp.exp(jax.random.uniform(key_cols, (1, D), jnp.float32, -1.15, 1.15))
    pattern = jnp.clip(jax.random.normal(key_base, (TOKENS, D), jnp.float32), -5.0, 5.0)
    return (pattern * row_scale * col_scale).astype(jnp.bfloat16)


def draw_page_table(key, part):
    groups = ALL_PAGES // PAGES_DEV
    key_source, key_slot = jax.random.split(key)
    pattern = jnp.arange(PAGES_DEV, dtype=jnp.int32) % groups
    holders = jax.vmap(lambda sub: jax.random.permutation(sub, pattern))(jax.random.split(key_source, groups))
    sources = holders.reshape(-1)
    onehot = (sources[:, None] == jnp.arange(groups, dtype=jnp.int32)[None, :]).astype(jnp.int32)
    before = jnp.cumsum(onehot, axis=0) - onehot
    ranking = jnp.sum(before * onehot, axis=1)
    shuffles = jax.vmap(lambda sub: jax.random.permutation(sub, PAGES_DEV))(jax.random.split(key_slot, groups))
    slot_ids = shuffles[sources, ranking]
    return (sources * PAGES_DEV + slot_ids).astype(jnp.int32)


def plant(values, rng, least, high):
    longest = values.shape.index(max(values.shape))
    spots = []
    for shift in (0, 1):
        where = [jax.random.randint(jax.random.fold_in(rng, axis), (), 0, length) for axis, length in enumerate(values.shape)]
        where[longest] = (where[longest] + shift) % values.shape[longest]
        spots.append(tuple(where))
    return values.at[spots[0]].set(least).at[spots[1]].set(high)


def block_scale(stream_key, dims, pieces, smallest, high):
    def one(dim, parts):
        steps = jax.random.uniform(jax.random.fold_in(jax.random.fold_in(stream_key, 6), dim), (parts,), jnp.float32, smallest / len(pieces), high / len(pieces))
        return jnp.repeat(jnp.exp(steps), dims[dim] // parts).reshape((-1,) + (1,) * (len(dims) - dim - 1))

    factor_of = one(*pieces[0])
    for cut in pieces[1:]:
        factor_of = factor_of * one(*cut)
    return factor_of


def cumulative_ranks(number_of, skew):
    weights = [(1 << 20) // math.isqrt(standing ** skew) + 1 for standing in range(1, number_of + 1)]
    width = 1 + sum(weights) // (1 << 30)
    return np.cumsum(np.array([max(1, weight // width) for weight in weights]))


def skewed_ids(own_key, extent, amount, slope):
    table = cumulative_ranks(amount, slope)
    lot = jax.random.randint(jax.random.fold_in(own_key, 1), extent, 0, int(table[amount - 1]))
    rank = jnp.searchsorted(jnp.asarray(table, jnp.int32), lot, side="right")
    return jax.random.permutation(jax.random.fold_in(own_key, 2), amount)[rank].astype(jnp.int32)


def profile(count, total, reach, skew):
    weights = [(1 << 20) // math.isqrt(grade ** skew) + 1 for grade in range(2, count + 1)]
    rest, holding = total - reach - (count - 1), [1] * (count - 1)
    while rest > 0:
        free = [i for i in range(count - 1) if holding[i] < reach]
        mass, left = sum([weights[i] for i in free]), rest
        for i in free:
            addition = min(reach - holding[i], max(1, left * weights[i] // mass), rest)
            holding[i] = holding[i] + addition
            rest = rest - addition
    return np.array([reach] + holding)


def ragged_sizes(rng, amount, total, bound, skew):
    if amount == 2:
        one = jax.random.randint(rng, (), max(1, total - bound), min(bound, total - 1) + 1)
        return jnp.stack([one, total - one])
    sizes = jnp.asarray(profile(amount, total, bound, skew), jnp.int32)
    twos = (amount - 1) // 2
    giver, receiver = sizes[1:1 + 2 * twos:2], sizes[2:2 + 2 * twos:2]
    room = jnp.minimum(giver - 1, bound - receiver)
    shifted = jax.random.randint(jax.random.fold_in(rng, 1), (twos,), 0, 1 << 20) % (room + 1)
    sizes = sizes.at[1:1 + 2 * twos:2].set(giver - shifted).at[2:2 + 2 * twos:2].set(receiver + shifted)
    return sizes[jax.random.permutation(jax.random.fold_in(rng, 2), amount)]


def gaussian(stream_key, shape, scale, bound, cuts=(), held_as=jnp.bfloat16):
    level = block_scale(stream_key, shape, cuts, -0.22, 0.18) if cuts else 1.0
    drawn = jax.random.normal(stream_key, shape, jnp.float32) * scale * level
    return jnp.minimum(jnp.maximum(drawn, -bound), bound).astype(held_as)


def setup_inputs(seed: int = 0) -> dict:
    seeds = jax.random.split(jax.random.key(seed), 12)
    hidden = draw_hidden(jax.random.fold_in(seeds[11], 71), 0)
    norm_gain = jnp.clip(1.0 + 0.18 * jax.random.normal(seeds[1], (D,), jnp.float32), 0.1, 1.9)
    qkv_weight = gaussian(seeds[2], (D, HEADS * (2 * FEAT + HD)), D ** -0.5, 0.125, ((1, 8),))
    out_weight = gaussian(seeds[3], (D, D), D ** -0.5, 0.125, ((0, 8),))
    adapter_down = gaussian(seeds[4], (D, ADAPTERS * RANK), D ** -0.5, 0.125, ((1, 8),))
    adapter_up = gaussian(seeds[5], (ADAPTERS * RANK, D), RANK ** -0.5, 1.5, ((0, 8),))
    vocab_rows = gaussian(seeds[6], (VOCAB, D), D ** -0.5, 0.125, ((0, 256),))
    segments = jnp.searchsorted(jnp.cumsum(ragged_sizes(seeds[7], REQS, TOKENS, ROWS, 2)), jnp.arange(TOKENS), side="right").astype(jnp.int32)
    request_adapter = plant(skewed_ids(seeds[8], (REQS,), ADAPTERS, 2), jax.random.fold_in(seeds[8], 3), 0, ADAPTERS - 1).astype(jnp.int32)
    adapter_slot = jax.random.permutation(seeds[9], ADAPTERS).astype(jnp.int32)
    page_table = draw_page_table(jax.random.fold_in(seeds[11], 71), 0)
    return dict(hidden=hidden, norm_gain=norm_gain, qkv_weight=qkv_weight, out_weight=out_weight, adapter_down=adapter_down, adapter_up=adapter_up, vocab_rows=vocab_rows, segments=segments, request_adapter=request_adapter, adapter_slot=adapter_slot, page_table=page_table)


EPSILON = 1e-05
PRECISE = lax.Precision.HIGHEST

def rms_normed(values, norm_gain):
    wide = values.astype(jnp.float32)
    meansq = lax.optimization_barrier(jnp.mean(wide * wide, axis=-1, keepdims=True))
    return (wide * lax.rsqrt(meansq + EPSILON) * norm_gain.astype(jnp.float32)).astype(jnp.bfloat16)

def features(vectors, feat_width):
    linear_part = vectors / feat_width ** 0.25
    outer_part = (vectors[..., :, None] * vectors[..., None, :]).reshape(vectors.shape[:-1] + (feat_width * feat_width,))
    outer_part = outer_part / (2.0 * feat_width) ** 0.5
    ones_part = jnp.ones(vectors.shape[:-1] + (1,), jnp.float32)
    return jnp.concatenate([ones_part, linear_part, outer_part], axis=-1)

def block_step(state_carry, block_inputs, feat_width):
    states, totals, owner_seg = state_carry
    phi_query, phi_key, query_rows, key_rows, value_rows, seg_ids = block_inputs
    scaling = feat_width ** (-0.5)
    block_len = seg_ids.shape[0]
    position = jnp.arange(block_len, dtype=jnp.int32)
    allowed = ((position[:, None] >= position[None, :]) & (seg_ids[:, None] == seg_ids[None, :])).astype(jnp.float32)
    carried = (seg_ids == owner_seg).astype(jnp.float32)[None, :]
    scores = jnp.einsum('hcf,hdf->hcd', query_rows, key_rows, precision=PRECISE) * scaling
    weights = (1.0 + scores + 0.5 * scores * scores) * allowed[None]
    numerator = jnp.einsum('hcd,hde->hce', weights, value_rows, precision=PRECISE)
    numerator = numerator + carried[..., None] * jnp.einsum('hcp,hpe->hce', phi_query, states, precision=PRECISE)
    denominator = lax.optimization_barrier(jnp.sum(weights, axis=-1)) + carried * jnp.einsum('hcp,hp->hc', phi_query, totals, precision=PRECISE)
    mixed_out = numerator / denominator[..., None]
    key_scores = jnp.einsum('hcf,hdf->hcd', key_rows, key_rows, precision=PRECISE) * scaling
    value_gram = jnp.einsum('hce,hde->hcd', value_rows, value_rows, precision=PRECISE)
    key_gram = (1.0 + key_scores + 0.5 * key_scores * key_scores) * value_gram
    masked_gram = jnp.einsum('cd,hde->hce', allowed, key_gram, precision=PRECISE)
    local_squares = lax.optimization_barrier(jnp.sum(masked_gram * allowed[None], axis=-1))
    along = lax.optimization_barrier(jnp.sum(jnp.einsum('hcp,hpe->hce', phi_key, states, precision=PRECISE) * value_rows, axis=-1))
    cross_squares = jnp.einsum('cd,hd->hc', allowed, along, precision=PRECISE)
    state_squares = lax.optimization_barrier(jnp.sum(states * states, axis=(1, 2)))
    squares = carried * (state_squares[:, None] + 2.0 * cross_squares) + local_squares
    counted = carried * totals[:, :1] + lax.optimization_barrier(jnp.sum(allowed, axis=-1))[None, :]
    state_norm = jnp.sqrt(squares / (counted * (feat_width * value_rows.shape[-1])))
    last_seg = seg_ids[-1]
    member = (seg_ids == last_seg).astype(jnp.float32)
    continues = (owner_seg == last_seg).astype(jnp.float32)
    new_states = continues * states + jnp.einsum('hcp,hce->hpe', phi_key * member[None, :, None], value_rows, precision=PRECISE)
    new_totals = continues * totals + jnp.einsum('hcp,c->hp', phi_key, member, precision=PRECISE)
    return ((new_states, new_totals, last_seg), (mixed_out, state_norm))

def reference(hidden, norm_gain, qkv_weight, out_weight, adapter_down, adapter_up, vocab_rows, segments, request_adapter, adapter_slot, page_table):
    ordered = hidden.reshape(ALL_PAGES, PAGE, D)[page_table].reshape(TOKENS, D)
    normed = rms_normed(ordered, norm_gain)
    projected = jnp.dot(normed, qkv_weight, preferred_element_type=jnp.float32).astype(jnp.bfloat16)
    block_len = min(256, ROWS)
    blocks = TOKENS // block_len
    grouped = projected.reshape(blocks, block_len, HEADS, 2 * FEAT + HD)
    seg_blocks = segments.reshape(blocks, block_len)

    def scan_step(state_carry, block_inputs):
        part_rows, seg_ids = block_inputs
        split_heads = jnp.transpose(part_rows.astype(jnp.float32), (1, 0, 2))
        query_rows = split_heads[..., :FEAT]
        key_rows = split_heads[..., FEAT:2 * FEAT]
        value_rows = split_heads[..., 2 * FEAT:]
        return block_step(state_carry, (features(query_rows, FEAT), features(key_rows, FEAT), query_rows, key_rows, value_rows, seg_ids), FEAT)
    initial = (jnp.zeros((HEADS, PHI, HD), jnp.float32), jnp.zeros((HEADS, PHI), jnp.float32), jnp.int32(-1))
    _, (mixed_out, state_norm) = lax.scan(scan_step, initial, (grouped, seg_blocks))
    attended = jnp.transpose(mixed_out, (0, 2, 1, 3)).reshape(TOKENS, HEADS * HD).astype(jnp.bfloat16)
    state_norms = jnp.transpose(state_norm, (1, 0, 2)).reshape(HEADS, TOKENS)
    adapter_of = request_adapter[segments]
    slot_ids = adapter_slot[adapter_of]
    slot_cols = ADAPT_DEV * RANK
    column_slot = jnp.arange(slot_cols, dtype=jnp.int32) // RANK
    head_cols = D // N_MP
    update = jnp.zeros((TOKENS, D), jnp.float32)
    for block_index in range(N_MP):
        lowered = jnp.dot(normed, adapter_down[:, block_index * slot_cols:(block_index + 1) * slot_cols], preferred_element_type=jnp.float32)
        matches = slot_ids[:, None] - block_index * ADAPT_DEV == column_slot[None, :]
        low_rank = jnp.where(matches, lowered, 0.0).astype(jnp.bfloat16)
        partial_value = jnp.dot(attended[:, block_index * head_cols:(block_index + 1) * head_cols], out_weight[block_index * head_cols:(block_index + 1) * head_cols, :], preferred_element_type=jnp.float32)
        partial_value = partial_value + jnp.dot(low_rank, adapter_up[block_index * slot_cols:(block_index + 1) * slot_cols, :], preferred_element_type=jnp.float32)
        rounded = lax.optimization_barrier(partial_value.astype(jnp.bfloat16))
        update = update + rounded.astype(jnp.float32)
    layer_update = update.astype(jnp.bfloat16)
    final_rows = (ordered.astype(jnp.float32) + layer_update.astype(jnp.float32)).astype(jnp.bfloat16)
    score_block = min(1024, TOKENS)

    def row_best(row_block):
        return lax.optimization_barrier(jnp.max(jnp.dot(row_block, vocab_rows.T, preferred_element_type=jnp.float32), axis=1))
    max_logits = lax.map(row_best, final_rows.reshape(TOKENS // score_block, score_block, D)).reshape(TOKENS)
    return (layer_update, state_norms, max_logits)
```

```python
import jax
import jax.numpy as jnp
from jax import lax
from jax.sharding import PartitionSpec as P

FEAT = 16
HD = 112
RANK = 16


EPSILON = 1e-05
PRECISE = lax.Precision.HIGHEST


def from_behind(value, axis, by):
    size = lax.axis_size(axis)
    pairs = [(i, i + by) for i in range(size) if 0 <= i + by < size]
    return lax.ppermute(value, axis, pairs)


def rms_normed(values, norm_gain):
    wide = values.astype(jnp.float32)
    meansq = jnp.mean(wide * wide, axis=-1, keepdims=True)
    return (wide * lax.rsqrt(meansq + EPSILON) * norm_gain).astype(jnp.bfloat16)


def features(vectors, feat_width):
    linear_part = vectors / feat_width**0.25
    outer_part = (vectors[..., :, None] * vectors[..., None, :]).reshape(
        vectors.shape[:-1] + (feat_width * feat_width,)
    )
    outer_part = outer_part / (2.0 * feat_width) ** 0.5
    ones_part = jnp.ones(vectors.shape[:-1] + (1,), jnp.float32)
    return jnp.concatenate([ones_part, linear_part, outer_part], axis=-1)


def block_step(state_carry, block_inputs, feat_width):
    states, totals, owner_seg = state_carry
    phi_query, phi_key, query_rows, key_rows, value_rows, seg_ids = block_inputs
    scaling = feat_width ** (-0.5)
    block_len = seg_ids.shape[0]
    position = jnp.arange(block_len, dtype=jnp.int32)
    allowed = (
        (position[:, None] >= position[None, :]) & (seg_ids[:, None] == seg_ids[None, :])
    ).astype(jnp.float32)
    carried = (seg_ids == owner_seg).astype(jnp.float32)[None, :]
    scores = jnp.einsum("hcf,hdf->hcd", query_rows, key_rows, precision=PRECISE) * scaling
    weights = (1.0 + scores + 0.5 * scores * scores) * allowed[None]
    numerator = jnp.einsum("hcd,hde->hce", weights, value_rows, precision=PRECISE)
    numerator = numerator + carried[..., None] * jnp.einsum(
        "hcp,hpe->hce", phi_query, states, precision=PRECISE
    )
    denominator = jnp.sum(weights, axis=-1) + carried * jnp.einsum(
        "hcp,hp->hc", phi_query, totals, precision=PRECISE
    )
    mixed_out = numerator / denominator[..., None]
    key_scores = jnp.einsum("hcf,hdf->hcd", key_rows, key_rows, precision=PRECISE) * scaling
    value_gram = jnp.einsum("hce,hde->hcd", value_rows, value_rows, precision=PRECISE)
    key_gram = (1.0 + key_scores + 0.5 * key_scores * key_scores) * value_gram
    masked_gram = jnp.einsum("cd,hde->hce", allowed, key_gram, precision=PRECISE)
    local_squares = jnp.sum(masked_gram * allowed[None], axis=-1)
    along = jnp.sum(
        jnp.einsum("hcp,hpe->hce", phi_key, states, precision=PRECISE) * value_rows, axis=-1
    )
    cross_squares = jnp.einsum("cd,hd->hc", allowed, along, precision=PRECISE)
    state_squares = jnp.sum(states * states, axis=(1, 2))
    squares = carried * (state_squares[:, None] + 2.0 * cross_squares) + local_squares
    counted = carried * totals[:, :1] + jnp.sum(allowed, axis=-1)[None, :]
    state_norm = jnp.sqrt(squares / (counted * (feat_width * value_rows.shape[-1])))
    last_seg = seg_ids[-1]
    member = (seg_ids == last_seg).astype(jnp.float32)
    continues = (owner_seg == last_seg).astype(jnp.float32)
    new_states = continues * states + jnp.einsum(
        "hcp,hce->hpe", phi_key * member[None, :, None], value_rows, precision=PRECISE
    )
    new_totals = continues * totals + jnp.einsum("hcp,c->hp", phi_key, member, precision=PRECISE)
    return ((new_states, new_totals, last_seg), (mixed_out, state_norm))


def best_of(candidates, piece):
    logits = jnp.einsum("rd,vd->rv", candidates, piece, preferred_element_type=jnp.float32)
    return jnp.max(logits, axis=1)


def on_device(
    hidden,
    norm_gain,
    qkv_weight,
    out_weight,
    adapter_down,
    adapter_up,
    vocab_rows,
    segments,
    request_adapter,
    adapter_slot,
    page_table,
):
    groups = lax.axis_size("group")
    own_group = lax.axis_index("group")
    shards = lax.axis_size("mp")
    own_shard = lax.axis_index("mp")
    rows_here = segments.shape[0]
    model_width = hidden.shape[1]
    slice_width = model_width // shards
    table = page_table.reshape(groups, -1)
    per_group = table.shape[1]
    per_peer = per_group // groups
    page_len = rows_here // per_group
    holders = table // per_group
    position = jnp.arange(per_group, dtype=jnp.int32)
    sort_keys = jnp.where(holders == own_group, position[None, :], per_group + position[None, :])
    ranked = jnp.argsort(sort_keys, axis=1)[:, :per_peer]
    picked = jnp.take_along_axis(table, ranked, axis=1) - own_group * per_group
    outgoing = hidden.reshape(per_group, page_len, model_width)[picked]
    normed_pages = rms_normed(outgoing, norm_gain)
    projected_pages = jnp.einsum(
        "abrd,dc->abrc", normed_pages, qkv_weight, preferred_element_type=jnp.float32
    ).astype(jnp.bfloat16)
    lowered_pages = jnp.einsum(
        "abrd,dc->abrc", normed_pages, adapter_down, preferred_element_type=jnp.float32
    ).astype(jnp.bfloat16)
    kept_pages = lax.dynamic_slice_in_dim(outgoing, own_shard * slice_width, slice_width, 3)
    arrived = (
        lax.all_to_all(kept_pages, "group", split_axis=0, concat_axis=0, tiled=True),
        lax.all_to_all(projected_pages, "group", split_axis=0, concat_axis=0, tiled=True),
        lax.all_to_all(lowered_pages, "group", split_axis=0, concat_axis=0, tiled=True),
    )
    own_holders = lax.dynamic_index_in_dim(holders, own_group, 0, keepdims=False)
    onehot = (own_holders[:, None] == jnp.arange(groups, dtype=jnp.int32)[None, :]).astype(
        jnp.int32
    )
    earlier = jnp.sum((jnp.cumsum(onehot, axis=0) - onehot) * onehot, axis=1)
    source_rows = own_holders * per_peer + earlier

    def placed(received):
        gathered_rows = received.reshape((groups * per_peer,) + received.shape[2:])[source_rows]
        return gathered_rows.reshape((rows_here,) + received.shape[3:])

    residual, projected, lowered = [placed(received) for received in arrived]
    group_vocab = lax.all_gather(vocab_rows, "group", axis=0, tiled=True)
    group_vocab, projected = lax.optimization_barrier((group_vocab, projected))
    heads_here = projected.shape[1] // (2 * FEAT + HD)
    split_heads = jnp.transpose(
        projected.reshape(rows_here, heads_here, 2 * FEAT + HD).astype(jnp.float32), (1, 0, 2)
    )
    query_rows = split_heads[..., :FEAT]
    key_rows = split_heads[..., FEAT : 2 * FEAT]
    value_rows = split_heads[..., 2 * FEAT :]
    phi_query = features(query_rows, FEAT)
    phi_key = features(key_rows, FEAT)
    last_seg = segments[-1]
    member = (segments == last_seg).astype(jnp.float32)
    end_state = jnp.einsum(
        "hcp,hce->hpe", phi_key * member[None, :, None], value_rows, precision=PRECISE
    )
    end_totals = jnp.einsum("hcp,c->hp", phi_key, member, precision=PRECISE)
    end_tag = jnp.reshape(last_seg + 1, (1,)).astype(jnp.float32)
    got_state, got_totals, got_tag = (
        from_behind(end_state.astype(jnp.bfloat16), "group", 1).astype(end_state.dtype),
        from_behind(end_totals.astype(jnp.bfloat16), "group", 1).astype(end_totals.dtype),
        from_behind(end_tag.astype(jnp.bfloat16), "group", 1).astype(end_tag.dtype),
    )
    initial = (got_state, got_totals, got_tag[0].astype(jnp.int32) - 1)
    block_len = min(256, rows_here)
    blocks = rows_here // block_len

    def regroup(values):
        return jnp.transpose(
            values.reshape(values.shape[0], blocks, block_len, values.shape[-1]), (1, 0, 2, 3)
        )

    scan_inputs = (
        regroup(phi_query),
        regroup(phi_key),
        regroup(query_rows),
        regroup(key_rows),
        regroup(value_rows),
        segments.reshape(blocks, block_len),
    )

    def scan_step(state_carry, block_inputs):
        return block_step(state_carry, block_inputs, FEAT)

    _, (mixed_out, state_norm) = lax.scan(scan_step, initial, scan_inputs)
    attended = (
        jnp.transpose(mixed_out, (0, 2, 1, 3))
        .reshape(rows_here, heads_here * HD)
        .astype(jnp.bfloat16)
    )
    state_norms = jnp.transpose(state_norm, (1, 0, 2)).reshape(heads_here, rows_here)
    request_ids = jnp.arange(request_adapter.shape[0], dtype=jnp.int32)
    adapter_of = jnp.sum(
        jnp.where(segments[:, None] == request_ids[None, :], request_adapter[None, :], 0), axis=1
    )
    adapter_ids = jnp.arange(adapter_slot.shape[0], dtype=jnp.int32)
    slot_ids = jnp.sum(
        jnp.where(adapter_of[:, None] == adapter_ids[None, :], adapter_slot[None, :], 0), axis=1
    )
    column_slot = jnp.arange(lowered.shape[1], dtype=jnp.int32) // RANK
    local_slot = slot_ids - own_shard * (lowered.shape[1] // RANK)
    low_rank = jnp.where(
        local_slot[:, None] == column_slot[None, :], lowered, jnp.zeros_like(lowered)
    )
    partial_value = jnp.dot(attended, out_weight, preferred_element_type=jnp.float32)
    partial_value = partial_value + jnp.dot(
        low_rank, adapter_up, preferred_element_type=jnp.float32
    )
    summed = lax.psum_scatter(
        partial_value.astype(jnp.bfloat16), "mp", scatter_dimension=1, tiled=True
    )
    final_rows = (residual.astype(jnp.float32) + summed.astype(jnp.float32)).astype(jnp.bfloat16)
    group_rows = lax.all_gather(final_rows, "mp", axis=1, tiled=True)
    partial_best = best_of(group_rows, group_vocab)
    max_logits = lax.dynamic_slice_in_dim(
        lax.pmax(partial_best, "mp"), own_shard * (rows_here // shards), rows_here // shards
    )
    return (summed, state_norms, max_logits)


def solution(mesh):
    placed = (
        P("group", None),
        P(),
        P(None, "mp"),
        P("mp", None),
        P(None, "mp"),
        P("mp", None),
        P(("group", "mp"), None),
        P("group"),
        P(),
        P(),
        P(),
    )
    return jax.shard_map(
        on_device,
        mesh=mesh,
        in_specs=placed,
        out_specs=(P("group", "mp"), P("mp", "group"), P(("group", "mp"))),
        check_vma=False,
    )
```

```python
import jax
import jax.numpy as jnp
from jax import lax
from jax.sharding import PartitionSpec as P

FEAT = 16
HD = 112
RANK = 16


EPSILON = 1e-05
PRECISE = lax.Precision.HIGHEST


def from_behind(value, axis, by):
    size = lax.axis_size(axis)
    pairs = [(i, i + by) for i in range(size) if 0 <= i + by < size]
    return lax.ppermute(value, axis, pairs)


def rms_normed(values, norm_gain):
    wide = values.astype(jnp.float32)
    meansq = jnp.mean(wide * wide, axis=-1, keepdims=True)
    return (wide * lax.rsqrt(meansq + EPSILON) * norm_gain).astype(jnp.bfloat16)


def features(vectors, feat_width):
    linear_part = vectors / feat_width**0.25
    outer_part = (vectors[..., :, None] * vectors[..., None, :]).reshape(
        vectors.shape[:-1] + (feat_width * feat_width,)
    )
    outer_part = outer_part / (2.0 * feat_width) ** 0.5
    ones_part = jnp.ones(vectors.shape[:-1] + (1,), jnp.float32)
    return jnp.concatenate([ones_part, linear_part, outer_part], axis=-1)


def block_step(state_carry, block_inputs, feat_width):
    states, totals, owner_seg = state_carry
    phi_query, phi_key, query_rows, key_rows, value_rows, seg_ids = block_inputs
    scaling = feat_width ** (-0.5)
    block_len = seg_ids.shape[0]
    position = jnp.arange(block_len, dtype=jnp.int32)
    allowed = (
        (position[:, None] >= position[None, :]) & (seg_ids[:, None] == seg_ids[None, :])
    ).astype(jnp.float32)
    carried = (seg_ids == owner_seg).astype(jnp.float32)[None, :]
    scores = jnp.einsum("hcf,hdf->hcd", query_rows, key_rows, precision=PRECISE) * scaling
    weights = (1.0 + scores + 0.5 * scores * scores) * allowed[None]
    numerator = jnp.einsum("hcd,hde->hce", weights, value_rows, precision=PRECISE)
    numerator = numerator + carried[..., None] * jnp.einsum(
        "hcp,hpe->hce", phi_query, states, precision=PRECISE
    )
    denominator = jnp.sum(weights, axis=-1) + carried * jnp.einsum(
        "hcp,hp->hc", phi_query, totals, precision=PRECISE
    )
    mixed_out = numerator / denominator[..., None]
    key_scores = jnp.einsum("hcf,hdf->hcd", key_rows, key_rows, precision=PRECISE) * scaling
    value_gram = jnp.einsum("hce,hde->hcd", value_rows, value_rows, precision=PRECISE)
    key_gram = (1.0 + key_scores + 0.5 * key_scores * key_scores) * value_gram
    masked_gram = jnp.einsum("cd,hde->hce", allowed, key_gram, precision=PRECISE)
    local_squares = jnp.sum(masked_gram * allowed[None], axis=-1)
    along = jnp.sum(
        jnp.einsum("hcp,hpe->hce", phi_key, states, precision=PRECISE) * value_rows, axis=-1
    )
    cross_squares = jnp.einsum("cd,hd->hc", allowed, along, precision=PRECISE)
    state_squares = jnp.sum(states * states, axis=(1, 2))
    squares = carried * (state_squares[:, None] + 2.0 * cross_squares) + local_squares
    counted = carried * totals[:, :1] + jnp.sum(allowed, axis=-1)[None, :]
    state_norm = jnp.sqrt(squares / (counted * (feat_width * value_rows.shape[-1])))
    last_seg = seg_ids[-1]
    member = (seg_ids == last_seg).astype(jnp.float32)
    continues = (owner_seg == last_seg).astype(jnp.float32)
    new_states = continues * states + jnp.einsum(
        "hcp,hce->hpe", phi_key * member[None, :, None], value_rows, precision=PRECISE
    )
    new_totals = continues * totals + jnp.einsum("hcp,c->hp", phi_key, member, precision=PRECISE)
    return ((new_states, new_totals, last_seg), (mixed_out, state_norm))


def best_of(candidates, piece):
    logits = jnp.einsum("rd,vd->rv", candidates, piece, preferred_element_type=jnp.float32)
    return jnp.max(logits, axis=1)


def on_device(
    hidden,
    norm_gain,
    qkv_weight,
    out_weight,
    adapter_down,
    adapter_up,
    vocab_rows,
    segments,
    request_adapter,
    adapter_slot,
    page_table,
):
    groups = lax.axis_size("group")
    own_group = lax.axis_index("group")
    shards = lax.axis_size("mp")
    own_shard = lax.axis_index("mp")
    rows_here = segments.shape[0]
    model_width = hidden.shape[1]
    slice_width = model_width // shards
    table = page_table.reshape(groups, -1)
    per_group = table.shape[1]
    per_peer = per_group // groups
    page_len = rows_here // per_group
    holders = table // per_group
    position = jnp.arange(per_group, dtype=jnp.int32)
    sort_keys = jnp.where(holders == own_group, position[None, :], per_group + position[None, :])
    ranked = jnp.argsort(sort_keys, axis=1)[:, :per_peer]
    picked = jnp.take_along_axis(table, ranked, axis=1) - own_group * per_group
    outgoing = hidden.reshape(per_group, page_len, model_width)[picked]
    normed_pages = rms_normed(outgoing, norm_gain)
    projected_pages = jnp.einsum(
        "abrd,dc->abrc", normed_pages, qkv_weight, preferred_element_type=jnp.float32
    ).astype(jnp.bfloat16)
    lowered_pages = jnp.einsum(
        "abrd,dc->abrc", normed_pages, adapter_down, preferred_element_type=jnp.float32
    ).astype(jnp.bfloat16)
    kept_pages = lax.dynamic_slice_in_dim(outgoing, own_shard * slice_width, slice_width, 3)
    widths = (kept_pages.shape[3], projected_pages.shape[3], lowered_pages.shape[3])
    packed = lax.all_to_all(
        jnp.concatenate([kept_pages, projected_pages, lowered_pages], axis=3),
        "group", split_axis=0, concat_axis=0, tiled=True,
    )
    arrived = (
        packed[..., : widths[0]],
        packed[..., widths[0] : widths[0] + widths[1]],
        packed[..., widths[0] + widths[1] :],
    )
    own_holders = lax.dynamic_index_in_dim(holders, own_group, 0, keepdims=False)
    onehot = (own_holders[:, None] == jnp.arange(groups, dtype=jnp.int32)[None, :]).astype(
        jnp.int32
    )
    earlier = jnp.sum((jnp.cumsum(onehot, axis=0) - onehot) * onehot, axis=1)
    source_rows = own_holders * per_peer + earlier

    def placed(received):
        gathered_rows = received.reshape((groups * per_peer,) + received.shape[2:])[source_rows]
        return gathered_rows.reshape((rows_here,) + received.shape[3:])

    residual, projected, lowered = [placed(received) for received in arrived]
    group_vocab = lax.all_gather(vocab_rows, "group", axis=0, tiled=True)
    heads_here = projected.shape[1] // (2 * FEAT + HD)
    split_heads = jnp.transpose(
        projected.reshape(rows_here, heads_here, 2 * FEAT + HD).astype(jnp.float32), (1, 0, 2)
    )
    query_rows = split_heads[..., :FEAT]
    key_rows = split_heads[..., FEAT : 2 * FEAT]
    value_rows = split_heads[..., 2 * FEAT :]
    phi_query = features(query_rows, FEAT)
    phi_key = features(key_rows, FEAT)
    last_seg = segments[-1]
    member = (segments == last_seg).astype(jnp.float32)
    end_state = jnp.einsum(
        "hcp,hce->hpe", phi_key * member[None, :, None], value_rows, precision=PRECISE
    )
    end_totals = jnp.einsum("hcp,c->hp", phi_key, member, precision=PRECISE)
    end_tag = jnp.reshape(last_seg + 1, (1,)).astype(jnp.float32)
    state_size, totals_size = end_state.size, end_totals.size
    handed = from_behind(
        jnp.concatenate(
            [end_state.reshape(-1), end_totals.reshape(-1), end_tag]
        ).astype(jnp.bfloat16),
        "group",
        1,
    ).astype(jnp.float32)
    got_state = handed[:state_size].reshape(end_state.shape)
    got_totals = handed[state_size : state_size + totals_size].reshape(end_totals.shape)
    got_tag = handed[state_size + totals_size :]
    initial = (got_state, got_totals, got_tag[0].astype(jnp.int32) - 1)
    block_len = min(256, rows_here)
    blocks = rows_here // block_len

    def regroup(values):
        return jnp.transpose(
            values.reshape(values.shape[0], blocks, block_len, values.shape[-1]), (1, 0, 2, 3)
        )

    scan_inputs = (
        regroup(phi_query),
        regroup(phi_key),
        regroup(query_rows),
        regroup(key_rows),
        regroup(value_rows),
        segments.reshape(blocks, block_len),
    )

    def scan_step(state_carry, block_inputs):
        return block_step(state_carry, block_inputs, FEAT)

    _, (mixed_out, state_norm) = lax.scan(scan_step, initial, scan_inputs)
    attended = (
        jnp.transpose(mixed_out, (0, 2, 1, 3))
        .reshape(rows_here, heads_here * HD)
        .astype(jnp.bfloat16)
    )
    group_vocab, attended = lax.optimization_barrier((group_vocab, attended))
    state_norms = jnp.transpose(state_norm, (1, 0, 2)).reshape(heads_here, rows_here)
    request_ids = jnp.arange(request_adapter.shape[0], dtype=jnp.int32)
    adapter_of = jnp.sum(
        jnp.where(segments[:, None] == request_ids[None, :], request_adapter[None, :], 0), axis=1
    )
    adapter_ids = jnp.arange(adapter_slot.shape[0], dtype=jnp.int32)
    slot_ids = jnp.sum(
        jnp.where(adapter_of[:, None] == adapter_ids[None, :], adapter_slot[None, :], 0), axis=1
    )
    column_slot = jnp.arange(lowered.shape[1], dtype=jnp.int32) // RANK
    local_slot = slot_ids - own_shard * (lowered.shape[1] // RANK)
    low_rank = jnp.where(
        local_slot[:, None] == column_slot[None, :], lowered, jnp.zeros_like(lowered)
    )
    partial_value = jnp.dot(attended, out_weight, preferred_element_type=jnp.float32)
    partial_value = partial_value + jnp.dot(
        low_rank, adapter_up, preferred_element_type=jnp.float32
    )
    summed = lax.psum_scatter(
        partial_value.astype(jnp.bfloat16), "mp", scatter_dimension=1, tiled=True
    )
    final_rows = (residual.astype(jnp.float32) + summed.astype(jnp.float32)).astype(jnp.bfloat16)
    group_rows = lax.all_gather(final_rows, "mp", axis=1, tiled=True)
    partial_best = best_of(group_rows, group_vocab)
    max_logits = lax.dynamic_slice_in_dim(
        lax.pmax(partial_best, "mp"), own_shard * (rows_here // shards), rows_here // shards
    )
    return (summed, state_norms, max_logits)


def solution(mesh):
    placed = (
        P("group", None),
        P(),
        P(None, "mp"),
        P("mp", None),
        P(None, "mp"),
        P("mp", None),
        P(("group", "mp"), None),
        P("group"),
        P(),
        P(),
        P(),
    )
    return jax.shard_map(
        on_device,
        mesh=mesh,
        in_specs=placed,
        out_specs=(P("group", "mp"), P("mp", "group"), P(("group", "mp"))),
        check_vma=False,
    )
```

```python
import jax
import jax.numpy as jnp
from jax import lax
from jax.sharding import PartitionSpec as P
from jax.experimental import pallas as pl
from jax.experimental.pallas import tpu as pltpu

FEAT = 16
HD = 112
RANK = 16


EPSILON = 1e-05
PRECISE = lax.Precision.HIGHEST


def from_behind(value, axis, by):
    size = lax.axis_size(axis)
    pairs = [(i, i + by) for i in range(size) if 0 <= i + by < size]
    return lax.ppermute(value, axis, pairs)


def rms_normed(values, norm_gain):
    wide = values.astype(jnp.float32)
    meansq = jnp.mean(wide * wide, axis=-1, keepdims=True)
    return (wide * lax.rsqrt(meansq + EPSILON) * norm_gain).astype(jnp.bfloat16)


def features(vectors, feat_width):
    linear_part = vectors / feat_width**0.25
    outer_part = (vectors[..., :, None] * vectors[..., None, :]).reshape(
        vectors.shape[:-1] + (feat_width * feat_width,)
    )
    outer_part = outer_part / (2.0 * feat_width) ** 0.5
    ones_part = jnp.ones(vectors.shape[:-1] + (1,), jnp.float32)
    return jnp.concatenate([ones_part, linear_part, outer_part], axis=-1)


def block_step(state_carry, block_inputs, feat_width):
    states, totals, owner_seg = state_carry
    phi_query, phi_key, query_rows, key_rows, value_rows, seg_ids = block_inputs
    scaling = feat_width ** (-0.5)
    block_len = seg_ids.shape[0]
    position = jnp.arange(block_len, dtype=jnp.int32)
    allowed = (
        (position[:, None] >= position[None, :]) & (seg_ids[:, None] == seg_ids[None, :])
    ).astype(jnp.float32)
    carried = (seg_ids == owner_seg).astype(jnp.float32)[None, :]
    scores = jnp.einsum("hcf,hdf->hcd", query_rows, key_rows, precision=PRECISE) * scaling
    weights = (1.0 + scores + 0.5 * scores * scores) * allowed[None]
    numerator = jnp.einsum("hcd,hde->hce", weights, value_rows, precision=PRECISE)
    numerator = numerator + carried[..., None] * jnp.einsum(
        "hcp,hpe->hce", phi_query, states, precision=PRECISE
    )
    denominator = jnp.sum(weights, axis=-1) + carried * jnp.einsum(
        "hcp,hp->hc", phi_query, totals, precision=PRECISE
    )
    mixed_out = numerator / denominator[..., None]
    key_scores = jnp.einsum("hcf,hdf->hcd", key_rows, key_rows, precision=PRECISE) * scaling
    value_gram = jnp.einsum("hce,hde->hcd", value_rows, value_rows, precision=PRECISE)
    key_gram = (1.0 + key_scores + 0.5 * key_scores * key_scores) * value_gram
    masked_gram = jnp.einsum("cd,hde->hce", allowed, key_gram, precision=PRECISE)
    local_squares = jnp.sum(masked_gram * allowed[None], axis=-1)
    along = jnp.sum(
        jnp.einsum("hcp,hpe->hce", phi_key, states, precision=PRECISE) * value_rows, axis=-1
    )
    cross_squares = jnp.einsum("cd,hd->hc", allowed, along, precision=PRECISE)
    state_squares = jnp.sum(states * states, axis=(1, 2))
    squares = carried * (state_squares[:, None] + 2.0 * cross_squares) + local_squares
    counted = carried * totals[:, :1] + jnp.sum(allowed, axis=-1)[None, :]
    state_norm = jnp.sqrt(squares / (counted * (feat_width * value_rows.shape[-1])))
    last_seg = seg_ids[-1]
    member = (seg_ids == last_seg).astype(jnp.float32)
    continues = (owner_seg == last_seg).astype(jnp.float32)
    new_states = continues * states + jnp.einsum(
        "hcp,hce->hpe", phi_key * member[None, :, None], value_rows, precision=PRECISE
    )
    new_totals = continues * totals + jnp.einsum("hcp,c->hp", phi_key, member, precision=PRECISE)
    return ((new_states, new_totals, last_seg), (mixed_out, state_norm))


def best_of(candidates, piece):
    logits = jnp.einsum("rd,vd->rv", candidates, piece, preferred_element_type=jnp.float32)
    return jnp.max(logits, axis=1)


def exchange_kernel(
    part_ref, resid_ref, vocab_ref, upd_ref, best_ref,
    land, rows, tops, got, sems,
):
    n = part_ref.shape[0]
    block_rows = best_ref.shape[0]
    me = lax.axis_index("mp")
    grp = lax.axis_index("group")
    peers = [lax.rem(me + k, n) for k in range(1, n)]
    mesh_id = pl.DeviceIdType.MESH

    barrier = pltpu.get_barrier_semaphore()
    for p in peers:
        pl.semaphore_signal(barrier, inc=1, device_id=(grp, p), device_id_type=mesh_id)
    pl.semaphore_wait(barrier, n - 1)

    def send_all(phase, src_of, dst):
        copies = []
        for p in peers:
            copy = pltpu.make_async_remote_copy(
                src_ref=src_of(p),
                dst_ref=dst.at[me],
                send_sem=sems.at[phase, 0, p],
                recv_sem=sems.at[phase, 1, me],
                device_id=(grp, p),
                device_id_type=mesh_id,
            )
            copy.start()
            copies.append(copy)
        return copies

    def finish(phase, copies, src_of, dst):
        for copy in copies:
            copy.wait_send()
        for q in peers:
            pltpu.make_async_remote_copy(
                src_ref=src_of(q),
                dst_ref=dst.at[q],
                send_sem=sems.at[phase, 0, q],
                recv_sem=sems.at[phase, 1, q],
                device_id=(grp, q),
                device_id_type=mesh_id,
            ).wait_recv()

    part_of = lambda p: part_ref.at[p]
    sent = send_all(0, part_of, land)
    finish(0, sent, part_of, land)
    total = part_ref[me].astype(jnp.float32)
    for q in peers:
        total = total + land[q].astype(jnp.float32)
    update = total.astype(upd_ref.dtype)
    upd_ref[...] = update
    rows[me] = (resid_ref[...].astype(jnp.float32) + update.astype(jnp.float32)).astype(
        rows.dtype
    )

    own_rows = lambda p: rows.at[me]
    sent = send_all(1, own_rows, rows)
    finish(1, sent, own_rows, rows)
    scores = jnp.zeros((rows.shape[1], vocab_ref.shape[1]), jnp.float32)
    for j in range(n):
        scores = scores + lax.dot_general(
            rows[j], vocab_ref[j], (((1,), (1,)), ((), ())),
            preferred_element_type=jnp.float32,
        )
    for p in range(n):
        piece = jnp.max(scores[p * block_rows : (p + 1) * block_rows], axis=1, keepdims=True)
        tops[p] = jnp.broadcast_to(piece, tops.shape[1:])

    top_of = lambda p: tops.at[p]
    sent = send_all(2, top_of, got)
    finish(2, sent, top_of, got)
    best = tops[me]
    for q in peers:
        best = jnp.maximum(best, got[q])
    best_ref[...] = best


def mp_exchange(parts, residual, vocab_blocks):
    n, rows_here, width = parts.shape
    block_rows = rows_here // n
    vmem = pl.BlockSpec(memory_space=pltpu.VMEM)
    return pl.pallas_call(
        exchange_kernel,
        out_shape=(
            jax.ShapeDtypeStruct((rows_here, width), jnp.bfloat16),
            jax.ShapeDtypeStruct((block_rows, 128), jnp.float32),
        ),
        in_specs=[vmem] * 3,
        out_specs=(vmem, vmem),
        scratch_shapes=[
            pltpu.VMEM((n, rows_here, width), jnp.bfloat16),
            pltpu.VMEM((n, rows_here, width), jnp.bfloat16),
            pltpu.VMEM((n, block_rows, 128), jnp.float32),
            pltpu.VMEM((n, block_rows, 128), jnp.float32),
            pltpu.SemaphoreType.DMA((3, 2, n)),
        ],
        compiler_params=pltpu.CompilerParams(collective_id=0, has_side_effects=True),
    )(parts, residual, vocab_blocks)


def on_device(
    hidden,
    norm_gain,
    qkv_weight,
    out_weight,
    adapter_down,
    adapter_up,
    vocab_rows,
    segments,
    request_adapter,
    adapter_slot,
    page_table,
):
    groups = lax.axis_size("group")
    own_group = lax.axis_index("group")
    shards = lax.axis_size("mp")
    own_shard = lax.axis_index("mp")
    rows_here = segments.shape[0]
    model_width = hidden.shape[1]
    slice_width = model_width // shards
    table = page_table.reshape(groups, -1)
    per_group = table.shape[1]
    per_peer = per_group // groups
    page_len = rows_here // per_group
    holders = table // per_group
    position = jnp.arange(per_group, dtype=jnp.int32)
    sort_keys = jnp.where(holders == own_group, position[None, :], per_group + position[None, :])
    ranked = jnp.argsort(sort_keys, axis=1)[:, :per_peer]
    picked = jnp.take_along_axis(table, ranked, axis=1) - own_group * per_group
    outgoing = hidden.reshape(per_group, page_len, model_width)[picked]
    normed_pages = rms_normed(outgoing, norm_gain)
    projected_pages = jnp.einsum(
        "abrd,dc->abrc", normed_pages, qkv_weight, preferred_element_type=jnp.float32
    ).astype(jnp.bfloat16)
    lowered_pages = jnp.einsum(
        "abrd,dc->abrc", normed_pages, adapter_down, preferred_element_type=jnp.float32
    ).astype(jnp.bfloat16)
    kept_pages = lax.dynamic_slice_in_dim(outgoing, own_shard * slice_width, slice_width, 3)
    widths = (kept_pages.shape[3], projected_pages.shape[3], lowered_pages.shape[3])
    packed = lax.all_to_all(
        jnp.concatenate([kept_pages, projected_pages, lowered_pages], axis=3),
        "group", split_axis=0, concat_axis=0, tiled=True,
    )
    arrived = (
        packed[..., : widths[0]],
        packed[..., widths[0] : widths[0] + widths[1]],
        packed[..., widths[0] + widths[1] :],
    )
    own_holders = lax.dynamic_index_in_dim(holders, own_group, 0, keepdims=False)
    onehot = (own_holders[:, None] == jnp.arange(groups, dtype=jnp.int32)[None, :]).astype(
        jnp.int32
    )
    earlier = jnp.sum((jnp.cumsum(onehot, axis=0) - onehot) * onehot, axis=1)
    source_rows = own_holders * per_peer + earlier

    def placed(received):
        gathered_rows = received.reshape((groups * per_peer,) + received.shape[2:])[source_rows]
        return gathered_rows.reshape((rows_here,) + received.shape[3:])

    residual, projected, lowered = [placed(received) for received in arrived]
    group_vocab = lax.all_gather(vocab_rows, "group", axis=0, tiled=True)
    heads_here = projected.shape[1] // (2 * FEAT + HD)
    split_heads = jnp.transpose(
        projected.reshape(rows_here, heads_here, 2 * FEAT + HD).astype(jnp.float32), (1, 0, 2)
    )
    query_rows = split_heads[..., :FEAT]
    key_rows = split_heads[..., FEAT : 2 * FEAT]
    value_rows = split_heads[..., 2 * FEAT :]
    phi_query = features(query_rows, FEAT)
    phi_key = features(key_rows, FEAT)
    last_seg = segments[-1]
    member = (segments == last_seg).astype(jnp.float32)
    end_state = jnp.einsum(
        "hcp,hce->hpe", phi_key * member[None, :, None], value_rows, precision=PRECISE
    )
    end_totals = jnp.einsum("hcp,c->hp", phi_key, member, precision=PRECISE)
    end_tag = jnp.reshape(last_seg + 1, (1,)).astype(jnp.float32)
    state_size, totals_size = end_state.size, end_totals.size
    handed = from_behind(
        jnp.concatenate(
            [end_state.reshape(-1), end_totals.reshape(-1), end_tag]
        ).astype(jnp.bfloat16),
        "group",
        1,
    ).astype(jnp.float32)
    got_state = handed[:state_size].reshape(end_state.shape)
    got_totals = handed[state_size : state_size + totals_size].reshape(end_totals.shape)
    got_tag = handed[state_size + totals_size :]
    initial = (got_state, got_totals, got_tag[0].astype(jnp.int32) - 1)
    block_len = min(256, rows_here)
    blocks = rows_here // block_len

    def regroup(values):
        return jnp.transpose(
            values.reshape(values.shape[0], blocks, block_len, values.shape[-1]), (1, 0, 2, 3)
        )

    scan_inputs = (
        regroup(phi_query),
        regroup(phi_key),
        regroup(query_rows),
        regroup(key_rows),
        regroup(value_rows),
        segments.reshape(blocks, block_len),
    )

    def scan_step(state_carry, block_inputs):
        return block_step(state_carry, block_inputs, FEAT)

    _, (mixed_out, state_norm) = lax.scan(scan_step, initial, scan_inputs)
    attended = (
        jnp.transpose(mixed_out, (0, 2, 1, 3))
        .reshape(rows_here, heads_here * HD)
        .astype(jnp.bfloat16)
    )
    group_vocab, attended = lax.optimization_barrier((group_vocab, attended))
    state_norms = jnp.transpose(state_norm, (1, 0, 2)).reshape(heads_here, rows_here)
    request_ids = jnp.arange(request_adapter.shape[0], dtype=jnp.int32)
    adapter_of = jnp.sum(
        jnp.where(segments[:, None] == request_ids[None, :], request_adapter[None, :], 0), axis=1
    )
    adapter_ids = jnp.arange(adapter_slot.shape[0], dtype=jnp.int32)
    slot_ids = jnp.sum(
        jnp.where(adapter_of[:, None] == adapter_ids[None, :], adapter_slot[None, :], 0), axis=1
    )
    column_slot = jnp.arange(lowered.shape[1], dtype=jnp.int32) // RANK
    local_slot = slot_ids - own_shard * (lowered.shape[1] // RANK)
    low_rank = jnp.where(
        local_slot[:, None] == column_slot[None, :], lowered, jnp.zeros_like(lowered)
    )
    out_blocks = out_weight.reshape(out_weight.shape[0], shards, slice_width)
    up_blocks = adapter_up.reshape(adapter_up.shape[0], shards, slice_width)
    partial_value = jnp.einsum(
        "rk,kjc->jrc", attended, out_blocks, preferred_element_type=jnp.float32
    ) + jnp.einsum("rk,kjc->jrc", low_rank, up_blocks, preferred_element_type=jnp.float32)
    vocab_blocks = jnp.transpose(
        group_vocab.reshape(group_vocab.shape[0], shards, slice_width), (1, 0, 2)
    )
    summed, best = mp_exchange(partial_value.astype(jnp.bfloat16), residual, vocab_blocks)
    max_logits = best[:, 0]
    return (summed, state_norms, max_logits)


def solution(mesh):
    placed = (
        P("group", None),
        P(),
        P(None, "mp"),
        P("mp", None),
        P(None, "mp"),
        P("mp", None),
        P(("group", "mp"), None),
        P("group"),
        P(),
        P(),
        P(),
    )
    return jax.shard_map(
        on_device,
        mesh=mesh,
        in_specs=placed,
        out_specs=(P("group", "mp"), P("mp", "group"), P(("group", "mp"))),
        check_vma=False,
    )
```

```python
import jax
import jax.numpy as jnp
from jax import lax
from jax.sharding import PartitionSpec as P
from jax.experimental import pallas as pl
from jax.experimental.pallas import tpu as pltpu

FEAT = 16
HD = 112
RANK = 16


EPSILON = 1e-05
PRECISE = lax.Precision.HIGHEST


def from_behind(value, axis, by):
    size = lax.axis_size(axis)
    pairs = [(i, i + by) for i in range(size) if 0 <= i + by < size]
    return lax.ppermute(value, axis, pairs)


def rms_normed(values, norm_gain):
    wide = values.astype(jnp.float32)
    meansq = jnp.mean(wide * wide, axis=-1, keepdims=True)
    return (wide * lax.rsqrt(meansq + EPSILON) * norm_gain).astype(jnp.bfloat16)


def features(vectors, feat_width):
    linear_part = vectors / feat_width**0.25
    outer_part = (vectors[..., :, None] * vectors[..., None, :]).reshape(
        vectors.shape[:-1] + (feat_width * feat_width,)
    )
    outer_part = outer_part / (2.0 * feat_width) ** 0.5
    ones_part = jnp.ones(vectors.shape[:-1] + (1,), jnp.float32)
    return jnp.concatenate([ones_part, linear_part, outer_part], axis=-1)


def block_step(state_carry, block_inputs, feat_width):
    states, totals, owner_seg = state_carry
    phi_query, phi_key, query_rows, key_rows, value_rows, seg_ids = block_inputs
    scaling = feat_width ** (-0.5)
    block_len = seg_ids.shape[0]
    position = jnp.arange(block_len, dtype=jnp.int32)
    allowed = (
        (position[:, None] >= position[None, :]) & (seg_ids[:, None] == seg_ids[None, :])
    ).astype(jnp.float32)
    carried = (seg_ids == owner_seg).astype(jnp.float32)[None, :]
    scores = jnp.einsum("hcf,hdf->hcd", query_rows, key_rows, precision=PRECISE) * scaling
    weights = (1.0 + scores + 0.5 * scores * scores) * allowed[None]
    numerator = jnp.einsum("hcd,hde->hce", weights, value_rows, precision=PRECISE)
    numerator = numerator + carried[..., None] * jnp.einsum(
        "hcp,hpe->hce", phi_query, states, precision=PRECISE
    )
    denominator = jnp.sum(weights, axis=-1) + carried * jnp.einsum(
        "hcp,hp->hc", phi_query, totals, precision=PRECISE
    )
    mixed_out = numerator / denominator[..., None]
    key_scores = jnp.einsum("hcf,hdf->hcd", key_rows, key_rows, precision=PRECISE) * scaling
    value_gram = jnp.einsum("hce,hde->hcd", value_rows, value_rows, precision=PRECISE)
    key_gram = (1.0 + key_scores + 0.5 * key_scores * key_scores) * value_gram
    masked_gram = jnp.einsum("cd,hde->hce", allowed, key_gram, precision=PRECISE)
    local_squares = jnp.sum(masked_gram * allowed[None], axis=-1)
    along = jnp.sum(
        jnp.einsum("hcp,hpe->hce", phi_key, states, precision=PRECISE) * value_rows, axis=-1
    )
    cross_squares = jnp.einsum("cd,hd->hc", allowed, along, precision=PRECISE)
    state_squares = jnp.sum(states * states, axis=(1, 2))
    squares = carried * (state_squares[:, None] + 2.0 * cross_squares) + local_squares
    counted = carried * totals[:, :1] + jnp.sum(allowed, axis=-1)[None, :]
    state_norm = jnp.sqrt(squares / (counted * (feat_width * value_rows.shape[-1])))
    last_seg = seg_ids[-1]
    member = (seg_ids == last_seg).astype(jnp.float32)
    continues = (owner_seg == last_seg).astype(jnp.float32)
    new_states = continues * states + jnp.einsum(
        "hcp,hce->hpe", phi_key * member[None, :, None], value_rows, precision=PRECISE
    )
    new_totals = continues * totals + jnp.einsum("hcp,c->hp", phi_key, member, precision=PRECISE)
    return ((new_states, new_totals, last_seg), (mixed_out, state_norm))


def best_of(candidates, piece):
    logits = jnp.einsum("rd,vd->rv", candidates, piece, preferred_element_type=jnp.float32)
    return jnp.max(logits, axis=1)


def exchange_kernel(
    part_ref, resid_ref, vocab_ref, upd_ref, best_ref,
    land, acc, rows, tops, got, ring_sems, top_sems,
):
    n = part_ref.shape[0]
    half = part_ref.shape[1] // 2
    block_rows = best_ref.shape[0]
    me = lax.axis_index("mp")
    grp = lax.axis_index("group")
    peers = [lax.rem(me + k, n) for k in range(1, n)]
    mesh_id = pl.DeviceIdType.MESH
    towards = (lax.rem(me + 1, n), lax.rem(me + n - 1, n))
    spans = (pl.ds(0, half), pl.ds(half, half))

    barrier = pltpu.get_barrier_semaphore()
    for p in peers:
        pl.semaphore_signal(barrier, inc=1, device_id=(grp, p), device_id_type=mesh_id)
    pl.semaphore_wait(barrier, n - 1)

    def ring_copy(phase, way, step, src, dst):
        return pltpu.make_async_remote_copy(
            src_ref=src,
            dst_ref=dst,
            send_sem=ring_sems.at[phase, way, 0, step],
            recv_sem=ring_sems.at[phase, way, 1, step],
            device_id=(grp, towards[way]),
            device_id_type=mesh_id,
        )

    def rs_chunk(way, step):
        return lax.rem(me + (n - 1 - step if way == 0 else 1 + step) + n, n)

    for step in range(n - 1):
        copies = []
        for way in range(2):
            chunk = rs_chunk(way, step)
            if step == 0:
                src = part_ref.at[chunk, spans[way]]
            else:
                acc[way, step] = (
                    land[way, step - 1].astype(jnp.float32)
                    + part_ref[chunk, spans[way]].astype(jnp.float32)
                ).astype(acc.dtype)
                src = acc.at[way, step]
            copy = ring_copy(0, way, step, src, land.at[way, step])
            copy.start()
            copies.append(copy)
        for copy in copies:
            copy.wait()
    for way in range(2):
        total = land[way, n - 2].astype(jnp.float32) + part_ref[me, spans[way]].astype(
            jnp.float32
        )
        update = total.astype(upd_ref.dtype)
        upd_ref[spans[way]] = update
        rows[me, spans[way]] = (
            resid_ref[spans[way]].astype(jnp.float32) + update.astype(jnp.float32)
        ).astype(rows.dtype)

    for step in range(n - 1):
        copies = []
        for way in range(2):
            chunk = lax.rem(me + (n - step if way == 0 else step), n)
            view = rows.at[chunk, spans[way]]
            copy = ring_copy(1, way, step, view, view)
            copy.start()
            copies.append(copy)
        for copy in copies:
            copy.wait()

    scores = jnp.zeros((rows.shape[1], vocab_ref.shape[1]), jnp.float32)
    for j in range(n):
        scores = scores + lax.dot_general(
            rows[j], vocab_ref[j], (((1,), (1,)), ((), ())),
            preferred_element_type=jnp.float32,
        )
    for p in range(n):
        piece = jnp.max(scores[p * block_rows : (p + 1) * block_rows], axis=1, keepdims=True)
        tops[p] = jnp.broadcast_to(piece, tops.shape[1:])

    sent = []
    for p in peers:
        copy = pltpu.make_async_remote_copy(
            src_ref=tops.at[p],
            dst_ref=got.at[me],
            send_sem=top_sems.at[0, p],
            recv_sem=top_sems.at[1, me],
            device_id=(grp, p),
            device_id_type=mesh_id,
        )
        copy.start()
        sent.append(copy)
    for copy in sent:
        copy.wait_send()
    for q in peers:
        pltpu.make_async_remote_copy(
            src_ref=tops.at[q],
            dst_ref=got.at[q],
            send_sem=top_sems.at[0, q],
            recv_sem=top_sems.at[1, q],
            device_id=(grp, q),
            device_id_type=mesh_id,
        ).wait_recv()
    best = tops[me]
    for q in peers:
        best = jnp.maximum(best, got[q])
    best_ref[...] = best


def mp_exchange(parts, residual, vocab_blocks):
    n, rows_here, width = parts.shape
    block_rows = rows_here // n
    vmem = pl.BlockSpec(memory_space=pltpu.VMEM)
    return pl.pallas_call(
        exchange_kernel,
        out_shape=(
            jax.ShapeDtypeStruct((rows_here, width), jnp.bfloat16),
            jax.ShapeDtypeStruct((block_rows, 128), jnp.float32),
        ),
        in_specs=[vmem] * 3,
        out_specs=(vmem, vmem),
        scratch_shapes=[
            pltpu.VMEM((2, n - 1, rows_here // 2, width), jnp.bfloat16),
            pltpu.VMEM((2, n - 1, rows_here // 2, width), jnp.bfloat16),
            pltpu.VMEM((n, rows_here, width), jnp.bfloat16),
            pltpu.VMEM((n, block_rows, 128), jnp.float32),
            pltpu.VMEM((n, block_rows, 128), jnp.float32),
            pltpu.SemaphoreType.DMA((2, 2, 2, n - 1)),
            pltpu.SemaphoreType.DMA((2, n)),
        ],
        compiler_params=pltpu.CompilerParams(collective_id=0, has_side_effects=True),
    )(parts, residual, vocab_blocks)


def on_device(
    hidden,
    norm_gain,
    qkv_weight,
    out_weight,
    adapter_down,
    adapter_up,
    vocab_rows,
    segments,
    request_adapter,
    adapter_slot,
    page_table,
):
    groups = lax.axis_size("group")
    own_group = lax.axis_index("group")
    shards = lax.axis_size("mp")
    own_shard = lax.axis_index("mp")
    rows_here = segments.shape[0]
    model_width = hidden.shape[1]
    slice_width = model_width // shards
    table = page_table.reshape(groups, -1)
    per_group = table.shape[1]
    per_peer = per_group // groups
    page_len = rows_here // per_group
    holders = table // per_group
    position = jnp.arange(per_group, dtype=jnp.int32)
    sort_keys = jnp.where(holders == own_group, position[None, :], per_group + position[None, :])
    ranked = jnp.argsort(sort_keys, axis=1)[:, :per_peer]
    picked = jnp.take_along_axis(table, ranked, axis=1) - own_group * per_group
    outgoing = hidden.reshape(per_group, page_len, model_width)[picked]
    normed_pages = rms_normed(outgoing, norm_gain)
    projected_pages = jnp.einsum(
        "abrd,dc->abrc", normed_pages, qkv_weight, preferred_element_type=jnp.float32
    ).astype(jnp.bfloat16)
    lowered_pages = jnp.einsum(
        "abrd,dc->abrc", normed_pages, adapter_down, preferred_element_type=jnp.float32
    ).astype(jnp.bfloat16)
    kept_pages = lax.dynamic_slice_in_dim(outgoing, own_shard * slice_width, slice_width, 3)
    widths = (kept_pages.shape[3], projected_pages.shape[3], lowered_pages.shape[3])
    packed = lax.all_to_all(
        jnp.concatenate([kept_pages, projected_pages, lowered_pages], axis=3),
        "group", split_axis=0, concat_axis=0, tiled=True,
    )
    arrived = (
        packed[..., : widths[0]],
        packed[..., widths[0] : widths[0] + widths[1]],
        packed[..., widths[0] + widths[1] :],
    )
    own_holders = lax.dynamic_index_in_dim(holders, own_group, 0, keepdims=False)
    onehot = (own_holders[:, None] == jnp.arange(groups, dtype=jnp.int32)[None, :]).astype(
        jnp.int32
    )
    earlier = jnp.sum((jnp.cumsum(onehot, axis=0) - onehot) * onehot, axis=1)
    source_rows = own_holders * per_peer + earlier

    def placed(received):
        gathered_rows = received.reshape((groups * per_peer,) + received.shape[2:])[source_rows]
        return gathered_rows.reshape((rows_here,) + received.shape[3:])

    residual, projected, lowered = [placed(received) for received in arrived]
    group_vocab = lax.all_gather(vocab_rows, "group", axis=0, tiled=True)
    heads_here = projected.shape[1] // (2 * FEAT + HD)
    split_heads = jnp.transpose(
        projected.reshape(rows_here, heads_here, 2 * FEAT + HD).astype(jnp.float32), (1, 0, 2)
    )
    query_rows = split_heads[..., :FEAT]
    key_rows = split_heads[..., FEAT : 2 * FEAT]
    value_rows = split_heads[..., 2 * FEAT :]
    phi_query = features(query_rows, FEAT)
    phi_key = features(key_rows, FEAT)
    last_seg = segments[-1]
    member = (segments == last_seg).astype(jnp.float32)
    end_state = jnp.einsum(
        "hcp,hce->hpe", phi_key * member[None, :, None], value_rows, precision=PRECISE
    )
    end_totals = jnp.einsum("hcp,c->hp", phi_key, member, precision=PRECISE)
    end_tag = jnp.reshape(last_seg + 1, (1,)).astype(jnp.float32)
    state_size, totals_size = end_state.size, end_totals.size
    handed = from_behind(
        jnp.concatenate(
            [end_state.reshape(-1), end_totals.reshape(-1), end_tag]
        ).astype(jnp.bfloat16),
        "group",
        1,
    ).astype(jnp.float32)
    got_state = handed[:state_size].reshape(end_state.shape)
    got_totals = handed[state_size : state_size + totals_size].reshape(end_totals.shape)
    got_tag = handed[state_size + totals_size :]
    initial = (got_state, got_totals, got_tag[0].astype(jnp.int32) - 1)
    block_len = min(256, rows_here)
    blocks = rows_here // block_len

    def regroup(values):
        return jnp.transpose(
            values.reshape(values.shape[0], blocks, block_len, values.shape[-1]), (1, 0, 2, 3)
        )

    scan_inputs = (
        regroup(phi_query),
        regroup(phi_key),
        regroup(query_rows),
        regroup(key_rows),
        regroup(value_rows),
        segments.reshape(blocks, block_len),
    )

    def scan_step(state_carry, block_inputs):
        return block_step(state_carry, block_inputs, FEAT)

    _, (mixed_out, state_norm) = lax.scan(scan_step, initial, scan_inputs)
    attended = (
        jnp.transpose(mixed_out, (0, 2, 1, 3))
        .reshape(rows_here, heads_here * HD)
        .astype(jnp.bfloat16)
    )
    group_vocab, attended = lax.optimization_barrier((group_vocab, attended))
    state_norms = jnp.transpose(state_norm, (1, 0, 2)).reshape(heads_here, rows_here)
    request_ids = jnp.arange(request_adapter.shape[0], dtype=jnp.int32)
    adapter_of = jnp.sum(
        jnp.where(segments[:, None] == request_ids[None, :], request_adapter[None, :], 0), axis=1
    )
    adapter_ids = jnp.arange(adapter_slot.shape[0], dtype=jnp.int32)
    slot_ids = jnp.sum(
        jnp.where(adapter_of[:, None] == adapter_ids[None, :], adapter_slot[None, :], 0), axis=1
    )
    column_slot = jnp.arange(lowered.shape[1], dtype=jnp.int32) // RANK
    local_slot = slot_ids - own_shard * (lowered.shape[1] // RANK)
    low_rank = jnp.where(
        local_slot[:, None] == column_slot[None, :], lowered, jnp.zeros_like(lowered)
    )
    out_blocks = out_weight.reshape(out_weight.shape[0], shards, slice_width)
    up_blocks = adapter_up.reshape(adapter_up.shape[0], shards, slice_width)
    partial_value = jnp.einsum(
        "rk,kjc->jrc", attended, out_blocks, preferred_element_type=jnp.float32
    ) + jnp.einsum("rk,kjc->jrc", low_rank, up_blocks, preferred_element_type=jnp.float32)
    vocab_blocks = jnp.transpose(
        group_vocab.reshape(group_vocab.shape[0], shards, slice_width), (1, 0, 2)
    )
    summed, best = mp_exchange(partial_value.astype(jnp.bfloat16), residual, vocab_blocks)
    max_logits = best[:, 0]
    return (summed, state_norms, max_logits)


def solution(mesh):
    placed = (
        P("group", None),
        P(),
        P(None, "mp"),
        P("mp", None),
        P(None, "mp"),
        P("mp", None),
        P(("group", "mp"), None),
        P("group"),
        P(),
        P(),
        P(),
    )
    return jax.shard_map(
        on_device,
        mesh=mesh,
        in_specs=placed,
        out_specs=(P("group", "mp"), P("mp", "group"), P(("group", "mp"))),
        check_vma=False,
    )
```

```python
import jax
import jax.numpy as jnp
from jax import lax
from jax.sharding import PartitionSpec as P
from jax.experimental import pallas as pl
from jax.experimental.pallas import tpu as pltpu

FEAT = 16
HD = 112
RANK = 16


EPSILON = 1e-05
PRECISE = lax.Precision.HIGHEST


def from_behind(value, axis, by):
    size = lax.axis_size(axis)
    pairs = [(i, i + by) for i in range(size) if 0 <= i + by < size]
    return lax.ppermute(value, axis, pairs)


def rms_normed(values, norm_gain):
    wide = values.astype(jnp.float32)
    meansq = jnp.mean(wide * wide, axis=-1, keepdims=True)
    return (wide * lax.rsqrt(meansq + EPSILON) * norm_gain).astype(jnp.bfloat16)


def features(vectors, feat_width):
    linear_part = vectors / feat_width**0.25
    outer_part = (vectors[..., :, None] * vectors[..., None, :]).reshape(
        vectors.shape[:-1] + (feat_width * feat_width,)
    )
    outer_part = outer_part / (2.0 * feat_width) ** 0.5
    ones_part = jnp.ones(vectors.shape[:-1] + (1,), jnp.float32)
    return jnp.concatenate([ones_part, linear_part, outer_part], axis=-1)


def block_step(state_carry, block_inputs, feat_width):
    states, totals, owner_seg = state_carry
    phi_query, phi_key, query_rows, key_rows, value_rows, seg_ids = block_inputs
    scaling = feat_width ** (-0.5)
    block_len = seg_ids.shape[0]
    position = jnp.arange(block_len, dtype=jnp.int32)
    allowed = (
        (position[:, None] >= position[None, :]) & (seg_ids[:, None] == seg_ids[None, :])
    ).astype(jnp.float32)
    carried = (seg_ids == owner_seg).astype(jnp.float32)[None, :]
    scores = jnp.einsum("hcf,hdf->hcd", query_rows, key_rows, precision=PRECISE) * scaling
    weights = (1.0 + scores + 0.5 * scores * scores) * allowed[None]
    numerator = jnp.einsum("hcd,hde->hce", weights, value_rows, precision=PRECISE)
    numerator = numerator + carried[..., None] * jnp.einsum(
        "hcp,hpe->hce", phi_query, states, precision=PRECISE
    )
    denominator = jnp.sum(weights, axis=-1) + carried * jnp.einsum(
        "hcp,hp->hc", phi_query, totals, precision=PRECISE
    )
    mixed_out = numerator / denominator[..., None]
    key_scores = jnp.einsum("hcf,hdf->hcd", key_rows, key_rows, precision=PRECISE) * scaling
    value_gram = jnp.einsum("hce,hde->hcd", value_rows, value_rows, precision=PRECISE)
    key_gram = (1.0 + key_scores + 0.5 * key_scores * key_scores) * value_gram
    diagonal = (position[:, None] == position[None, :]).astype(jnp.float32)
    row_terms = jnp.sum(key_gram * (allowed * (2.0 - diagonal))[None], axis=-1)
    local_squares = jnp.einsum("cd,hd->hc", allowed, row_terms, precision=PRECISE)
    along = jnp.sum(
        jnp.einsum("hcp,hpe->hce", phi_key, states, precision=PRECISE) * value_rows, axis=-1
    )
    cross_squares = jnp.einsum("cd,hd->hc", allowed, along, precision=PRECISE)
    state_squares = jnp.sum(states * states, axis=(1, 2))
    squares = carried * (state_squares[:, None] + 2.0 * cross_squares) + local_squares
    counted = carried * totals[:, :1] + jnp.sum(allowed, axis=-1)[None, :]
    state_norm = jnp.sqrt(squares / (counted * (feat_width * value_rows.shape[-1])))
    last_seg = seg_ids[-1]
    member = (seg_ids == last_seg).astype(jnp.float32)
    continues = (owner_seg == last_seg).astype(jnp.float32)
    new_states = continues * states + jnp.einsum(
        "hcp,hce->hpe", phi_key * member[None, :, None], value_rows, precision=PRECISE
    )
    new_totals = continues * totals + jnp.einsum("hcp,c->hp", phi_key, member, precision=PRECISE)
    return ((new_states, new_totals, last_seg), (mixed_out, state_norm))


def best_of(candidates, piece):
    logits = jnp.einsum("rd,vd->rv", candidates, piece, preferred_element_type=jnp.float32)
    return jnp.max(logits, axis=1)


def top_kernel(tops, best_ref, got, sems):
    n = tops.shape[0]
    me = lax.axis_index("mp")
    grp = lax.axis_index("group")
    peers = [lax.rem(me + k, n) for k in range(1, n)]
    mesh_id = pl.DeviceIdType.MESH
    barrier = pltpu.get_barrier_semaphore()
    for p in peers:
        pl.semaphore_signal(barrier, inc=1, device_id=(grp, p), device_id_type=mesh_id)
    pl.semaphore_wait(barrier, n - 1)
    sent = []
    for p in peers:
        copy = pltpu.make_async_remote_copy(
            src_ref=tops.at[p],
            dst_ref=got.at[me],
            send_sem=sems.at[0, p],
            recv_sem=sems.at[1, me],
            device_id=(grp, p),
            device_id_type=mesh_id,
        )
        copy.start()
        sent.append(copy)
    for copy in sent:
        copy.wait_send()
    for q in peers:
        pltpu.make_async_remote_copy(
            src_ref=tops.at[q],
            dst_ref=got.at[q],
            send_sem=sems.at[0, q],
            recv_sem=sems.at[1, q],
            device_id=(grp, q),
            device_id_type=mesh_id,
        ).wait_recv()
    best = tops[me]
    for q in peers:
        best = jnp.maximum(best, got[q])
    best_ref[...] = best


def mp_max(partial_best, shards):
    block_rows = partial_best.shape[0] // shards
    tops = jnp.broadcast_to(partial_best.reshape(shards, block_rows, 1), (shards, block_rows, 128))
    vmem = pl.BlockSpec(memory_space=pltpu.VMEM)
    best = pl.pallas_call(
        top_kernel,
        out_shape=jax.ShapeDtypeStruct((block_rows, 128), jnp.float32),
        in_specs=[vmem],
        out_specs=vmem,
        scratch_shapes=[
            pltpu.VMEM((shards, block_rows, 128), jnp.float32),
            pltpu.SemaphoreType.DMA((2, shards)),
        ],
        compiler_params=pltpu.CompilerParams(collective_id=0, has_side_effects=True),
    )(tops)
    return best[:, 0]


def on_device(
    hidden,
    norm_gain,
    qkv_weight,
    out_weight,
    adapter_down,
    adapter_up,
    vocab_rows,
    segments,
    request_adapter,
    adapter_slot,
    page_table,
):
    groups = lax.axis_size("group")
    own_group = lax.axis_index("group")
    shards = lax.axis_size("mp")
    own_shard = lax.axis_index("mp")
    rows_here = segments.shape[0]
    model_width = hidden.shape[1]
    slice_width = model_width // shards
    table = page_table.reshape(groups, -1)
    per_group = table.shape[1]
    per_peer = per_group // groups
    page_len = rows_here // per_group
    holders = table // per_group
    position = jnp.arange(per_group, dtype=jnp.int32)
    sort_keys = jnp.where(holders == own_group, position[None, :], per_group + position[None, :])
    ranked = jnp.argsort(sort_keys, axis=1)[:, :per_peer]
    picked = jnp.take_along_axis(table, ranked, axis=1) - own_group * per_group
    outgoing = hidden.reshape(per_group, page_len, model_width)[picked]
    normed_pages = rms_normed(outgoing, norm_gain)
    projected_pages = jnp.einsum(
        "abrd,dc->abrc", normed_pages, qkv_weight, preferred_element_type=jnp.float32
    ).astype(jnp.bfloat16)
    lowered_pages = jnp.einsum(
        "abrd,dc->abrc", normed_pages, adapter_down, preferred_element_type=jnp.float32
    ).astype(jnp.bfloat16)
    kept_pages = lax.dynamic_slice_in_dim(outgoing, own_shard * slice_width, slice_width, 3)
    widths = (kept_pages.shape[3], projected_pages.shape[3], lowered_pages.shape[3])
    packed = lax.all_to_all(
        jnp.concatenate([kept_pages, projected_pages, lowered_pages], axis=3),
        "group", split_axis=0, concat_axis=0, tiled=True,
    )
    arrived = (
        packed[..., : widths[0]],
        packed[..., widths[0] : widths[0] + widths[1]],
        packed[..., widths[0] + widths[1] :],
    )
    own_holders = lax.dynamic_index_in_dim(holders, own_group, 0, keepdims=False)
    onehot = (own_holders[:, None] == jnp.arange(groups, dtype=jnp.int32)[None, :]).astype(
        jnp.int32
    )
    earlier = jnp.sum((jnp.cumsum(onehot, axis=0) - onehot) * onehot, axis=1)
    source_rows = own_holders * per_peer + earlier

    def placed(received):
        gathered_rows = received.reshape((groups * per_peer,) + received.shape[2:])[source_rows]
        return gathered_rows.reshape((rows_here,) + received.shape[3:])

    residual, projected, lowered = [placed(received) for received in arrived]
    group_vocab = lax.all_gather(vocab_rows, "group", axis=0, tiled=True)
    heads_here = projected.shape[1] // (2 * FEAT + HD)
    split_heads = jnp.transpose(
        projected.reshape(rows_here, heads_here, 2 * FEAT + HD).astype(jnp.float32), (1, 0, 2)
    )
    query_rows = split_heads[..., :FEAT]
    key_rows = split_heads[..., FEAT : 2 * FEAT]
    value_rows = split_heads[..., 2 * FEAT :]
    phi_query = features(query_rows, FEAT)
    phi_key = features(key_rows, FEAT)
    last_seg = segments[-1]
    member = (segments == last_seg).astype(jnp.float32)
    end_state = jnp.einsum(
        "hcp,hce->hpe", phi_key * member[None, :, None], value_rows, precision=PRECISE
    )
    end_totals = jnp.einsum("hcp,c->hp", phi_key, member, precision=PRECISE)
    end_tag = jnp.reshape(last_seg + 1, (1,)).astype(jnp.float32)
    state_size, totals_size = end_state.size, end_totals.size
    handed = from_behind(
        jnp.concatenate(
            [end_state.reshape(-1), end_totals.reshape(-1), end_tag]
        ).astype(jnp.bfloat16),
        "group",
        1,
    ).astype(jnp.float32)
    got_state = handed[:state_size].reshape(end_state.shape)
    got_totals = handed[state_size : state_size + totals_size].reshape(end_totals.shape)
    got_tag = handed[state_size + totals_size :]
    initial = (got_state, got_totals, got_tag[0].astype(jnp.int32) - 1)
    block_len = rows_here
    blocks = rows_here // block_len

    def regroup(values):
        return jnp.transpose(
            values.reshape(values.shape[0], blocks, block_len, values.shape[-1]), (1, 0, 2, 3)
        )

    scan_inputs = (
        regroup(phi_query),
        regroup(phi_key),
        regroup(query_rows),
        regroup(key_rows),
        regroup(value_rows),
        segments.reshape(blocks, block_len),
    )

    def scan_step(state_carry, block_inputs):
        return block_step(state_carry, block_inputs, FEAT)

    _, (mixed_out, state_norm) = lax.scan(scan_step, initial, scan_inputs)
    attended = (
        jnp.transpose(mixed_out, (0, 2, 1, 3))
        .reshape(rows_here, heads_here * HD)
        .astype(jnp.bfloat16)
    )
    group_vocab, attended = lax.optimization_barrier((group_vocab, attended))
    state_norms = jnp.transpose(state_norm, (1, 0, 2)).reshape(heads_here, rows_here)
    request_ids = jnp.arange(request_adapter.shape[0], dtype=jnp.int32)
    adapter_of = jnp.sum(
        jnp.where(segments[:, None] == request_ids[None, :], request_adapter[None, :], 0), axis=1
    )
    adapter_ids = jnp.arange(adapter_slot.shape[0], dtype=jnp.int32)
    slot_ids = jnp.sum(
        jnp.where(adapter_of[:, None] == adapter_ids[None, :], adapter_slot[None, :], 0), axis=1
    )
    column_slot = jnp.arange(lowered.shape[1], dtype=jnp.int32) // RANK
    local_slot = slot_ids - own_shard * (lowered.shape[1] // RANK)
    low_rank = jnp.where(
        local_slot[:, None] == column_slot[None, :], lowered, jnp.zeros_like(lowered)
    )
    partial_value = jnp.dot(attended, out_weight, preferred_element_type=jnp.float32)
    partial_value = partial_value + jnp.dot(
        low_rank, adapter_up, preferred_element_type=jnp.float32
    )
    summed = lax.psum_scatter(
        partial_value.astype(jnp.bfloat16), "mp", scatter_dimension=1, tiled=True
    )
    final_rows = (residual.astype(jnp.float32) + summed.astype(jnp.float32)).astype(jnp.bfloat16)
    group_rows = lax.all_gather(final_rows, "mp", axis=1, tiled=True)
    partial_best = best_of(group_rows, group_vocab)
    max_logits = mp_max(partial_best, shards)
    return (summed, state_norms, max_logits)


def solution(mesh):
    placed = (
        P("group", None),
        P(),
        P(None, "mp"),
        P("mp", None),
        P(None, "mp"),
        P("mp", None),
        P(("group", "mp"), None),
        P("group"),
        P(),
        P(),
        P(),
    )
    return jax.shard_map(
        on_device,
        mesh=mesh,
        in_specs=placed,
        out_specs=(P("group", "mp"), P("mp", "group"), P(("group", "mp"))),
        check_vma=False,
    )
```

```python
import jax
import jax.numpy as jnp
from jax import lax
from jax.sharding import PartitionSpec as P
from jax.experimental import pallas as pl
from jax.experimental.pallas import tpu as pltpu

FEAT = 16
HD = 112
RANK = 16


EPSILON = 1e-05
PRECISE = lax.Precision.HIGHEST


def from_behind(value, axis, by):
    size = lax.axis_size(axis)
    pairs = [(i, i + by) for i in range(size) if 0 <= i + by < size]
    return lax.ppermute(value, axis, pairs)


def rms_normed(values, norm_gain):
    wide = values.astype(jnp.float32)
    meansq = jnp.mean(wide * wide, axis=-1, keepdims=True)
    return (wide * lax.rsqrt(meansq + EPSILON) * norm_gain).astype(jnp.bfloat16)


def features(vectors, feat_width):
    linear_part = vectors / feat_width**0.25
    outer_part = (vectors[..., :, None] * vectors[..., None, :]).reshape(
        vectors.shape[:-1] + (feat_width * feat_width,)
    )
    outer_part = outer_part / (2.0 * feat_width) ** 0.5
    ones_part = jnp.ones(vectors.shape[:-1] + (1,), jnp.float32)
    return jnp.concatenate([ones_part, linear_part, outer_part], axis=-1)


def block_step(state_carry, block_inputs, feat_width):
    states, totals, owner_seg = state_carry
    phi_query, phi_key, query_rows, key_rows, value_rows, seg_ids = block_inputs
    scaling = feat_width ** (-0.5)
    block_len = seg_ids.shape[0]
    position = jnp.arange(block_len, dtype=jnp.int32)
    allowed = (
        (position[:, None] >= position[None, :]) & (seg_ids[:, None] == seg_ids[None, :])
    ).astype(jnp.float32)
    carried = (seg_ids == owner_seg).astype(jnp.float32)[None, :]
    scores = jnp.einsum("hcf,hdf->hcd", query_rows, key_rows, precision=PRECISE) * scaling
    weights = (1.0 + scores + 0.5 * scores * scores) * allowed[None]
    numerator = jnp.einsum("hcd,hde->hce", weights, value_rows, precision=PRECISE)
    numerator = numerator + carried[..., None] * jnp.einsum(
        "hcp,hpe->hce", phi_query, states, precision=PRECISE
    )
    denominator = jnp.sum(weights, axis=-1) + carried * jnp.einsum(
        "hcp,hp->hc", phi_query, totals, precision=PRECISE
    )
    mixed_out = numerator / denominator[..., None]
    key_scores = jnp.einsum("hcf,hdf->hcd", key_rows, key_rows, precision=PRECISE) * scaling
    value_gram = jnp.einsum("hce,hde->hcd", value_rows, value_rows, precision=PRECISE)
    key_gram = (1.0 + key_scores + 0.5 * key_scores * key_scores) * value_gram
    diagonal = (position[:, None] == position[None, :]).astype(jnp.float32)
    row_terms = jnp.sum(key_gram * (allowed * (2.0 - diagonal))[None], axis=-1)
    local_squares = jnp.einsum("cd,hd->hc", allowed, row_terms, precision=PRECISE)
    along = jnp.sum(
        jnp.einsum("hcp,hpe->hce", phi_key, states, precision=PRECISE) * value_rows, axis=-1
    )
    cross_squares = jnp.einsum("cd,hd->hc", allowed, along, precision=PRECISE)
    state_squares = jnp.sum(states * states, axis=(1, 2))
    squares = carried * (state_squares[:, None] + 2.0 * cross_squares) + local_squares
    counted = carried * totals[:, :1] + jnp.sum(allowed, axis=-1)[None, :]
    state_norm = jnp.sqrt(squares / (counted * (feat_width * value_rows.shape[-1])))
    last_seg = seg_ids[-1]
    member = (seg_ids == last_seg).astype(jnp.float32)
    continues = (owner_seg == last_seg).astype(jnp.float32)
    new_states = continues * states + jnp.einsum(
        "hcp,hce->hpe", phi_key * member[None, :, None], value_rows, precision=PRECISE
    )
    new_totals = continues * totals + jnp.einsum("hcp,c->hp", phi_key, member, precision=PRECISE)
    return ((new_states, new_totals, last_seg), (mixed_out, state_norm))


def best_of(candidates, piece):
    logits = jnp.einsum("rd,vd->rv", candidates, piece, preferred_element_type=jnp.float32)
    return jnp.max(logits, axis=1)


def exchange_kernel(
    part_ref, resid_ref, vocab_ref, upd_ref, best_ref,
    land, acc, rows, tops, got, ring_sems, top_sems,
):
    n = part_ref.shape[0]
    quarter = part_ref.shape[1] // 4
    block_rows = best_ref.shape[0]
    me = lax.axis_index("mp")
    grp = lax.axis_index("group")
    peers = [lax.rem(me + k, n) for k in range(1, n)]
    mesh_id = pl.DeviceIdType.MESH
    towards = (lax.rem(me + 1, n), lax.rem(me + n - 1, n))
    chains = [(0, 0), (1, 2), (0, 1), (1, 3)]
    spans = [pl.ds(quarter * piece, quarter) for _, piece in chains]

    barrier = pltpu.get_barrier_semaphore()
    for p in peers:
        pl.semaphore_signal(barrier, inc=1, device_id=(grp, p), device_id_type=mesh_id)
    pl.semaphore_wait(barrier, n - 1)

    def ring_copy(phase, chain, step, src, dst):
        return pltpu.make_async_remote_copy(
            src_ref=src,
            dst_ref=dst,
            send_sem=ring_sems.at[phase, chain, 0, step],
            recv_sem=ring_sems.at[phase, chain, 1, step],
            device_id=(grp, towards[chains[chain][0]]),
            device_id_type=mesh_id,
        )

    def rs_chunk(chain, step):
        way = chains[chain][0]
        return lax.rem(me + (n - 1 - step if way == 0 else 1 + step) + n, n)

    pending = [None] * len(chains)
    for step in range(n - 1):
        for chain in range(len(chains)):
            chunk = rs_chunk(chain, step)
            if step == 0:
                src = part_ref.at[chunk, spans[chain]]
            else:
                pending[chain].wait()
                acc[chain, step] = (
                    land[chain, step - 1].astype(jnp.float32)
                    + part_ref[chunk, spans[chain]].astype(jnp.float32)
                ).astype(acc.dtype)
                src = acc.at[chain, step]
            pending[chain] = ring_copy(0, chain, step, src, land.at[chain, step])
            pending[chain].start()
    for chain in range(len(chains)):
        pending[chain].wait()
        total = land[chain, n - 2].astype(jnp.float32) + part_ref[
            me, spans[chain]
        ].astype(jnp.float32)
        update = total.astype(upd_ref.dtype)
        upd_ref[spans[chain]] = update
        rows[me, spans[chain]] = (
            resid_ref[spans[chain]].astype(jnp.float32) + update.astype(jnp.float32)
        ).astype(rows.dtype)

    for step in range(n - 1):
        for chain in range(len(chains)):
            if step > 0:
                pending[chain].wait()
            way = chains[chain][0]
            chunk = lax.rem(me + (n - step if way == 0 else step), n)
            view = rows.at[chunk, spans[chain]]
            pending[chain] = ring_copy(1, chain, step, view, view)
            pending[chain].start()
    for chain in range(len(chains)):
        pending[chain].wait()

    scores = jnp.zeros((rows.shape[1], vocab_ref.shape[0] * vocab_ref.shape[2]), jnp.float32)
    for j in range(n):
        block = vocab_ref[:, j].reshape(scores.shape[1], rows.shape[2])
        scores = scores + lax.dot_general(
            rows[j], block, (((1,), (1,)), ((), ())),
            preferred_element_type=jnp.float32,
        )
    for p in range(n):
        piece = jnp.max(scores[p * block_rows : (p + 1) * block_rows], axis=1, keepdims=True)
        tops[p] = jnp.broadcast_to(piece, tops.shape[1:])

    sent = []
    for p in peers:
        copy = pltpu.make_async_remote_copy(
            src_ref=tops.at[p],
            dst_ref=got.at[me],
            send_sem=top_sems.at[0, p],
            recv_sem=top_sems.at[1, me],
            device_id=(grp, p),
            device_id_type=mesh_id,
        )
        copy.start()
        sent.append(copy)
    for copy in sent:
        copy.wait_send()
    for q in peers:
        pltpu.make_async_remote_copy(
            src_ref=tops.at[q],
            dst_ref=got.at[q],
            send_sem=top_sems.at[0, q],
            recv_sem=top_sems.at[1, q],
            device_id=(grp, q),
            device_id_type=mesh_id,
        ).wait_recv()
    best = tops[me]
    for q in peers:
        best = jnp.maximum(best, got[q])
    best_ref[...] = best


def mp_exchange(parts, residual, vocab_blocks):
    n, rows_here, width = parts.shape
    block_rows = rows_here // n
    chains = 4
    vmem = pl.BlockSpec(memory_space=pltpu.VMEM)
    return pl.pallas_call(
        exchange_kernel,
        out_shape=(
            jax.ShapeDtypeStruct((rows_here, width), jnp.bfloat16),
            jax.ShapeDtypeStruct((block_rows, 128), jnp.float32),
        ),
        in_specs=[vmem] * 3,
        out_specs=(vmem, vmem),
        scratch_shapes=[
            pltpu.VMEM((chains, n - 1, rows_here // chains, width), jnp.bfloat16),
            pltpu.VMEM((chains, n - 1, rows_here // chains, width), jnp.bfloat16),
            pltpu.VMEM((n, rows_here, width), jnp.bfloat16),
            pltpu.VMEM((n, block_rows, 128), jnp.float32),
            pltpu.VMEM((n, block_rows, 128), jnp.float32),
            pltpu.SemaphoreType.DMA((2, chains, 2, n - 1)),
            pltpu.SemaphoreType.DMA((2, n)),
        ],
        compiler_params=pltpu.CompilerParams(collective_id=0, has_side_effects=True),
    )(parts, residual, vocab_blocks)


def on_device(
    hidden,
    norm_gain,
    qkv_weight,
    out_weight,
    adapter_down,
    adapter_up,
    vocab_rows,
    segments,
    request_adapter,
    adapter_slot,
    page_table,
):
    groups = lax.axis_size("group")
    own_group = lax.axis_index("group")
    shards = lax.axis_size("mp")
    own_shard = lax.axis_index("mp")
    rows_here = segments.shape[0]
    model_width = hidden.shape[1]
    slice_width = model_width // shards
    table = page_table.reshape(groups, -1)
    per_group = table.shape[1]
    per_peer = per_group // groups
    page_len = rows_here // per_group
    holders = table // per_group
    position = jnp.arange(per_group, dtype=jnp.int32)
    sort_keys = jnp.where(holders == own_group, position[None, :], per_group + position[None, :])
    ranked = jnp.argsort(sort_keys, axis=1)[:, :per_peer]
    picked = jnp.take_along_axis(table, ranked, axis=1) - own_group * per_group
    outgoing = hidden.reshape(per_group, page_len, model_width)[picked]
    normed_pages = rms_normed(outgoing, norm_gain)
    projected_pages = jnp.einsum(
        "abrd,dc->abrc", normed_pages, qkv_weight, preferred_element_type=jnp.float32
    ).astype(jnp.bfloat16)
    lowered_pages = jnp.einsum(
        "abrd,dc->abrc", normed_pages, adapter_down, preferred_element_type=jnp.float32
    ).astype(jnp.bfloat16)
    kept_pages = lax.dynamic_slice_in_dim(outgoing, own_shard * slice_width, slice_width, 3)
    widths = (kept_pages.shape[3], projected_pages.shape[3], lowered_pages.shape[3])
    packed = lax.all_to_all(
        jnp.concatenate([kept_pages, projected_pages, lowered_pages], axis=3),
        "group", split_axis=0, concat_axis=0, tiled=True,
    )
    arrived = (
        packed[..., : widths[0]],
        packed[..., widths[0] : widths[0] + widths[1]],
        packed[..., widths[0] + widths[1] :],
    )
    own_holders = lax.dynamic_index_in_dim(holders, own_group, 0, keepdims=False)
    onehot = (own_holders[:, None] == jnp.arange(groups, dtype=jnp.int32)[None, :]).astype(
        jnp.int32
    )
    earlier = jnp.sum((jnp.cumsum(onehot, axis=0) - onehot) * onehot, axis=1)
    source_rows = own_holders * per_peer + earlier

    def placed(received):
        gathered_rows = received.reshape((groups * per_peer,) + received.shape[2:])[source_rows]
        return gathered_rows.reshape((rows_here,) + received.shape[3:])

    residual, projected, lowered = [placed(received) for received in arrived]
    vocab_pieces = jnp.transpose(
        vocab_rows.reshape(vocab_rows.shape[0], shards, slice_width), (1, 0, 2)
    )
    group_vocab = lax.all_gather(vocab_pieces[None], "group", axis=0, tiled=True)
    heads_here = projected.shape[1] // (2 * FEAT + HD)
    split_heads = jnp.transpose(
        projected.reshape(rows_here, heads_here, 2 * FEAT + HD).astype(jnp.float32), (1, 0, 2)
    )
    query_rows = split_heads[..., :FEAT]
    key_rows = split_heads[..., FEAT : 2 * FEAT]
    value_rows = split_heads[..., 2 * FEAT :]
    phi_query = features(query_rows, FEAT)
    phi_key = features(key_rows, FEAT)
    last_seg = segments[-1]
    member = (segments == last_seg).astype(jnp.float32)
    end_state = jnp.einsum(
        "hcp,hce->hpe", phi_key * member[None, :, None], value_rows, precision=PRECISE
    )
    end_totals = jnp.einsum("hcp,c->hp", phi_key, member, precision=PRECISE)
    end_tag = jnp.reshape(last_seg + 1, (1,)).astype(jnp.float32)
    state_size, totals_size = end_state.size, end_totals.size
    handed = from_behind(
        jnp.concatenate(
            [end_state.reshape(-1), end_totals.reshape(-1), end_tag]
        ).astype(jnp.bfloat16),
        "group",
        1,
    ).astype(jnp.float32)
    got_state = handed[:state_size].reshape(end_state.shape)
    got_totals = handed[state_size : state_size + totals_size].reshape(end_totals.shape)
    got_tag = handed[state_size + totals_size :]
    initial = (got_state, got_totals, got_tag[0].astype(jnp.int32) - 1)
    block_len = rows_here
    blocks = rows_here // block_len

    def regroup(values):
        return jnp.transpose(
            values.reshape(values.shape[0], blocks, block_len, values.shape[-1]), (1, 0, 2, 3)
        )

    scan_inputs = (
        regroup(phi_query),
        regroup(phi_key),
        regroup(query_rows),
        regroup(key_rows),
        regroup(value_rows),
        segments.reshape(blocks, block_len),
    )

    def scan_step(state_carry, block_inputs):
        return block_step(state_carry, block_inputs, FEAT)

    _, (mixed_out, state_norm) = lax.scan(scan_step, initial, scan_inputs)
    attended = (
        jnp.transpose(mixed_out, (0, 2, 1, 3))
        .reshape(rows_here, heads_here * HD)
        .astype(jnp.bfloat16)
    )
    group_vocab, attended = lax.optimization_barrier((group_vocab, attended))
    state_norms = jnp.transpose(state_norm, (1, 0, 2)).reshape(heads_here, rows_here)
    request_ids = jnp.arange(request_adapter.shape[0], dtype=jnp.int32)
    adapter_of = jnp.sum(
        jnp.where(segments[:, None] == request_ids[None, :], request_adapter[None, :], 0), axis=1
    )
    adapter_ids = jnp.arange(adapter_slot.shape[0], dtype=jnp.int32)
    slot_ids = jnp.sum(
        jnp.where(adapter_of[:, None] == adapter_ids[None, :], adapter_slot[None, :], 0), axis=1
    )
    column_slot = jnp.arange(lowered.shape[1], dtype=jnp.int32) // RANK
    local_slot = slot_ids - own_shard * (lowered.shape[1] // RANK)
    low_rank = jnp.where(
        local_slot[:, None] == column_slot[None, :], lowered, jnp.zeros_like(lowered)
    )
    out_blocks = jnp.transpose(out_weight.reshape(out_weight.shape[0], shards, slice_width), (1, 0, 2))
    up_blocks = jnp.transpose(adapter_up.reshape(adapter_up.shape[0], shards, slice_width), (1, 0, 2))
    partial_value = jnp.einsum(
        "rk,jkc->jrc", attended, out_blocks, preferred_element_type=jnp.float32
    ) + jnp.einsum("rk,jkc->jrc", low_rank, up_blocks, preferred_element_type=jnp.float32)
    summed, best = mp_exchange(partial_value.astype(jnp.bfloat16), residual, group_vocab)
    max_logits = best[:, 0]
    return (summed, state_norms, max_logits)


def solution(mesh):
    placed = (
        P("group", None),
        P(),
        P(None, "mp"),
        P("mp", None),
        P(None, "mp"),
        P("mp", None),
        P(("group", "mp"), None),
        P("group"),
        P(),
        P(),
        P(),
    )
    return jax.shard_map(
        on_device,
        mesh=mesh,
        in_specs=placed,
        out_specs=(P("group", "mp"), P("mp", "group"), P(("group", "mp"))),
        check_vma=False,
    )
```

```python
import jax
import jax.numpy as jnp
from jax import lax
from jax.sharding import PartitionSpec as P
from jax.experimental import pallas as pl
from jax.experimental.pallas import tpu as pltpu

FEAT = 16
HD = 112
RANK = 16


EPSILON = 1e-05
PRECISE = lax.Precision.HIGHEST


def from_behind(value, axis, by):
    size = lax.axis_size(axis)
    pairs = [(i, i + by) for i in range(size) if 0 <= i + by < size]
    return lax.ppermute(value, axis, pairs)


def rms_normed(values, norm_gain):
    wide = values.astype(jnp.float32)
    meansq = jnp.mean(wide * wide, axis=-1, keepdims=True)
    return (wide * lax.rsqrt(meansq + EPSILON) * norm_gain).astype(jnp.bfloat16)


def features(vectors, feat_width):
    linear_part = vectors / feat_width**0.25
    outer_part = (vectors[..., :, None] * vectors[..., None, :]).reshape(
        vectors.shape[:-1] + (feat_width * feat_width,)
    )
    outer_part = outer_part / (2.0 * feat_width) ** 0.5
    ones_part = jnp.ones(vectors.shape[:-1] + (1,), jnp.float32)
    return jnp.concatenate([ones_part, linear_part, outer_part], axis=-1)


def block_step(state_carry, block_inputs, feat_width):
    states, totals, owner_seg = state_carry
    phi_query, phi_key, query_rows, key_rows, value_rows, seg_ids = block_inputs
    scaling = feat_width ** (-0.5)
    block_len = seg_ids.shape[0]
    position = jnp.arange(block_len, dtype=jnp.int32)
    allowed = (
        (position[:, None] >= position[None, :]) & (seg_ids[:, None] == seg_ids[None, :])
    ).astype(jnp.float32)
    carried = (seg_ids == owner_seg).astype(jnp.float32)[None, :]
    scores = jnp.einsum("hcf,hdf->hcd", query_rows, key_rows, precision=PRECISE) * scaling
    weights = (1.0 + scores + 0.5 * scores * scores) * allowed[None]
    numerator = jnp.einsum("hcd,hde->hce", weights, value_rows, precision=PRECISE)
    numerator = numerator + carried[..., None] * jnp.einsum(
        "hcp,hpe->hce", phi_query, states, precision=PRECISE
    )
    denominator = jnp.sum(weights, axis=-1) + carried * jnp.einsum(
        "hcp,hp->hc", phi_query, totals, precision=PRECISE
    )
    mixed_out = numerator / denominator[..., None]
    key_scores = jnp.einsum("hcf,hdf->hcd", key_rows, key_rows, precision=PRECISE) * scaling
    value_gram = jnp.einsum("hce,hde->hcd", value_rows, value_rows, precision=PRECISE)
    key_gram = (1.0 + key_scores + 0.5 * key_scores * key_scores) * value_gram
    diagonal = (position[:, None] == position[None, :]).astype(jnp.float32)
    row_terms = jnp.sum(key_gram * (allowed * (2.0 - diagonal))[None], axis=-1)
    local_squares = jnp.einsum("cd,hd->hc", allowed, row_terms, precision=PRECISE)
    along = jnp.sum(
        jnp.einsum("hcp,hpe->hce", phi_key, states, precision=PRECISE) * value_rows, axis=-1
    )
    cross_squares = jnp.einsum("cd,hd->hc", allowed, along, precision=PRECISE)
    state_squares = jnp.sum(states * states, axis=(1, 2))
    squares = carried * (state_squares[:, None] + 2.0 * cross_squares) + local_squares
    counted = carried * totals[:, :1] + jnp.sum(allowed, axis=-1)[None, :]
    state_norm = jnp.sqrt(squares / (counted * (feat_width * value_rows.shape[-1])))
    last_seg = seg_ids[-1]
    member = (seg_ids == last_seg).astype(jnp.float32)
    continues = (owner_seg == last_seg).astype(jnp.float32)
    new_states = continues * states + jnp.einsum(
        "hcp,hce->hpe", phi_key * member[None, :, None], value_rows, precision=PRECISE
    )
    new_totals = continues * totals + jnp.einsum("hcp,c->hp", phi_key, member, precision=PRECISE)
    return ((new_states, new_totals, last_seg), (mixed_out, state_norm))


def best_of(candidates, piece):
    logits = jnp.einsum("rd,vd->rv", candidates, piece, preferred_element_type=jnp.float32)
    return jnp.max(logits, axis=1)


def exchange_kernel(
    part_ref, resid_ref, vocab_ref, upd_ref, best_ref,
    land, acc, rows, tops, got, ring_sems, top_sems,
):
    n = part_ref.shape[0]
    quarter = part_ref.shape[1] // 4
    block_rows = best_ref.shape[0]
    me = lax.axis_index("mp")
    grp = lax.axis_index("group")
    peers = [lax.rem(me + k, n) for k in range(1, n)]
    mesh_id = pl.DeviceIdType.MESH
    towards = (lax.rem(me + 1, n), lax.rem(me + n - 1, n))
    chains = [(0, 0), (1, 2), (0, 1), (1, 3)]
    spans = [pl.ds(quarter * piece, quarter) for _, piece in chains]

    barrier = pltpu.get_barrier_semaphore()
    for p in peers:
        pl.semaphore_signal(barrier, inc=1, device_id=(grp, p), device_id_type=mesh_id)
    pl.semaphore_wait(barrier, n - 1)

    def ring_copy(phase, chain, step, src, dst):
        return pltpu.make_async_remote_copy(
            src_ref=src,
            dst_ref=dst,
            send_sem=ring_sems.at[phase, chain, 0, step],
            recv_sem=ring_sems.at[phase, chain, 1, step],
            device_id=(grp, towards[chains[chain][0]]),
            device_id_type=mesh_id,
        )

    def rs_chunk(chain, step):
        way = chains[chain][0]
        return lax.rem(me + (n - 1 - step if way == 0 else 1 + step) + n, n)

    pending = [None] * len(chains)
    for step in range(n - 1):
        for chain in range(len(chains)):
            chunk = rs_chunk(chain, step)
            if step == 0:
                src = part_ref.at[chunk, spans[chain]]
            else:
                pending[chain].wait()
                acc[chain, step] = (
                    land[chain, step - 1].astype(jnp.float32)
                    + part_ref[chunk, spans[chain]].astype(jnp.float32)
                ).astype(acc.dtype)
                src = acc.at[chain, step]
            pending[chain] = ring_copy(0, chain, step, src, land.at[chain, step])
            pending[chain].start()
    for chain in range(len(chains)):
        pending[chain].wait()
        total = land[chain, n - 2].astype(jnp.float32) + part_ref[
            me, spans[chain]
        ].astype(jnp.float32)
        update = total.astype(upd_ref.dtype)
        upd_ref[spans[chain]] = update
        rows[me, spans[chain]] = (
            resid_ref[spans[chain]].astype(jnp.float32) + update.astype(jnp.float32)
        ).astype(rows.dtype)

    for step in range(n - 1):
        for chain in range(len(chains)):
            if step > 0:
                pending[chain].wait()
            way = chains[chain][0]
            chunk = lax.rem(me + (n - step if way == 0 else step), n)
            view = rows.at[chunk, spans[chain]]
            pending[chain] = ring_copy(1, chain, step, view, view)
            pending[chain].start()
    for chain in range(len(chains)):
        pending[chain].wait()

    scores = jnp.zeros((rows.shape[1], vocab_ref.shape[0] * vocab_ref.shape[2]), jnp.float32)
    for j in range(n):
        block = vocab_ref[:, j].reshape(scores.shape[1], rows.shape[2])
        scores = scores + lax.dot_general(
            rows[j], block, (((1,), (1,)), ((), ())),
            preferred_element_type=jnp.float32,
        )
    for p in range(n):
        piece = jnp.max(scores[p * block_rows : (p + 1) * block_rows], axis=1, keepdims=True)
        tops[p] = jnp.broadcast_to(piece, tops.shape[1:])

    sent = []
    for p in peers:
        copy = pltpu.make_async_remote_copy(
            src_ref=tops.at[p],
            dst_ref=got.at[me],
            send_sem=top_sems.at[0, p],
            recv_sem=top_sems.at[1, me],
            device_id=(grp, p),
            device_id_type=mesh_id,
        )
        copy.start()
        sent.append(copy)
    for copy in sent:
        copy.wait_send()
    for q in peers:
        pltpu.make_async_remote_copy(
            src_ref=tops.at[q],
            dst_ref=got.at[q],
            send_sem=top_sems.at[0, q],
            recv_sem=top_sems.at[1, q],
            device_id=(grp, q),
            device_id_type=mesh_id,
        ).wait_recv()
    best = tops[me]
    for q in peers:
        best = jnp.maximum(best, got[q])
    best_ref[...] = best


def mp_exchange(parts, residual, vocab_blocks):
    n, rows_here, width = parts.shape
    block_rows = rows_here // n
    chains = 4
    vmem = pl.BlockSpec(memory_space=pltpu.VMEM)
    return pl.pallas_call(
        exchange_kernel,
        out_shape=(
            jax.ShapeDtypeStruct((rows_here, width), jnp.bfloat16),
            jax.ShapeDtypeStruct((block_rows, 128), jnp.float32),
        ),
        in_specs=[vmem] * 3,
        out_specs=(vmem, vmem),
        scratch_shapes=[
            pltpu.VMEM((chains, n - 1, rows_here // chains, width), jnp.bfloat16),
            pltpu.VMEM((chains, n - 1, rows_here // chains, width), jnp.bfloat16),
            pltpu.VMEM((n, rows_here, width), jnp.bfloat16),
            pltpu.VMEM((n, block_rows, 128), jnp.float32),
            pltpu.VMEM((n, block_rows, 128), jnp.float32),
            pltpu.SemaphoreType.DMA((2, chains, 2, n - 1)),
            pltpu.SemaphoreType.DMA((2, n)),
        ],
        compiler_params=pltpu.CompilerParams(collective_id=0, has_side_effects=True),
    )(parts, residual, vocab_blocks)


def on_device(
    hidden,
    norm_gain,
    qkv_weight,
    out_weight,
    adapter_down,
    adapter_up,
    vocab_rows,
    segments,
    request_adapter,
    adapter_slot,
    page_table,
):
    groups = lax.axis_size("group")
    own_group = lax.axis_index("group")
    shards = lax.axis_size("mp")
    own_shard = lax.axis_index("mp")
    rows_here = segments.shape[0]
    model_width = hidden.shape[1]
    slice_width = model_width // shards
    table = page_table.reshape(groups, -1)
    per_group = table.shape[1]
    per_peer = per_group // groups
    page_len = rows_here // per_group
    holders = table // per_group
    position = jnp.arange(per_group, dtype=jnp.int32)
    sort_keys = jnp.where(holders == own_group, position[None, :], per_group + position[None, :])
    ranked = jnp.argsort(sort_keys, axis=1)[:, :per_peer]
    picked = jnp.take_along_axis(table, ranked, axis=1) - own_group * per_group
    outgoing = hidden.reshape(per_group, page_len, model_width)[picked]
    normed_pages = rms_normed(outgoing, norm_gain)
    projected_pages = jnp.einsum(
        "abrd,dc->abrc", normed_pages, qkv_weight, preferred_element_type=jnp.float32
    ).astype(jnp.bfloat16)
    lowered_pages = jnp.einsum(
        "abrd,dc->abrc", normed_pages, adapter_down, preferred_element_type=jnp.float32
    ).astype(jnp.bfloat16)
    kept_pages = lax.dynamic_slice_in_dim(outgoing, own_shard * slice_width, slice_width, 3)
    widths = (kept_pages.shape[3], projected_pages.shape[3], lowered_pages.shape[3])
    packed = lax.all_to_all(
        jnp.concatenate([kept_pages, projected_pages, lowered_pages], axis=3),
        "group", split_axis=0, concat_axis=0, tiled=True,
    )
    arrived = (
        packed[..., : widths[0]],
        packed[..., widths[0] : widths[0] + widths[1]],
        packed[..., widths[0] + widths[1] :],
    )
    own_holders = lax.dynamic_index_in_dim(holders, own_group, 0, keepdims=False)
    onehot = (own_holders[:, None] == jnp.arange(groups, dtype=jnp.int32)[None, :]).astype(
        jnp.int32
    )
    earlier = jnp.sum((jnp.cumsum(onehot, axis=0) - onehot) * onehot, axis=1)
    source_rows = own_holders * per_peer + earlier

    def placed(received):
        gathered_rows = received.reshape((groups * per_peer,) + received.shape[2:])[source_rows]
        return gathered_rows.reshape((rows_here,) + received.shape[3:])

    residual, projected, lowered = [placed(received) for received in arrived]
    vocab_pieces = jnp.transpose(
        vocab_rows.reshape(vocab_rows.shape[0], shards, slice_width), (1, 0, 2)
    )
    group_vocab = lax.all_gather(vocab_pieces[None], "group", axis=0, tiled=True)
    heads_here = projected.shape[1] // (2 * FEAT + HD)
    split_heads = jnp.transpose(
        projected.reshape(rows_here, heads_here, 2 * FEAT + HD).astype(jnp.float32), (1, 0, 2)
    )
    query_rows = split_heads[..., :FEAT]
    key_rows = split_heads[..., FEAT : 2 * FEAT]
    value_rows = split_heads[..., 2 * FEAT :]
    phi_query = features(query_rows, FEAT)
    phi_key = features(key_rows, FEAT)
    last_seg = segments[-1]
    member = (segments == last_seg).astype(jnp.float32)
    end_state = jnp.einsum(
        "hcp,hce->hpe", phi_key * member[None, :, None], value_rows, precision=PRECISE
    )
    end_totals = jnp.einsum("hcp,c->hp", phi_key, member, precision=PRECISE)
    end_tag = jnp.reshape(last_seg + 1, (1,)).astype(jnp.float32)
    state_size, totals_size = end_state.size, end_totals.size
    handed = from_behind(
        jnp.concatenate(
            [end_state.reshape(-1), end_totals.reshape(-1), end_tag]
        ).astype(jnp.bfloat16),
        "group",
        1,
    ).astype(jnp.float32)
    got_state = handed[:state_size].reshape(end_state.shape)
    got_totals = handed[state_size : state_size + totals_size].reshape(end_totals.shape)
    got_tag = handed[state_size + totals_size :]
    initial = (got_state, got_totals, got_tag[0].astype(jnp.int32) - 1)
    block_len = rows_here
    blocks = rows_here // block_len

    def regroup(values):
        return jnp.transpose(
            values.reshape(values.shape[0], blocks, block_len, values.shape[-1]), (1, 0, 2, 3)
        )

    scan_inputs = (
        regroup(phi_query),
        regroup(phi_key),
        regroup(query_rows),
        regroup(key_rows),
        regroup(value_rows),
        segments.reshape(blocks, block_len),
    )

    def scan_step(state_carry, block_inputs):
        return block_step(state_carry, block_inputs, FEAT)

    _, (mixed_out, state_norm) = lax.scan(scan_step, initial, scan_inputs)
    attended = (
        jnp.transpose(mixed_out, (0, 2, 1, 3))
        .reshape(rows_here, heads_here * HD)
        .astype(jnp.bfloat16)
    )
    group_vocab, attended = lax.optimization_barrier((group_vocab, attended))
    state_norms = jnp.transpose(state_norm, (1, 0, 2)).reshape(heads_here, rows_here)
    request_ids = jnp.arange(request_adapter.shape[0], dtype=jnp.int32)
    adapter_of = jnp.sum(
        jnp.where(segments[:, None] == request_ids[None, :], request_adapter[None, :], 0), axis=1
    )
    adapter_ids = jnp.arange(adapter_slot.shape[0], dtype=jnp.int32)
    slot_ids = jnp.sum(
        jnp.where(adapter_of[:, None] == adapter_ids[None, :], adapter_slot[None, :], 0), axis=1
    )
    column_slot = jnp.arange(lowered.shape[1], dtype=jnp.int32) // RANK
    local_slot = slot_ids - own_shard * (lowered.shape[1] // RANK)
    low_rank = jnp.where(
        local_slot[:, None] == column_slot[None, :], lowered, jnp.zeros_like(lowered)
    )
    partial_value = jnp.dot(attended, out_weight, preferred_element_type=jnp.float32)
    partial_value = partial_value + jnp.dot(
        low_rank, adapter_up, preferred_element_type=jnp.float32
    )
    partial_value = jnp.transpose(
        partial_value.astype(jnp.bfloat16).reshape(rows_here, shards, slice_width), (1, 0, 2)
    )
    summed, best = mp_exchange(partial_value, residual, group_vocab)
    max_logits = best[:, 0]
    return (summed, state_norms, max_logits)


def solution(mesh):
    placed = (
        P("group", None),
        P(),
        P(None, "mp"),
        P("mp", None),
        P(None, "mp"),
        P("mp", None),
        P(("group", "mp"), None),
        P("group"),
        P(),
        P(),
        P(),
    )
    return jax.shard_map(
        on_device,
        mesh=mesh,
        in_specs=placed,
        out_specs=(P("group", "mp"), P("mp", "group"), P(("group", "mp"))),
        check_vma=False,
    )
```

```python
import jax
import jax.numpy as jnp
from jax import lax
from jax.sharding import PartitionSpec as P
from jax.experimental import pallas as pl
from jax.experimental.pallas import tpu as pltpu

FEAT = 16
HD = 112
RANK = 16


EPSILON = 1e-05
PRECISE = lax.Precision.HIGHEST


def from_behind(value, axis, by):
    size = lax.axis_size(axis)
    pairs = [(i, i + by) for i in range(size) if 0 <= i + by < size]
    return lax.ppermute(value, axis, pairs)


def rms_normed(values, norm_gain):
    wide = values.astype(jnp.float32)
    meansq = jnp.mean(wide * wide, axis=-1, keepdims=True)
    return (wide * lax.rsqrt(meansq + EPSILON) * norm_gain).astype(jnp.bfloat16)


def features(vectors, feat_width):
    linear_part = vectors / feat_width**0.25
    outer_part = (vectors[..., :, None] * vectors[..., None, :]).reshape(
        vectors.shape[:-1] + (feat_width * feat_width,)
    )
    outer_part = outer_part / (2.0 * feat_width) ** 0.5
    ones_part = jnp.ones(vectors.shape[:-1] + (1,), jnp.float32)
    return jnp.concatenate([ones_part, linear_part, outer_part], axis=-1)


def block_step(state_carry, block_inputs, feat_width):
    states, totals, owner_seg = state_carry
    phi_query, phi_key, query_rows, key_rows, value_rows, seg_ids = block_inputs
    scaling = feat_width ** (-0.5)
    block_len = seg_ids.shape[0]
    position = jnp.arange(block_len, dtype=jnp.int32)
    allowed = (
        (position[:, None] >= position[None, :]) & (seg_ids[:, None] == seg_ids[None, :])
    ).astype(jnp.float32)
    carried = (seg_ids == owner_seg).astype(jnp.float32)[None, :]
    scores = jnp.einsum("hcf,hdf->hcd", query_rows, key_rows, precision=PRECISE) * scaling
    weights = (1.0 + scores + 0.5 * scores * scores) * allowed[None]
    numerator = jnp.einsum("hcd,hde->hce", weights, value_rows, precision=PRECISE)
    numerator = numerator + carried[..., None] * jnp.einsum(
        "hcp,hpe->hce", phi_query, states, precision=PRECISE
    )
    denominator = jnp.sum(weights, axis=-1) + carried * jnp.einsum(
        "hcp,hp->hc", phi_query, totals, precision=PRECISE
    )
    mixed_out = numerator / denominator[..., None]
    key_scores = jnp.einsum("hcf,hdf->hcd", key_rows, key_rows, precision=PRECISE) * scaling
    value_gram = jnp.einsum("hce,hde->hcd", value_rows, value_rows, precision=PRECISE)
    key_gram = (1.0 + key_scores + 0.5 * key_scores * key_scores) * value_gram
    diagonal = (position[:, None] == position[None, :]).astype(jnp.float32)
    row_terms = jnp.sum(key_gram * (allowed * (2.0 - diagonal))[None], axis=-1)
    local_squares = jnp.einsum("cd,hd->hc", allowed, row_terms, precision=PRECISE)
    along = jnp.sum(
        jnp.einsum("hcp,hpe->hce", phi_key, states, precision=PRECISE) * value_rows, axis=-1
    )
    cross_squares = jnp.einsum("cd,hd->hc", allowed, along, precision=PRECISE)
    state_squares = jnp.sum(states * states, axis=(1, 2))
    squares = carried * (state_squares[:, None] + 2.0 * cross_squares) + local_squares
    counted = carried * totals[:, :1] + jnp.sum(allowed, axis=-1)[None, :]
    state_norm = jnp.sqrt(squares / (counted * (feat_width * value_rows.shape[-1])))
    last_seg = seg_ids[-1]
    member = (seg_ids == last_seg).astype(jnp.float32)
    continues = (owner_seg == last_seg).astype(jnp.float32)
    new_states = continues * states + jnp.einsum(
        "hcp,hce->hpe", phi_key * member[None, :, None], value_rows, precision=PRECISE
    )
    new_totals = continues * totals + jnp.einsum("hcp,c->hp", phi_key, member, precision=PRECISE)
    return ((new_states, new_totals, last_seg), (mixed_out, state_norm))


def best_of(candidates, piece):
    logits = jnp.einsum("rd,vd->rv", candidates, piece, preferred_element_type=jnp.float32)
    return jnp.max(logits, axis=1)


def exchange_kernel(
    att_ref, low_ref, w_ref, u_ref, resid_ref, vocab_ref, upd_ref, best_ref,
    land, acc, rows, tops, got, ring_sems, top_sems,
):
    n = w_ref.shape[0]
    quarter = att_ref.shape[0] // 4
    block_rows = best_ref.shape[0]
    me = lax.axis_index("mp")
    grp = lax.axis_index("group")
    peers = [lax.rem(me + k, n) for k in range(1, n)]
    mesh_id = pl.DeviceIdType.MESH
    towards = (lax.rem(me + 1, n), lax.rem(me + n - 1, n))
    chains = [(0, 0), (1, 2), (0, 1), (1, 3)]
    spans = [pl.ds(quarter * piece, quarter) for _, piece in chains]

    barrier = pltpu.get_barrier_semaphore()
    for p in peers:
        pl.semaphore_signal(barrier, inc=1, device_id=(grp, p), device_id_type=mesh_id)
    pl.semaphore_wait(barrier, n - 1)

    def ring_copy(phase, chain, step, src, dst):
        return pltpu.make_async_remote_copy(
            src_ref=src,
            dst_ref=dst,
            send_sem=ring_sems.at[phase, chain, 0, step],
            recv_sem=ring_sems.at[phase, chain, 1, step],
            device_id=(grp, towards[chains[chain][0]]),
            device_id_type=mesh_id,
        )

    def rs_chunk(chain, step):
        way = chains[chain][0]
        return lax.rem(me + (n - 1 - step if way == 0 else 1 + step) + n, n)

    def part(chunk, span):
        value = jnp.dot(att_ref[span], w_ref[chunk], preferred_element_type=jnp.float32)
        value = value + jnp.dot(low_ref[span], u_ref[chunk], preferred_element_type=jnp.float32)
        return value.astype(jnp.bfloat16).astype(jnp.float32)

    pending = [None] * len(chains)
    for step in range(n - 1):
        for chain in range(len(chains)):
            chunk = rs_chunk(chain, step)
            if step == 0:
                acc[chain, step] = part(chunk, spans[chain]).astype(acc.dtype)
            else:
                pending[chain].wait()
                acc[chain, step] = (
                    land[chain, step - 1].astype(jnp.float32) + part(chunk, spans[chain])
                ).astype(acc.dtype)
            src = acc.at[chain, step]
            pending[chain] = ring_copy(0, chain, step, src, land.at[chain, step])
            pending[chain].start()
    for chain in range(len(chains)):
        pending[chain].wait()
        total = land[chain, n - 2].astype(jnp.float32) + part(me, spans[chain])
        update = total.astype(upd_ref.dtype)
        upd_ref[spans[chain]] = update
        rows[me, spans[chain]] = (
            resid_ref[spans[chain]].astype(jnp.float32) + update.astype(jnp.float32)
        ).astype(rows.dtype)

    for step in range(n - 1):
        for chain in range(len(chains)):
            if step > 0:
                pending[chain].wait()
            way = chains[chain][0]
            chunk = lax.rem(me + (n - step if way == 0 else step), n)
            view = rows.at[chunk, spans[chain]]
            pending[chain] = ring_copy(1, chain, step, view, view)
            pending[chain].start()
    for chain in range(len(chains)):
        pending[chain].wait()

    scores = jnp.zeros((rows.shape[1], vocab_ref.shape[0] * vocab_ref.shape[2]), jnp.float32)
    for j in range(n):
        block = vocab_ref[:, j].reshape(scores.shape[1], rows.shape[2])
        scores = scores + lax.dot_general(
            rows[j], block, (((1,), (1,)), ((), ())),
            preferred_element_type=jnp.float32,
        )
    for p in range(n):
        piece = jnp.max(scores[p * block_rows : (p + 1) * block_rows], axis=1, keepdims=True)
        tops[p] = jnp.broadcast_to(piece, tops.shape[1:])

    sent = []
    for p in peers:
        copy = pltpu.make_async_remote_copy(
            src_ref=tops.at[p],
            dst_ref=got.at[me],
            send_sem=top_sems.at[0, p],
            recv_sem=top_sems.at[1, me],
            device_id=(grp, p),
            device_id_type=mesh_id,
        )
        copy.start()
        sent.append(copy)
    for copy in sent:
        copy.wait_send()
    for q in peers:
        pltpu.make_async_remote_copy(
            src_ref=tops.at[q],
            dst_ref=got.at[q],
            send_sem=top_sems.at[0, q],
            recv_sem=top_sems.at[1, q],
            device_id=(grp, q),
            device_id_type=mesh_id,
        ).wait_recv()
    best = tops[me]
    for q in peers:
        best = jnp.maximum(best, got[q])
    best_ref[...] = best


def mp_exchange(attended, low_rank, out_blocks, up_blocks, residual, vocab_blocks):
    n, _, width = out_blocks.shape
    rows_here = attended.shape[0]
    block_rows = rows_here // n
    chains = 4
    vmem = pl.BlockSpec(memory_space=pltpu.VMEM)
    return pl.pallas_call(
        exchange_kernel,
        out_shape=(
            jax.ShapeDtypeStruct((rows_here, width), jnp.bfloat16),
            jax.ShapeDtypeStruct((block_rows, 128), jnp.float32),
        ),
        in_specs=[vmem] * 6,
        out_specs=(vmem, vmem),
        scratch_shapes=[
            pltpu.VMEM((chains, n - 1, rows_here // chains, width), jnp.bfloat16),
            pltpu.VMEM((chains, n - 1, rows_here // chains, width), jnp.bfloat16),
            pltpu.VMEM((n, rows_here, width), jnp.bfloat16),
            pltpu.VMEM((n, block_rows, 128), jnp.float32),
            pltpu.VMEM((n, block_rows, 128), jnp.float32),
            pltpu.SemaphoreType.DMA((2, chains, 2, n - 1)),
            pltpu.SemaphoreType.DMA((2, n)),
        ],
        compiler_params=pltpu.CompilerParams(collective_id=0, has_side_effects=True),
    )(attended, low_rank, out_blocks, up_blocks, residual, vocab_blocks)


def on_device(
    hidden,
    norm_gain,
    qkv_weight,
    out_weight,
    adapter_down,
    adapter_up,
    vocab_rows,
    segments,
    request_adapter,
    adapter_slot,
    page_table,
):
    groups = lax.axis_size("group")
    own_group = lax.axis_index("group")
    shards = lax.axis_size("mp")
    own_shard = lax.axis_index("mp")
    rows_here = segments.shape[0]
    model_width = hidden.shape[1]
    slice_width = model_width // shards
    table = page_table.reshape(groups, -1)
    per_group = table.shape[1]
    per_peer = per_group // groups
    page_len = rows_here // per_group
    holders = table // per_group
    position = jnp.arange(per_group, dtype=jnp.int32)
    sort_keys = jnp.where(holders == own_group, position[None, :], per_group + position[None, :])
    ranked = jnp.argsort(sort_keys, axis=1)[:, :per_peer]
    picked = jnp.take_along_axis(table, ranked, axis=1) - own_group * per_group
    outgoing = hidden.reshape(per_group, page_len, model_width)[picked]
    normed_pages = rms_normed(outgoing, norm_gain)
    projected_pages = jnp.einsum(
        "abrd,dc->abrc", normed_pages, qkv_weight, preferred_element_type=jnp.float32
    ).astype(jnp.bfloat16)
    lowered_pages = jnp.einsum(
        "abrd,dc->abrc", normed_pages, adapter_down, preferred_element_type=jnp.float32
    ).astype(jnp.bfloat16)
    kept_pages = lax.dynamic_slice_in_dim(outgoing, own_shard * slice_width, slice_width, 3)
    widths = (kept_pages.shape[3], projected_pages.shape[3], lowered_pages.shape[3])
    packed = lax.all_to_all(
        jnp.concatenate([kept_pages, projected_pages, lowered_pages], axis=3),
        "group", split_axis=0, concat_axis=0, tiled=True,
    )
    arrived = (
        packed[..., : widths[0]],
        packed[..., widths[0] : widths[0] + widths[1]],
        packed[..., widths[0] + widths[1] :],
    )
    own_holders = lax.dynamic_index_in_dim(holders, own_group, 0, keepdims=False)
    onehot = (own_holders[:, None] == jnp.arange(groups, dtype=jnp.int32)[None, :]).astype(
        jnp.int32
    )
    earlier = jnp.sum((jnp.cumsum(onehot, axis=0) - onehot) * onehot, axis=1)
    source_rows = own_holders * per_peer + earlier

    def placed(received):
        gathered_rows = received.reshape((groups * per_peer,) + received.shape[2:])[source_rows]
        return gathered_rows.reshape((rows_here,) + received.shape[3:])

    residual, projected, lowered = [placed(received) for received in arrived]
    vocab_pieces = jnp.transpose(
        vocab_rows.reshape(vocab_rows.shape[0], shards, slice_width), (1, 0, 2)
    )
    group_vocab = lax.all_gather(vocab_pieces[None], "group", axis=0, tiled=True)
    heads_here = projected.shape[1] // (2 * FEAT + HD)
    split_heads = jnp.transpose(
        projected.reshape(rows_here, heads_here, 2 * FEAT + HD).astype(jnp.float32), (1, 0, 2)
    )
    query_rows = split_heads[..., :FEAT]
    key_rows = split_heads[..., FEAT : 2 * FEAT]
    value_rows = split_heads[..., 2 * FEAT :]
    phi_query = features(query_rows, FEAT)
    phi_key = features(key_rows, FEAT)
    last_seg = segments[-1]
    member = (segments == last_seg).astype(jnp.float32)
    end_state = jnp.einsum(
        "hcp,hce->hpe", phi_key * member[None, :, None], value_rows, precision=PRECISE
    )
    end_totals = jnp.einsum("hcp,c->hp", phi_key, member, precision=PRECISE)
    end_tag = jnp.reshape(last_seg + 1, (1,)).astype(jnp.float32)
    state_size, totals_size = end_state.size, end_totals.size
    handed = from_behind(
        jnp.concatenate(
            [end_state.reshape(-1), end_totals.reshape(-1), end_tag]
        ).astype(jnp.bfloat16),
        "group",
        1,
    ).astype(jnp.float32)
    got_state = handed[:state_size].reshape(end_state.shape)
    got_totals = handed[state_size : state_size + totals_size].reshape(end_totals.shape)
    got_tag = handed[state_size + totals_size :]
    initial = (got_state, got_totals, got_tag[0].astype(jnp.int32) - 1)
    block_len = rows_here
    blocks = rows_here // block_len

    def regroup(values):
        return jnp.transpose(
            values.reshape(values.shape[0], blocks, block_len, values.shape[-1]), (1, 0, 2, 3)
        )

    scan_inputs = (
        regroup(phi_query),
        regroup(phi_key),
        regroup(query_rows),
        regroup(key_rows),
        regroup(value_rows),
        segments.reshape(blocks, block_len),
    )

    def scan_step(state_carry, block_inputs):
        return block_step(state_carry, block_inputs, FEAT)

    _, (mixed_out, state_norm) = lax.scan(scan_step, initial, scan_inputs)
    attended = (
        jnp.transpose(mixed_out, (0, 2, 1, 3))
        .reshape(rows_here, heads_here * HD)
        .astype(jnp.bfloat16)
    )
    group_vocab, attended = lax.optimization_barrier((group_vocab, attended))
    state_norms = jnp.transpose(state_norm, (1, 0, 2)).reshape(heads_here, rows_here)
    request_ids = jnp.arange(request_adapter.shape[0], dtype=jnp.int32)
    adapter_of = jnp.sum(
        jnp.where(segments[:, None] == request_ids[None, :], request_adapter[None, :], 0), axis=1
    )
    adapter_ids = jnp.arange(adapter_slot.shape[0], dtype=jnp.int32)
    slot_ids = jnp.sum(
        jnp.where(adapter_of[:, None] == adapter_ids[None, :], adapter_slot[None, :], 0), axis=1
    )
    column_slot = jnp.arange(lowered.shape[1], dtype=jnp.int32) // RANK
    local_slot = slot_ids - own_shard * (lowered.shape[1] // RANK)
    low_rank = jnp.where(
        local_slot[:, None] == column_slot[None, :], lowered, jnp.zeros_like(lowered)
    )
    out_blocks = jnp.transpose(
        out_weight.reshape(out_weight.shape[0], shards, slice_width), (1, 0, 2)
    )
    up_blocks = jnp.transpose(
        adapter_up.reshape(adapter_up.shape[0], shards, slice_width), (1, 0, 2)
    )
    summed, best = mp_exchange(attended, low_rank, out_blocks, up_blocks, residual, group_vocab)
    max_logits = best[:, 0]
    return (summed, state_norms, max_logits)


def solution(mesh):
    placed = (
        P("group", None),
        P(),
        P(None, "mp"),
        P("mp", None),
        P(None, "mp"),
        P("mp", None),
        P(("group", "mp"), None),
        P("group"),
        P(),
        P(),
        P(),
    )
    return jax.shard_map(
        on_device,
        mesh=mesh,
        in_specs=placed,
        out_specs=(P("group", "mp"), P("mp", "group"), P(("group", "mp"))),
        check_vma=False,
    )
```

```python
import jax
import jax.numpy as jnp
from jax import lax
from jax.sharding import PartitionSpec as P
from jax.experimental import pallas as pl
from jax.experimental.pallas import tpu as pltpu

FEAT = 16
HD = 112
RANK = 16


EPSILON = 1e-05
PRECISE = lax.Precision.HIGHEST


def from_behind(value, axis, by):
    size = lax.axis_size(axis)
    pairs = [(i, i + by) for i in range(size) if 0 <= i + by < size]
    return lax.ppermute(value, axis, pairs)


def rms_normed(values, norm_gain):
    wide = values.astype(jnp.float32)
    meansq = jnp.mean(wide * wide, axis=-1, keepdims=True)
    return (wide * lax.rsqrt(meansq + EPSILON) * norm_gain).astype(jnp.bfloat16)


def features(vectors, feat_width):
    linear_part = vectors / feat_width**0.25
    outer_part = (vectors[..., :, None] * vectors[..., None, :]).reshape(
        vectors.shape[:-1] + (feat_width * feat_width,)
    )
    outer_part = outer_part / (2.0 * feat_width) ** 0.5
    ones_part = jnp.ones(vectors.shape[:-1] + (1,), jnp.float32)
    return jnp.concatenate([ones_part, linear_part, outer_part], axis=-1)


def block_step(state_carry, block_inputs, feat_width):
    states, totals, owner_seg = state_carry
    phi_query, phi_key, query_rows, key_rows, value_rows, seg_ids = block_inputs
    scaling = feat_width ** (-0.5)
    block_len = seg_ids.shape[0]
    position = jnp.arange(block_len, dtype=jnp.int32)
    allowed = (
        (position[:, None] >= position[None, :]) & (seg_ids[:, None] == seg_ids[None, :])
    ).astype(jnp.float32)
    carried = (seg_ids == owner_seg).astype(jnp.float32)[None, :]
    scores = jnp.einsum("hcf,hdf->hcd", query_rows, key_rows, precision=PRECISE) * scaling
    weights = (1.0 + scores + 0.5 * scores * scores) * allowed[None]
    numerator = jnp.einsum("hcd,hde->hce", weights, value_rows, precision=PRECISE)
    numerator = numerator + carried[..., None] * jnp.einsum(
        "hcp,hpe->hce", phi_query, states, precision=PRECISE
    )
    denominator = jnp.sum(weights, axis=-1) + carried * jnp.einsum(
        "hcp,hp->hc", phi_query, totals, precision=PRECISE
    )
    mixed_out = numerator / denominator[..., None]
    key_scores = jnp.einsum("hcf,hdf->hcd", key_rows, key_rows, precision=PRECISE) * scaling
    value_gram = jnp.einsum("hce,hde->hcd", value_rows, value_rows, precision=PRECISE)
    key_gram = (1.0 + key_scores + 0.5 * key_scores * key_scores) * value_gram
    diagonal = (position[:, None] == position[None, :]).astype(jnp.float32)
    row_terms = jnp.sum(key_gram * (allowed * (2.0 - diagonal))[None], axis=-1)
    local_squares = jnp.einsum("cd,hd->hc", allowed, row_terms, precision=PRECISE)
    along = jnp.sum(
        jnp.einsum("hcp,hpe->hce", phi_key, states, precision=PRECISE) * value_rows, axis=-1
    )
    cross_squares = jnp.einsum("cd,hd->hc", allowed, along, precision=PRECISE)
    state_squares = jnp.sum(states * states, axis=(1, 2))
    squares = carried * (state_squares[:, None] + 2.0 * cross_squares) + local_squares
    counted = carried * totals[:, :1] + jnp.sum(allowed, axis=-1)[None, :]
    state_norm = jnp.sqrt(squares / (counted * (feat_width * value_rows.shape[-1])))
    last_seg = seg_ids[-1]
    member = (seg_ids == last_seg).astype(jnp.float32)
    continues = (owner_seg == last_seg).astype(jnp.float32)
    new_states = continues * states + jnp.einsum(
        "hcp,hce->hpe", phi_key * member[None, :, None], value_rows, precision=PRECISE
    )
    new_totals = continues * totals + jnp.einsum("hcp,c->hp", phi_key, member, precision=PRECISE)
    return ((new_states, new_totals, last_seg), (mixed_out, state_norm))


def best_of(candidates, piece):
    logits = jnp.einsum("rd,vd->rv", candidates, piece, preferred_element_type=jnp.float32)
    return jnp.max(logits, axis=1)


def exchange_kernel(
    att_ref, low_ref, w_ref, u_ref, resid_ref, vocab_ref, upd_ref, best_ref,
    land, acc, rows, tops, got, ring_sems, top_sems,
):
    n = w_ref.shape[0]
    quarter = att_ref.shape[0] // 8
    block_rows = best_ref.shape[0]
    me = lax.axis_index("mp")
    grp = lax.axis_index("group")
    peers = [lax.rem(me + k, n) for k in range(1, n)]
    mesh_id = pl.DeviceIdType.MESH
    towards = (lax.rem(me + 1, n), lax.rem(me + n - 1, n))
    chains = [(0, 0), (1, 4), (0, 1), (1, 5), (0, 2), (1, 6), (0, 3), (1, 7)]
    spans = [pl.ds(quarter * piece, quarter) for _, piece in chains]

    barrier = pltpu.get_barrier_semaphore()
    for p in peers:
        pl.semaphore_signal(barrier, inc=1, device_id=(grp, p), device_id_type=mesh_id)
    pl.semaphore_wait(barrier, n - 1)

    def ring_copy(phase, chain, step, src, dst):
        return pltpu.make_async_remote_copy(
            src_ref=src,
            dst_ref=dst,
            send_sem=ring_sems.at[phase, chain, 0, step],
            recv_sem=ring_sems.at[phase, chain, 1, step],
            device_id=(grp, towards[chains[chain][0]]),
            device_id_type=mesh_id,
        )

    def rs_chunk(chain, step):
        way = chains[chain][0]
        return lax.rem(me + (n - 1 - step if way == 0 else 1 + step) + n, n)

    def part(chunk, span):
        value = jnp.dot(att_ref[span], w_ref[chunk], preferred_element_type=jnp.float32)
        value = value + jnp.dot(low_ref[span], u_ref[chunk], preferred_element_type=jnp.float32)
        return value.astype(jnp.bfloat16).astype(jnp.float32)

    pending = [None] * len(chains)
    for step in range(n - 1):
        for chain in range(len(chains)):
            chunk = rs_chunk(chain, step)
            if step == 0:
                acc[chain, step] = part(chunk, spans[chain]).astype(acc.dtype)
            else:
                pending[chain].wait()
                acc[chain, step] = (
                    land[chain, step - 1].astype(jnp.float32) + part(chunk, spans[chain])
                ).astype(acc.dtype)
            src = acc.at[chain, step]
            pending[chain] = ring_copy(0, chain, step, src, land.at[chain, step])
            pending[chain].start()
    for chain in range(len(chains)):
        pending[chain].wait()
        total = land[chain, n - 2].astype(jnp.float32) + part(me, spans[chain])
        update = total.astype(upd_ref.dtype)
        upd_ref[spans[chain]] = update
        rows[me, spans[chain]] = (
            resid_ref[spans[chain]].astype(jnp.float32) + update.astype(jnp.float32)
        ).astype(rows.dtype)

    for step in range(n - 1):
        for chain in range(len(chains)):
            if step > 0:
                pending[chain].wait()
            way = chains[chain][0]
            chunk = lax.rem(me + (n - step if way == 0 else step), n)
            view = rows.at[chunk, spans[chain]]
            pending[chain] = ring_copy(1, chain, step, view, view)
            pending[chain].start()
    for chain in range(len(chains)):
        pending[chain].wait()

    scores = jnp.zeros((rows.shape[1], vocab_ref.shape[0] * vocab_ref.shape[2]), jnp.float32)
    for j in range(n):
        block = vocab_ref[:, j].reshape(scores.shape[1], rows.shape[2])
        scores = scores + lax.dot_general(
            rows[j], block, (((1,), (1,)), ((), ())),
            preferred_element_type=jnp.float32,
        )
    for p in range(n):
        piece = jnp.max(scores[p * block_rows : (p + 1) * block_rows], axis=1, keepdims=True)
        tops[p] = jnp.broadcast_to(piece, tops.shape[1:])

    sent = []
    for p in peers:
        copy = pltpu.make_async_remote_copy(
            src_ref=tops.at[p],
            dst_ref=got.at[me],
            send_sem=top_sems.at[0, p],
            recv_sem=top_sems.at[1, me],
            device_id=(grp, p),
            device_id_type=mesh_id,
        )
        copy.start()
        sent.append(copy)
    for copy in sent:
        copy.wait_send()
    for q in peers:
        pltpu.make_async_remote_copy(
            src_ref=tops.at[q],
            dst_ref=got.at[q],
            send_sem=top_sems.at[0, q],
            recv_sem=top_sems.at[1, q],
            device_id=(grp, q),
            device_id_type=mesh_id,
        ).wait_recv()
    best = tops[me]
    for q in peers:
        best = jnp.maximum(best, got[q])
    best_ref[...] = best


def mp_exchange(attended, low_rank, out_blocks, up_blocks, residual, vocab_blocks):
    n, _, width = out_blocks.shape
    rows_here = attended.shape[0]
    block_rows = rows_here // n
    chains = 8
    vmem = pl.BlockSpec(memory_space=pltpu.VMEM)
    return pl.pallas_call(
        exchange_kernel,
        out_shape=(
            jax.ShapeDtypeStruct((rows_here, width), jnp.bfloat16),
            jax.ShapeDtypeStruct((block_rows, 128), jnp.float32),
        ),
        in_specs=[vmem] * 6,
        out_specs=(vmem, vmem),
        scratch_shapes=[
            pltpu.VMEM((chains, n - 1, rows_here // chains, width), jnp.bfloat16),
            pltpu.VMEM((chains, n - 1, rows_here // chains, width), jnp.bfloat16),
            pltpu.VMEM((n, rows_here, width), jnp.bfloat16),
            pltpu.VMEM((n, block_rows, 128), jnp.float32),
            pltpu.VMEM((n, block_rows, 128), jnp.float32),
            pltpu.SemaphoreType.DMA((2, chains, 2, n - 1)),
            pltpu.SemaphoreType.DMA((2, n)),
        ],
        compiler_params=pltpu.CompilerParams(collective_id=0, has_side_effects=True),
    )(attended, low_rank, out_blocks, up_blocks, residual, vocab_blocks)


def on_device(
    hidden,
    norm_gain,
    qkv_weight,
    out_weight,
    adapter_down,
    adapter_up,
    vocab_rows,
    segments,
    request_adapter,
    adapter_slot,
    page_table,
):
    groups = lax.axis_size("group")
    own_group = lax.axis_index("group")
    shards = lax.axis_size("mp")
    own_shard = lax.axis_index("mp")
    rows_here = segments.shape[0]
    model_width = hidden.shape[1]
    slice_width = model_width // shards
    table = page_table.reshape(groups, -1)
    per_group = table.shape[1]
    per_peer = per_group // groups
    page_len = rows_here // per_group
    holders = table // per_group
    position = jnp.arange(per_group, dtype=jnp.int32)
    sort_keys = jnp.where(holders == own_group, position[None, :], per_group + position[None, :])
    ranked = jnp.argsort(sort_keys, axis=1)[:, :per_peer]
    picked = jnp.take_along_axis(table, ranked, axis=1) - own_group * per_group
    outgoing = hidden.reshape(per_group, page_len, model_width)[picked]
    normed_pages = rms_normed(outgoing, norm_gain)
    projected_pages = jnp.einsum(
        "abrd,dc->abrc", normed_pages, qkv_weight, preferred_element_type=jnp.float32
    ).astype(jnp.bfloat16)
    lowered_pages = jnp.einsum(
        "abrd,dc->abrc", normed_pages, adapter_down, preferred_element_type=jnp.float32
    ).astype(jnp.bfloat16)
    kept_pages = lax.dynamic_slice_in_dim(outgoing, own_shard * slice_width, slice_width, 3)
    widths = (kept_pages.shape[3], projected_pages.shape[3], lowered_pages.shape[3])
    packed = lax.all_to_all(
        jnp.concatenate([kept_pages, projected_pages, lowered_pages], axis=3),
        "group", split_axis=0, concat_axis=0, tiled=True,
    )
    arrived = (
        packed[..., : widths[0]],
        packed[..., widths[0] : widths[0] + widths[1]],
        packed[..., widths[0] + widths[1] :],
    )
    own_holders = lax.dynamic_index_in_dim(holders, own_group, 0, keepdims=False)
    onehot = (own_holders[:, None] == jnp.arange(groups, dtype=jnp.int32)[None, :]).astype(
        jnp.int32
    )
    earlier = jnp.sum((jnp.cumsum(onehot, axis=0) - onehot) * onehot, axis=1)
    source_rows = own_holders * per_peer + earlier

    def placed(received):
        gathered_rows = received.reshape((groups * per_peer,) + received.shape[2:])[source_rows]
        return gathered_rows.reshape((rows_here,) + received.shape[3:])

    residual, projected, lowered = [placed(received) for received in arrived]
    vocab_pieces = jnp.transpose(
        vocab_rows.reshape(vocab_rows.shape[0], shards, slice_width), (1, 0, 2)
    )
    group_vocab = lax.all_gather(vocab_pieces[None], "group", axis=0, tiled=True)
    heads_here = projected.shape[1] // (2 * FEAT + HD)
    split_heads = jnp.transpose(
        projected.reshape(rows_here, heads_here, 2 * FEAT + HD).astype(jnp.float32), (1, 0, 2)
    )
    query_rows = split_heads[..., :FEAT]
    key_rows = split_heads[..., FEAT : 2 * FEAT]
    value_rows = split_heads[..., 2 * FEAT :]
    phi_query = features(query_rows, FEAT)
    phi_key = features(key_rows, FEAT)
    last_seg = segments[-1]
    member = (segments == last_seg).astype(jnp.float32)
    end_state = jnp.einsum(
        "hcp,hce->hpe", phi_key * member[None, :, None], value_rows, precision=PRECISE
    )
    end_totals = jnp.einsum("hcp,c->hp", phi_key, member, precision=PRECISE)
    end_tag = jnp.reshape(last_seg + 1, (1,)).astype(jnp.float32)
    state_size, totals_size = end_state.size, end_totals.size
    handed = from_behind(
        jnp.concatenate(
            [end_state.reshape(-1), end_totals.reshape(-1), end_tag]
        ).astype(jnp.bfloat16),
        "group",
        1,
    ).astype(jnp.float32)
    got_state = handed[:state_size].reshape(end_state.shape)
    got_totals = handed[state_size : state_size + totals_size].reshape(end_totals.shape)
    got_tag = handed[state_size + totals_size :]
    initial = (got_state, got_totals, got_tag[0].astype(jnp.int32) - 1)
    block_len = rows_here
    blocks = rows_here // block_len

    def regroup(values):
        return jnp.transpose(
            values.reshape(values.shape[0], blocks, block_len, values.shape[-1]), (1, 0, 2, 3)
        )

    scan_inputs = (
        regroup(phi_query),
        regroup(phi_key),
        regroup(query_rows),
        regroup(key_rows),
        regroup(value_rows),
        segments.reshape(blocks, block_len),
    )

    def scan_step(state_carry, block_inputs):
        return block_step(state_carry, block_inputs, FEAT)

    _, (mixed_out, state_norm) = lax.scan(scan_step, initial, scan_inputs)
    attended = (
        jnp.transpose(mixed_out, (0, 2, 1, 3))
        .reshape(rows_here, heads_here * HD)
        .astype(jnp.bfloat16)
    )
    group_vocab, attended = lax.optimization_barrier((group_vocab, attended))
    state_norms = jnp.transpose(state_norm, (1, 0, 2)).reshape(heads_here, rows_here)
    request_ids = jnp.arange(request_adapter.shape[0], dtype=jnp.int32)
    adapter_of = jnp.sum(
        jnp.where(segments[:, None] == request_ids[None, :], request_adapter[None, :], 0), axis=1
    )
    adapter_ids = jnp.arange(adapter_slot.shape[0], dtype=jnp.int32)
    slot_ids = jnp.sum(
        jnp.where(adapter_of[:, None] == adapter_ids[None, :], adapter_slot[None, :], 0), axis=1
    )
    column_slot = jnp.arange(lowered.shape[1], dtype=jnp.int32) // RANK
    local_slot = slot_ids - own_shard * (lowered.shape[1] // RANK)
    low_rank = jnp.where(
        local_slot[:, None] == column_slot[None, :], lowered, jnp.zeros_like(lowered)
    )
    out_blocks = jnp.transpose(
        out_weight.reshape(out_weight.shape[0], shards, slice_width), (1, 0, 2)
    )
    up_blocks = jnp.transpose(
        adapter_up.reshape(adapter_up.shape[0], shards, slice_width), (1, 0, 2)
    )
    summed, best = mp_exchange(attended, low_rank, out_blocks, up_blocks, residual, group_vocab)
    max_logits = best[:, 0]
    return (summed, state_norms, max_logits)


def solution(mesh):
    placed = (
        P("group", None),
        P(),
        P(None, "mp"),
        P("mp", None),
        P(None, "mp"),
        P("mp", None),
        P(("group", "mp"), None),
        P("group"),
        P(),
        P(),
        P(),
    )
    return jax.shard_map(
        on_device,
        mesh=mesh,
        in_specs=placed,
        out_specs=(P("group", "mp"), P("mp", "group"), P(("group", "mp"))),
        check_vma=False,
    )
```

```python
import jax
import jax.numpy as jnp
from jax import lax
from jax.sharding import PartitionSpec as P
from jax.experimental import pallas as pl
from jax.experimental.pallas import tpu as pltpu

FEAT = 16
HD = 112
RANK = 16


EPSILON = 1e-05
PRECISE = lax.Precision.HIGHEST


def from_behind(value, axis, by):
    size = lax.axis_size(axis)
    pairs = [(i, i + by) for i in range(size) if 0 <= i + by < size]
    return lax.ppermute(value, axis, pairs)


def rms_normed(values, norm_gain):
    wide = values.astype(jnp.float32)
    meansq = jnp.mean(wide * wide, axis=-1, keepdims=True)
    return (wide * lax.rsqrt(meansq + EPSILON) * norm_gain).astype(jnp.bfloat16)


def features(vectors, feat_width):
    linear_part = vectors / feat_width**0.25
    outer_part = (vectors[..., :, None] * vectors[..., None, :]).reshape(
        vectors.shape[:-1] + (feat_width * feat_width,)
    )
    outer_part = outer_part / (2.0 * feat_width) ** 0.5
    ones_part = jnp.ones(vectors.shape[:-1] + (1,), jnp.float32)
    return jnp.concatenate([ones_part, linear_part, outer_part], axis=-1)


def block_step(state_carry, block_inputs, feat_width):
    states, totals, owner_seg = state_carry
    phi_query, phi_key, query_rows, key_rows, value_rows, seg_ids = block_inputs
    scaling = feat_width ** (-0.5)
    block_len = seg_ids.shape[0]
    position = jnp.arange(block_len, dtype=jnp.int32)
    allowed = (
        (position[:, None] >= position[None, :]) & (seg_ids[:, None] == seg_ids[None, :])
    ).astype(jnp.float32)
    carried = (seg_ids == owner_seg).astype(jnp.float32)[None, :]
    scores = jnp.einsum("hcf,hdf->hcd", query_rows, key_rows, precision=PRECISE) * scaling
    weights = (1.0 + scores + 0.5 * scores * scores) * allowed[None]
    numerator = jnp.einsum("hcd,hde->hce", weights, value_rows, precision=PRECISE)
    numerator = numerator + carried[..., None] * jnp.einsum(
        "hcp,hpe->hce", phi_query, states, precision=PRECISE
    )
    denominator = jnp.sum(weights, axis=-1) + carried * jnp.einsum(
        "hcp,hp->hc", phi_query, totals, precision=PRECISE
    )
    mixed_out = numerator / denominator[..., None]
    key_scores = jnp.einsum("hcf,hdf->hcd", key_rows, key_rows, precision=PRECISE) * scaling
    value_gram = jnp.einsum("hce,hde->hcd", value_rows, value_rows, precision=PRECISE)
    key_gram = (1.0 + key_scores + 0.5 * key_scores * key_scores) * value_gram
    diagonal = (position[:, None] == position[None, :]).astype(jnp.float32)
    row_terms = jnp.sum(key_gram * (allowed * (2.0 - diagonal))[None], axis=-1)
    local_squares = jnp.einsum("cd,hd->hc", allowed, row_terms, precision=PRECISE)
    along = jnp.sum(
        jnp.einsum("hcp,hpe->hce", phi_key, states, precision=PRECISE) * value_rows, axis=-1
    )
    cross_squares = jnp.einsum("cd,hd->hc", allowed, along, precision=PRECISE)
    state_squares = jnp.sum(states * states, axis=(1, 2))
    squares = carried * (state_squares[:, None] + 2.0 * cross_squares) + local_squares
    counted = carried * totals[:, :1] + jnp.sum(allowed, axis=-1)[None, :]
    state_norm = jnp.sqrt(squares / (counted * (feat_width * value_rows.shape[-1])))
    last_seg = seg_ids[-1]
    member = (seg_ids == last_seg).astype(jnp.float32)
    continues = (owner_seg == last_seg).astype(jnp.float32)
    new_states = continues * states + jnp.einsum(
        "hcp,hce->hpe", phi_key * member[None, :, None], value_rows, precision=PRECISE
    )
    new_totals = continues * totals + jnp.einsum("hcp,c->hp", phi_key, member, precision=PRECISE)
    return ((new_states, new_totals, last_seg), (mixed_out, state_norm))


def best_of(candidates, piece):
    logits = jnp.einsum("rd,vd->rv", candidates, piece, preferred_element_type=jnp.float32)
    return jnp.max(logits, axis=1)


def exchange_kernel(
    att_ref, low_ref, w_ref, u_ref, resid_ref, vocab_ref, upd_ref, best_ref,
    land, acc, rows, tops, got, parts, ring_sems, top_sems,
):
    n = w_ref.shape[0]
    quarter = att_ref.shape[0] // 8
    block_rows = best_ref.shape[0]
    me = lax.axis_index("mp")
    grp = lax.axis_index("group")
    peers = [lax.rem(me + k, n) for k in range(1, n)]
    mesh_id = pl.DeviceIdType.MESH
    towards = (lax.rem(me + 1, n), lax.rem(me + n - 1, n))
    chains = [(0, 0), (1, 4), (0, 1), (1, 5), (0, 2), (1, 6), (0, 3), (1, 7)]
    spans = [pl.ds(quarter * piece, quarter) for _, piece in chains]

    for c in range(n):
        value = jnp.dot(att_ref[...], w_ref[c], preferred_element_type=jnp.float32)
        value = value + jnp.dot(low_ref[...], u_ref[c], preferred_element_type=jnp.float32)
        parts[c] = value.astype(parts.dtype)

    barrier = pltpu.get_barrier_semaphore()
    for p in peers:
        pl.semaphore_signal(barrier, inc=1, device_id=(grp, p), device_id_type=mesh_id)
    pl.semaphore_wait(barrier, n - 1)

    def ring_copy(phase, chain, step, src, dst):
        return pltpu.make_async_remote_copy(
            src_ref=src,
            dst_ref=dst,
            send_sem=ring_sems.at[phase, chain, 0, step],
            recv_sem=ring_sems.at[phase, chain, 1, step],
            device_id=(grp, towards[chains[chain][0]]),
            device_id_type=mesh_id,
        )

    def rs_chunk(chain, step):
        way = chains[chain][0]
        return lax.rem(me + (n - 1 - step if way == 0 else 1 + step) + n, n)

    def part(chunk, span):
        return parts[chunk, span].astype(jnp.float32)

    pending = [None] * len(chains)
    for step in range(n - 1):
        for chain in range(len(chains)):
            chunk = rs_chunk(chain, step)
            if step == 0:
                acc[chain, step] = part(chunk, spans[chain]).astype(acc.dtype)
            else:
                pending[chain].wait()
                acc[chain, step] = (
                    land[chain, step - 1].astype(jnp.float32) + part(chunk, spans[chain])
                ).astype(acc.dtype)
            src = acc.at[chain, step]
            pending[chain] = ring_copy(0, chain, step, src, land.at[chain, step])
            pending[chain].start()
    for chain in range(len(chains)):
        pending[chain].wait()
        total = land[chain, n - 2].astype(jnp.float32) + part(me, spans[chain])
        update = total.astype(upd_ref.dtype)
        upd_ref[spans[chain]] = update
        rows[me, spans[chain]] = (
            resid_ref[spans[chain]].astype(jnp.float32) + update.astype(jnp.float32)
        ).astype(rows.dtype)
        view = rows.at[me, spans[chain]]
        pending[chain] = ring_copy(1, chain, 0, view, view)
        pending[chain].start()

    for step in range(1, n - 1):
        for chain in range(len(chains)):
            pending[chain].wait()
            way = chains[chain][0]
            chunk = lax.rem(me + (n - step if way == 0 else step), n)
            view = rows.at[chunk, spans[chain]]
            pending[chain] = ring_copy(1, chain, step, view, view)
            pending[chain].start()
    for chain in range(len(chains)):
        pending[chain].wait()

    scores = jnp.zeros((rows.shape[1], vocab_ref.shape[0] * vocab_ref.shape[2]), jnp.float32)
    for j in range(n):
        block = vocab_ref[:, j].reshape(scores.shape[1], rows.shape[2])
        scores = scores + lax.dot_general(
            rows[j], block, (((1,), (1,)), ((), ())),
            preferred_element_type=jnp.float32,
        )
    for p in range(n):
        piece = jnp.max(scores[p * block_rows : (p + 1) * block_rows], axis=1, keepdims=True)
        tops[p] = jnp.broadcast_to(piece, tops.shape[1:])

    sent = []
    for p in peers:
        copy = pltpu.make_async_remote_copy(
            src_ref=tops.at[p],
            dst_ref=got.at[me],
            send_sem=top_sems.at[0, p],
            recv_sem=top_sems.at[1, me],
            device_id=(grp, p),
            device_id_type=mesh_id,
        )
        copy.start()
        sent.append(copy)
    for copy in sent:
        copy.wait_send()
    for q in peers:
        pltpu.make_async_remote_copy(
            src_ref=tops.at[q],
            dst_ref=got.at[q],
            send_sem=top_sems.at[0, q],
            recv_sem=top_sems.at[1, q],
            device_id=(grp, q),
            device_id_type=mesh_id,
        ).wait_recv()
    best = tops[me]
    for q in peers:
        best = jnp.maximum(best, got[q])
    best_ref[...] = best


def mp_exchange(attended, low_rank, out_blocks, up_blocks, residual, vocab_blocks):
    n, _, width = out_blocks.shape
    rows_here = attended.shape[0]
    block_rows = rows_here // n
    chains = 8
    vmem = pl.BlockSpec(memory_space=pltpu.VMEM)
    return pl.pallas_call(
        exchange_kernel,
        out_shape=(
            jax.ShapeDtypeStruct((rows_here, width), jnp.bfloat16),
            jax.ShapeDtypeStruct((block_rows, 128), jnp.float32),
        ),
        in_specs=[vmem] * 6,
        out_specs=(vmem, vmem),
        scratch_shapes=[
            pltpu.VMEM((chains, n - 1, rows_here // chains, width), jnp.bfloat16),
            pltpu.VMEM((chains, n - 1, rows_here // chains, width), jnp.bfloat16),
            pltpu.VMEM((n, rows_here, width), jnp.bfloat16),
            pltpu.VMEM((n, block_rows, 128), jnp.float32),
            pltpu.VMEM((n, block_rows, 128), jnp.float32),
            pltpu.VMEM((n, rows_here, width), jnp.bfloat16),
            pltpu.SemaphoreType.DMA((2, chains, 2, n - 1)),
            pltpu.SemaphoreType.DMA((2, n)),
        ],
        compiler_params=pltpu.CompilerParams(collective_id=0, has_side_effects=True),
    )(attended, low_rank, out_blocks, up_blocks, residual, vocab_blocks)


def on_device(
    hidden,
    norm_gain,
    qkv_weight,
    out_weight,
    adapter_down,
    adapter_up,
    vocab_rows,
    segments,
    request_adapter,
    adapter_slot,
    page_table,
):
    groups = lax.axis_size("group")
    own_group = lax.axis_index("group")
    shards = lax.axis_size("mp")
    own_shard = lax.axis_index("mp")
    rows_here = segments.shape[0]
    model_width = hidden.shape[1]
    slice_width = model_width // shards
    table = page_table.reshape(groups, -1)
    per_group = table.shape[1]
    per_peer = per_group // groups
    page_len = rows_here // per_group
    holders = table // per_group
    position = jnp.arange(per_group, dtype=jnp.int32)
    sort_keys = jnp.where(holders == own_group, position[None, :], per_group + position[None, :])
    ranked = jnp.argsort(sort_keys, axis=1)[:, :per_peer]
    picked = jnp.take_along_axis(table, ranked, axis=1) - own_group * per_group
    outgoing = hidden.reshape(per_group, page_len, model_width)[picked]
    normed_pages = rms_normed(outgoing, norm_gain)
    projected_pages = jnp.einsum(
        "abrd,dc->abrc", normed_pages, qkv_weight, preferred_element_type=jnp.float32
    ).astype(jnp.bfloat16)
    lowered_pages = jnp.einsum(
        "abrd,dc->abrc", normed_pages, adapter_down, preferred_element_type=jnp.float32
    ).astype(jnp.bfloat16)
    kept_pages = lax.dynamic_slice_in_dim(outgoing, own_shard * slice_width, slice_width, 3)
    widths = (kept_pages.shape[3], projected_pages.shape[3], lowered_pages.shape[3])
    packed = lax.all_to_all(
        jnp.concatenate([kept_pages, projected_pages, lowered_pages], axis=3),
        "group", split_axis=0, concat_axis=0, tiled=True,
    )
    arrived = (
        packed[..., : widths[0]],
        packed[..., widths[0] : widths[0] + widths[1]],
        packed[..., widths[0] + widths[1] :],
    )
    own_holders = lax.dynamic_index_in_dim(holders, own_group, 0, keepdims=False)
    onehot = (own_holders[:, None] == jnp.arange(groups, dtype=jnp.int32)[None, :]).astype(
        jnp.int32
    )
    earlier = jnp.sum((jnp.cumsum(onehot, axis=0) - onehot) * onehot, axis=1)
    source_rows = own_holders * per_peer + earlier

    def placed(received):
        gathered_rows = received.reshape((groups * per_peer,) + received.shape[2:])[source_rows]
        return gathered_rows.reshape((rows_here,) + received.shape[3:])

    residual, projected, lowered = [placed(received) for received in arrived]
    vocab_pieces = jnp.transpose(
        vocab_rows.reshape(vocab_rows.shape[0], shards, slice_width), (1, 0, 2)
    )
    group_vocab = lax.all_gather(vocab_pieces[None], "group", axis=0, tiled=True)
    heads_here = projected.shape[1] // (2 * FEAT + HD)
    split_heads = jnp.transpose(
        projected.reshape(rows_here, heads_here, 2 * FEAT + HD).astype(jnp.float32), (1, 0, 2)
    )
    query_rows = split_heads[..., :FEAT]
    key_rows = split_heads[..., FEAT : 2 * FEAT]
    value_rows = split_heads[..., 2 * FEAT :]
    phi_query = features(query_rows, FEAT)
    phi_key = features(key_rows, FEAT)
    last_seg = segments[-1]
    member = (segments == last_seg).astype(jnp.float32)
    end_state = jnp.einsum(
        "hcp,hce->hpe", phi_key * member[None, :, None], value_rows, precision=PRECISE
    )
    end_totals = jnp.einsum("hcp,c->hp", phi_key, member, precision=PRECISE)
    end_tag = jnp.reshape(last_seg + 1, (1,)).astype(jnp.float32)
    state_size, totals_size = end_state.size, end_totals.size
    handed = from_behind(
        jnp.concatenate(
            [end_state.reshape(-1), end_totals.reshape(-1), end_tag]
        ).astype(jnp.bfloat16),
        "group",
        1,
    ).astype(jnp.float32)
    got_state = handed[:state_size].reshape(end_state.shape)
    got_totals = handed[state_size : state_size + totals_size].reshape(end_totals.shape)
    got_tag = handed[state_size + totals_size :]
    initial = (got_state, got_totals, got_tag[0].astype(jnp.int32) - 1)
    block_len = rows_here
    blocks = rows_here // block_len

    def regroup(values):
        return jnp.transpose(
            values.reshape(values.shape[0], blocks, block_len, values.shape[-1]), (1, 0, 2, 3)
        )

    scan_inputs = (
        regroup(phi_query),
        regroup(phi_key),
        regroup(query_rows),
        regroup(key_rows),
        regroup(value_rows),
        segments.reshape(blocks, block_len),
    )

    def scan_step(state_carry, block_inputs):
        return block_step(state_carry, block_inputs, FEAT)

    _, (mixed_out, state_norm) = lax.scan(scan_step, initial, scan_inputs)
    attended = (
        jnp.transpose(mixed_out, (0, 2, 1, 3))
        .reshape(rows_here, heads_here * HD)
        .astype(jnp.bfloat16)
    )
    group_vocab, attended = lax.optimization_barrier((group_vocab, attended))
    state_norms = jnp.transpose(state_norm, (1, 0, 2)).reshape(heads_here, rows_here)
    request_ids = jnp.arange(request_adapter.shape[0], dtype=jnp.int32)
    adapter_of = jnp.sum(
        jnp.where(segments[:, None] == request_ids[None, :], request_adapter[None, :], 0), axis=1
    )
    adapter_ids = jnp.arange(adapter_slot.shape[0], dtype=jnp.int32)
    slot_ids = jnp.sum(
        jnp.where(adapter_of[:, None] == adapter_ids[None, :], adapter_slot[None, :], 0), axis=1
    )
    column_slot = jnp.arange(lowered.shape[1], dtype=jnp.int32) // RANK
    local_slot = slot_ids - own_shard * (lowered.shape[1] // RANK)
    low_rank = jnp.where(
        local_slot[:, None] == column_slot[None, :], lowered, jnp.zeros_like(lowered)
    )
    out_blocks = jnp.transpose(
        out_weight.reshape(out_weight.shape[0], shards, slice_width), (1, 0, 2)
    )
    up_blocks = jnp.transpose(
        adapter_up.reshape(adapter_up.shape[0], shards, slice_width), (1, 0, 2)
    )
    summed, best = mp_exchange(attended, low_rank, out_blocks, up_blocks, residual, group_vocab)
    max_logits = best[:, 0]
    return (summed, state_norms, max_logits)


def solution(mesh):
    placed = (
        P("group", None),
        P(),
        P(None, "mp"),
        P("mp", None),
        P(None, "mp"),
        P("mp", None),
        P(("group", "mp"), None),
        P("group"),
        P(),
        P(),
        P(),
    )
    return jax.shard_map(
        on_device,
        mesh=mesh,
        in_specs=placed,
        out_specs=(P("group", "mp"), P("mp", "group"), P(("group", "mp"))),
        check_vma=False,
    )
```

```python
import jax
import jax.numpy as jnp
from jax import lax
from jax.sharding import PartitionSpec as P
from jax.experimental import pallas as pl
from jax.experimental.pallas import tpu as pltpu

FEAT = 16
HD = 112
RANK = 16


EPSILON = 1e-05
PRECISE = lax.Precision.HIGHEST


def from_behind(value, axis, by):
    size = lax.axis_size(axis)
    pairs = [(i, i + by) for i in range(size) if 0 <= i + by < size]
    return lax.ppermute(value, axis, pairs)


def rms_normed(values, norm_gain):
    wide = values.astype(jnp.float32)
    meansq = jnp.mean(wide * wide, axis=-1, keepdims=True)
    return (wide * lax.rsqrt(meansq + EPSILON) * norm_gain).astype(jnp.bfloat16)


def features(vectors, feat_width):
    linear_part = vectors / feat_width**0.25
    outer_part = (vectors[..., :, None] * vectors[..., None, :]).reshape(
        vectors.shape[:-1] + (feat_width * feat_width,)
    )
    outer_part = outer_part / (2.0 * feat_width) ** 0.5
    ones_part = jnp.ones(vectors.shape[:-1] + (1,), jnp.float32)
    return jnp.concatenate([ones_part, linear_part, outer_part], axis=-1)


def block_step(state_carry, block_inputs, feat_width):
    states, totals, owner_seg = state_carry
    phi_query, phi_key, query_rows, key_rows, value_rows, seg_ids = block_inputs
    scaling = feat_width ** (-0.5)
    block_len = seg_ids.shape[0]
    position = jnp.arange(block_len, dtype=jnp.int32)
    allowed = (
        (position[:, None] >= position[None, :]) & (seg_ids[:, None] == seg_ids[None, :])
    ).astype(jnp.float32)
    carried = (seg_ids == owner_seg).astype(jnp.float32)[None, :]
    scores = jnp.einsum("hcf,hdf->hcd", query_rows, key_rows, precision=PRECISE) * scaling
    weights = (1.0 + scores + 0.5 * scores * scores) * allowed[None]
    numerator = jnp.einsum("hcd,hde->hce", weights, value_rows, precision=PRECISE)
    numerator = numerator + carried[..., None] * jnp.einsum(
        "hcp,hpe->hce", phi_query, states, precision=PRECISE
    )
    denominator = jnp.sum(weights, axis=-1) + carried * jnp.einsum(
        "hcp,hp->hc", phi_query, totals, precision=PRECISE
    )
    mixed_out = numerator / denominator[..., None]
    key_scores = jnp.einsum("hcf,hdf->hcd", key_rows, key_rows, precision=PRECISE) * scaling
    value_gram = jnp.einsum("hce,hde->hcd", value_rows, value_rows, precision=PRECISE)
    key_gram = (1.0 + key_scores + 0.5 * key_scores * key_scores) * value_gram
    diagonal = (position[:, None] == position[None, :]).astype(jnp.float32)
    row_terms = jnp.sum(key_gram * (allowed * (2.0 - diagonal))[None], axis=-1)
    local_squares = jnp.einsum("cd,hd->hc", allowed, row_terms, precision=PRECISE)
    along = jnp.sum(
        jnp.einsum("hcp,hpe->hce", phi_key, states, precision=PRECISE) * value_rows, axis=-1
    )
    cross_squares = jnp.einsum("cd,hd->hc", allowed, along, precision=PRECISE)
    state_squares = jnp.sum(states * states, axis=(1, 2))
    squares = carried * (state_squares[:, None] + 2.0 * cross_squares) + local_squares
    counted = carried * totals[:, :1] + jnp.sum(allowed, axis=-1)[None, :]
    state_norm = jnp.sqrt(squares / (counted * (feat_width * value_rows.shape[-1])))
    last_seg = seg_ids[-1]
    member = (seg_ids == last_seg).astype(jnp.float32)
    continues = (owner_seg == last_seg).astype(jnp.float32)
    new_states = continues * states + jnp.einsum(
        "hcp,hce->hpe", phi_key * member[None, :, None], value_rows, precision=PRECISE
    )
    new_totals = continues * totals + jnp.einsum("hcp,c->hp", phi_key, member, precision=PRECISE)
    return ((new_states, new_totals, last_seg), (mixed_out, state_norm))


def best_of(candidates, piece):
    logits = jnp.einsum("rd,vd->rv", candidates, piece, preferred_element_type=jnp.float32)
    return jnp.max(logits, axis=1)


def exchange_kernel(
    att_ref, low_ref, w_ref, u_ref, resid_ref, vocab_ref, upd_ref, best_ref,
    land, acc, rows, tops, got, parts, ring_sems, top_sems,
):
    n = w_ref.shape[0]
    quarter = att_ref.shape[0] // 8
    block_rows = best_ref.shape[0]
    me = lax.axis_index("mp")
    grp = lax.axis_index("group")
    peers = [lax.rem(me + k, n) for k in range(1, n)]
    mesh_id = pl.DeviceIdType.MESH
    towards = (lax.rem(me + 1, n), lax.rem(me + n - 1, n))
    chains = [(0, 0), (1, 4), (0, 1), (1, 5), (0, 2), (1, 6), (0, 3), (1, 7)]
    spans = [pl.ds(quarter * piece, quarter) for _, piece in chains]

    for c in range(n):
        value = jnp.dot(att_ref[...], w_ref[c], preferred_element_type=jnp.float32)
        value = value + jnp.dot(low_ref[...], u_ref[c], preferred_element_type=jnp.float32)
        parts[c] = value.astype(parts.dtype)

    barrier = pltpu.get_barrier_semaphore()
    for p in peers:
        pl.semaphore_signal(barrier, inc=1, device_id=(grp, p), device_id_type=mesh_id)
    pl.semaphore_wait(barrier, n - 1)

    def ring_copy(phase, chain, step, src, dst):
        return pltpu.make_async_remote_copy(
            src_ref=src,
            dst_ref=dst,
            send_sem=ring_sems.at[phase, chain, 0, step],
            recv_sem=ring_sems.at[phase, chain, 1, step],
            device_id=(grp, towards[chains[chain][0]]),
            device_id_type=mesh_id,
        )

    def rs_chunk(chain, step):
        way = chains[chain][0]
        return lax.rem(me + (n - 1 - step if way == 0 else 1 + step) + n, n)

    def part(chunk, span):
        return parts[chunk, span].astype(jnp.float32)

    pending = [None] * len(chains)
    for step in range(n - 1):
        for chain in range(len(chains)):
            chunk = rs_chunk(chain, step)
            if step == 0:
                acc[chain, step] = part(chunk, spans[chain]).astype(acc.dtype)
            else:
                pending[chain].wait()
                acc[chain, step] = (
                    land[chain, step - 1].astype(jnp.float32) + part(chunk, spans[chain])
                ).astype(acc.dtype)
            src = acc.at[chain, step]
            pending[chain] = ring_copy(0, chain, step, src, land.at[chain, step])
            pending[chain].start()
    for chain in range(len(chains)):
        pending[chain].wait()
        total = land[chain, n - 2].astype(jnp.float32) + part(me, spans[chain])
        update = total.astype(upd_ref.dtype)
        upd_ref[spans[chain]] = update
        rows[me, spans[chain]] = (
            resid_ref[spans[chain]].astype(jnp.float32) + update.astype(jnp.float32)
        ).astype(rows.dtype)
        view = rows.at[me, spans[chain]]
        pending[chain] = ring_copy(1, chain, 0, view, view)
        pending[chain].start()

    for step in range(1, n - 1):
        for chain in range(len(chains)):
            pending[chain].wait()
            way = chains[chain][0]
            chunk = lax.rem(me + (n - step if way == 0 else step), n)
            view = rows.at[chunk, spans[chain]]
            pending[chain] = ring_copy(1, chain, step, view, view)
            pending[chain].start()
    for chain in range(len(chains)):
        pending[chain].wait()

    scores = jnp.zeros((rows.shape[1], vocab_ref.shape[0] * vocab_ref.shape[2]), jnp.float32)
    for j in range(n):
        block = vocab_ref[:, j].reshape(scores.shape[1], rows.shape[2])
        scores = scores + lax.dot_general(
            rows[j], block, (((1,), (1,)), ((), ())),
            preferred_element_type=jnp.float32,
        )
    for p in range(n):
        piece = jnp.max(scores[p * block_rows : (p + 1) * block_rows], axis=1, keepdims=True)
        tops[p] = jnp.broadcast_to(piece, tops.shape[1:])

    sent = []
    for p in peers:
        copy = pltpu.make_async_remote_copy(
            src_ref=tops.at[p],
            dst_ref=got.at[me],
            send_sem=top_sems.at[0, p],
            recv_sem=top_sems.at[1, me],
            device_id=(grp, p),
            device_id_type=mesh_id,
        )
        copy.start()
        sent.append(copy)
    for copy in sent:
        copy.wait_send()
    for q in peers:
        pltpu.make_async_remote_copy(
            src_ref=tops.at[q],
            dst_ref=got.at[q],
            send_sem=top_sems.at[0, q],
            recv_sem=top_sems.at[1, q],
            device_id=(grp, q),
            device_id_type=mesh_id,
        ).wait_recv()
    best = tops[me]
    for q in peers:
        best = jnp.maximum(best, got[q])
    best_ref[...] = best


def mp_exchange(attended, low_rank, out_blocks, up_blocks, residual, vocab_blocks):
    n, _, width = out_blocks.shape
    rows_here = attended.shape[0]
    block_rows = rows_here // n
    chains = 8
    vmem = pl.BlockSpec(memory_space=pltpu.VMEM)
    return pl.pallas_call(
        exchange_kernel,
        out_shape=(
            jax.ShapeDtypeStruct((rows_here, width), jnp.bfloat16),
            jax.ShapeDtypeStruct((block_rows, 128), jnp.float32),
        ),
        in_specs=[vmem] * 6,
        out_specs=(vmem, vmem),
        scratch_shapes=[
            pltpu.VMEM((chains, n - 1, rows_here // chains, width), jnp.bfloat16),
            pltpu.VMEM((chains, n - 1, rows_here // chains, width), jnp.bfloat16),
            pltpu.VMEM((n, rows_here, width), jnp.bfloat16),
            pltpu.VMEM((n, block_rows, 128), jnp.float32),
            pltpu.VMEM((n, block_rows, 128), jnp.float32),
            pltpu.VMEM((n, rows_here, width), jnp.bfloat16),
            pltpu.SemaphoreType.DMA((2, chains, 2, n - 1)),
            pltpu.SemaphoreType.DMA((2, n)),
        ],
        compiler_params=pltpu.CompilerParams(collective_id=0, has_side_effects=True),
    )(attended, low_rank, out_blocks, up_blocks, residual, vocab_blocks)


def on_device(
    hidden,
    norm_gain,
    qkv_weight,
    out_weight,
    adapter_down,
    adapter_up,
    vocab_rows,
    segments,
    request_adapter,
    adapter_slot,
    page_table,
):
    groups = lax.axis_size("group")
    own_group = lax.axis_index("group")
    shards = lax.axis_size("mp")
    own_shard = lax.axis_index("mp")
    rows_here = segments.shape[0]
    model_width = hidden.shape[1]
    slice_width = model_width // shards
    table = page_table.reshape(groups, -1)
    per_group = table.shape[1]
    per_peer = per_group // groups
    page_len = rows_here // per_group
    holders = table // per_group
    position = jnp.arange(per_group, dtype=jnp.int32)
    sort_keys = jnp.where(holders == own_group, position[None, :], per_group + position[None, :])
    ranked = jnp.argsort(sort_keys, axis=1)[:, :per_peer]
    picked = jnp.take_along_axis(table, ranked, axis=1) - own_group * per_group
    outgoing = hidden.reshape(per_group, page_len, model_width)[picked]
    normed_pages = rms_normed(outgoing, norm_gain)
    projected_pages = jnp.einsum(
        "abrd,dc->abrc", normed_pages, qkv_weight, preferred_element_type=jnp.float32
    ).astype(jnp.bfloat16)
    lowered_pages = jnp.einsum(
        "abrd,dc->abrc", normed_pages, adapter_down, preferred_element_type=jnp.float32
    ).astype(jnp.bfloat16)
    kept_pages = lax.dynamic_slice_in_dim(outgoing, own_shard * slice_width, slice_width, 3)
    widths = (kept_pages.shape[3], projected_pages.shape[3], lowered_pages.shape[3])
    packed = lax.all_to_all(
        jnp.concatenate([kept_pages, projected_pages, lowered_pages], axis=3),
        "group", split_axis=0, concat_axis=0, tiled=True,
    )
    own_holders = lax.dynamic_index_in_dim(holders, own_group, 0, keepdims=False)
    onehot = (own_holders[:, None] == jnp.arange(groups, dtype=jnp.int32)[None, :]).astype(
        jnp.int32
    )
    earlier = jnp.sum((jnp.cumsum(onehot, axis=0) - onehot) * onehot, axis=1)
    source_rows = own_holders * per_peer + earlier

    def placed(received):
        gathered_rows = received.reshape((groups * per_peer,) + received.shape[2:])[source_rows]
        return gathered_rows.reshape((rows_here,) + received.shape[3:])

    all_rows = placed(packed)
    residual = all_rows[:, : widths[0]]
    projected = all_rows[:, widths[0] : widths[0] + widths[1]]
    lowered = all_rows[:, widths[0] + widths[1] :]
    vocab_pieces = jnp.transpose(
        vocab_rows.reshape(vocab_rows.shape[0], shards, slice_width), (1, 0, 2)
    )
    group_vocab = lax.all_gather(vocab_pieces[None], "group", axis=0, tiled=True)
    heads_here = projected.shape[1] // (2 * FEAT + HD)
    split_heads = jnp.transpose(
        projected.reshape(rows_here, heads_here, 2 * FEAT + HD).astype(jnp.float32), (1, 0, 2)
    )
    query_rows = split_heads[..., :FEAT]
    key_rows = split_heads[..., FEAT : 2 * FEAT]
    value_rows = split_heads[..., 2 * FEAT :]
    phi_query = features(query_rows, FEAT)
    phi_key = features(key_rows, FEAT)
    last_seg = segments[-1]
    member = (segments == last_seg).astype(jnp.float32)
    value_ones = jnp.concatenate(
        [value_rows, jnp.ones(value_rows.shape[:-1] + (1,), value_rows.dtype)], axis=-1
    )
    end_both = jnp.einsum(
        "hcp,hce->hpe", phi_key * member[None, :, None], value_ones, precision=PRECISE
    )
    end_both = jnp.pad(end_both, ((0, 0), (0, 1), (0, 0)))
    end_both = end_both.at[0, -1, 0].set((last_seg + 1).astype(jnp.float32))
    handed = from_behind(end_both.astype(jnp.bfloat16), "group", 1).astype(jnp.float32)
    got_state = handed[:, :-1, :-1]
    got_totals = handed[:, :-1, -1]
    got_tag = handed[0, -1, :1]
    initial = (got_state, got_totals, got_tag[0].astype(jnp.int32) - 1)
    block_len = rows_here
    blocks = rows_here // block_len

    def regroup(values):
        return jnp.transpose(
            values.reshape(values.shape[0], blocks, block_len, values.shape[-1]), (1, 0, 2, 3)
        )

    scan_inputs = (
        regroup(phi_query),
        regroup(phi_key),
        regroup(query_rows),
        regroup(key_rows),
        regroup(value_rows),
        segments.reshape(blocks, block_len),
    )

    def scan_step(state_carry, block_inputs):
        return block_step(state_carry, block_inputs, FEAT)

    _, (mixed_out, state_norm) = lax.scan(scan_step, initial, scan_inputs)
    attended = (
        jnp.transpose(mixed_out, (0, 2, 1, 3))
        .reshape(rows_here, heads_here * HD)
        .astype(jnp.bfloat16)
    )
    group_vocab, attended = lax.optimization_barrier((group_vocab, attended))
    state_norms = jnp.transpose(state_norm, (1, 0, 2)).reshape(heads_here, rows_here)
    request_ids = jnp.arange(request_adapter.shape[0], dtype=jnp.int32)
    adapter_of = jnp.sum(
        jnp.where(segments[:, None] == request_ids[None, :], request_adapter[None, :], 0), axis=1
    )
    adapter_ids = jnp.arange(adapter_slot.shape[0], dtype=jnp.int32)
    slot_ids = jnp.sum(
        jnp.where(adapter_of[:, None] == adapter_ids[None, :], adapter_slot[None, :], 0), axis=1
    )
    column_slot = jnp.arange(lowered.shape[1], dtype=jnp.int32) // RANK
    local_slot = slot_ids - own_shard * (lowered.shape[1] // RANK)
    low_rank = jnp.where(
        local_slot[:, None] == column_slot[None, :], lowered, jnp.zeros_like(lowered)
    )
    out_blocks = jnp.transpose(
        out_weight.reshape(out_weight.shape[0], shards, slice_width), (1, 0, 2)
    )
    up_blocks = jnp.transpose(
        adapter_up.reshape(adapter_up.shape[0], shards, slice_width), (1, 0, 2)
    )
    summed, best = mp_exchange(attended, low_rank, out_blocks, up_blocks, residual, group_vocab)
    max_logits = best[:, 0]
    return (summed, state_norms, max_logits)


def solution(mesh):
    placed = (
        P("group", None),
        P(),
        P(None, "mp"),
        P("mp", None),
        P(None, "mp"),
        P("mp", None),
        P(("group", "mp"), None),
        P("group"),
        P(),
        P(),
        P(),
    )
    return jax.shard_map(
        on_device,
        mesh=mesh,
        in_specs=placed,
        out_specs=(P("group", "mp"), P("mp", "group"), P(("group", "mp"))),
        check_vma=False,
    )
```

```python
import jax
import jax.numpy as jnp
from jax import lax
from jax.sharding import PartitionSpec as P
from jax.experimental import pallas as pl
from jax.experimental.pallas import tpu as pltpu

FEAT = 16
HD = 112
RANK = 16


EPSILON = 1e-05
PRECISE = lax.Precision.HIGHEST


def from_behind(value, axis, by):
    size = lax.axis_size(axis)
    pairs = [(i, i + by) for i in range(size) if 0 <= i + by < size]
    return lax.ppermute(value, axis, pairs)


def rms_normed(values, norm_gain):
    wide = values.astype(jnp.float32)
    meansq = jnp.mean(wide * wide, axis=-1, keepdims=True)
    return (wide * lax.rsqrt(meansq + EPSILON) * norm_gain).astype(jnp.bfloat16)


def features(vectors, feat_width):
    linear_part = vectors / feat_width**0.25
    outer_part = (vectors[..., :, None] * vectors[..., None, :]).reshape(
        vectors.shape[:-1] + (feat_width * feat_width,)
    )
    outer_part = outer_part / (2.0 * feat_width) ** 0.5
    ones_part = jnp.ones(vectors.shape[:-1] + (1,), jnp.float32)
    return jnp.concatenate([ones_part, linear_part, outer_part], axis=-1)


def block_step(state_carry, block_inputs, feat_width):
    states, totals, owner_seg = state_carry
    phi_query, phi_key, query_rows, key_rows, value_rows, seg_ids = block_inputs
    scaling = feat_width ** (-0.5)
    block_len = seg_ids.shape[0]
    position = jnp.arange(block_len, dtype=jnp.int32)
    allowed = (
        (position[:, None] >= position[None, :]) & (seg_ids[:, None] == seg_ids[None, :])
    ).astype(jnp.float32)
    carried = (seg_ids == owner_seg).astype(jnp.float32)[None, :]
    scores = jnp.einsum("hcf,hdf->hcd", query_rows, key_rows, precision=PRECISE) * scaling
    weights = (1.0 + scores + 0.5 * scores * scores) * allowed[None]
    numerator = jnp.einsum("hcd,hde->hce", weights, value_rows, precision=PRECISE)
    numerator = numerator + carried[..., None] * jnp.einsum(
        "hcp,hpe->hce", phi_query, states, precision=PRECISE
    )
    denominator = jnp.sum(weights, axis=-1) + carried * jnp.einsum(
        "hcp,hp->hc", phi_query, totals, precision=PRECISE
    )
    mixed_out = numerator / denominator[..., None]
    key_scores = jnp.einsum("hcf,hdf->hcd", key_rows, key_rows, precision=PRECISE) * scaling
    value_gram = jnp.einsum("hce,hde->hcd", value_rows, value_rows, precision=PRECISE)
    key_gram = (1.0 + key_scores + 0.5 * key_scores * key_scores) * value_gram
    diagonal = (position[:, None] == position[None, :]).astype(jnp.float32)
    row_terms = jnp.sum(key_gram * (allowed * (2.0 - diagonal))[None], axis=-1)
    local_squares = jnp.einsum("cd,hd->hc", allowed, row_terms, precision=PRECISE)
    along = jnp.sum(
        jnp.einsum("hcp,hpe->hce", phi_key, states, precision=PRECISE) * value_rows, axis=-1
    )
    cross_squares = jnp.einsum("cd,hd->hc", allowed, along, precision=PRECISE)
    state_squares = jnp.sum(states * states, axis=(1, 2))
    squares = carried * (state_squares[:, None] + 2.0 * cross_squares) + local_squares
    counted = carried * totals[:, :1] + jnp.sum(allowed, axis=-1)[None, :]
    state_norm = jnp.sqrt(squares / (counted * (feat_width * value_rows.shape[-1])))
    last_seg = seg_ids[-1]
    member = (seg_ids == last_seg).astype(jnp.float32)
    continues = (owner_seg == last_seg).astype(jnp.float32)
    new_states = continues * states + jnp.einsum(
        "hcp,hce->hpe", phi_key * member[None, :, None], value_rows, precision=PRECISE
    )
    new_totals = continues * totals + jnp.einsum("hcp,c->hp", phi_key, member, precision=PRECISE)
    return ((new_states, new_totals, last_seg), (mixed_out, state_norm))


def best_of(candidates, piece):
    logits = jnp.einsum("rd,vd->rv", candidates, piece, preferred_element_type=jnp.float32)
    return jnp.max(logits, axis=1)


def exchange_kernel(
    att_ref, low_ref, w_ref, u_ref, resid_ref, vocab_in, upd_ref, best_ref,
    land, acc, rows, tops, got, parts, vocab_ref, ring_sems, top_sems, vocab_sems,
):
    n = w_ref.shape[0]
    quarter = att_ref.shape[0] // 8
    block_rows = best_ref.shape[0]
    me = lax.axis_index("mp")
    grp = lax.axis_index("group")
    peers = [lax.rem(me + k, n) for k in range(1, n)]
    mesh_id = pl.DeviceIdType.MESH
    towards = (lax.rem(me + 1, n), lax.rem(me + n - 1, n))
    chains = [(0, 0), (1, 4), (0, 1), (1, 5), (0, 2), (1, 6), (0, 3), (1, 7)]
    spans = [pl.ds(quarter * piece, quarter) for _, piece in chains]

    for c in range(n):
        value = jnp.dot(att_ref[...], w_ref[c], preferred_element_type=jnp.float32)
        value = value + jnp.dot(low_ref[...], u_ref[c], preferred_element_type=jnp.float32)
        parts[c] = value.astype(parts.dtype)

    groups = vocab_ref.shape[0]
    holders = [lax.rem(grp + k, groups) for k in range(1, groups)]
    barrier = pltpu.get_barrier_semaphore()
    for p in peers:
        pl.semaphore_signal(barrier, inc=1, device_id=(grp, p), device_id_type=mesh_id)
    for h in holders:
        pl.semaphore_signal(barrier, inc=1, device_id=(h, me), device_id_type=mesh_id)
    pl.semaphore_wait(barrier, n - 1 + groups - 1)

    own_vocab = pltpu.make_async_copy(vocab_in, vocab_ref.at[grp], vocab_sems.at[2, 0])
    own_vocab.start()
    vocab_sent = []
    for h in holders:
        copy = pltpu.make_async_remote_copy(
            src_ref=vocab_in,
            dst_ref=vocab_ref.at[grp],
            send_sem=vocab_sems.at[0, h],
            recv_sem=vocab_sems.at[1, grp],
            device_id=(h, me),
            device_id_type=mesh_id,
        )
        copy.start()
        vocab_sent.append(copy)

    def ring_copy(phase, chain, step, src, dst):
        return pltpu.make_async_remote_copy(
            src_ref=src,
            dst_ref=dst,
            send_sem=ring_sems.at[phase, chain, 0, step],
            recv_sem=ring_sems.at[phase, chain, 1, step],
            device_id=(grp, towards[chains[chain][0]]),
            device_id_type=mesh_id,
        )

    def rs_chunk(chain, step):
        way = chains[chain][0]
        return lax.rem(me + (n - 1 - step if way == 0 else 1 + step) + n, n)

    def part(chunk, span):
        return parts[chunk, span].astype(jnp.float32)

    pending = [None] * len(chains)
    for step in range(n - 1):
        for chain in range(len(chains)):
            chunk = rs_chunk(chain, step)
            if step == 0:
                acc[chain, step] = part(chunk, spans[chain]).astype(acc.dtype)
            else:
                pending[chain].wait()
                acc[chain, step] = (
                    land[chain, step - 1].astype(jnp.float32) + part(chunk, spans[chain])
                ).astype(acc.dtype)
            src = acc.at[chain, step]
            pending[chain] = ring_copy(0, chain, step, src, land.at[chain, step])
            pending[chain].start()
    for chain in range(len(chains)):
        pending[chain].wait()
        total = land[chain, n - 2].astype(jnp.float32) + part(me, spans[chain])
        update = total.astype(upd_ref.dtype)
        upd_ref[spans[chain]] = update
        rows[me, spans[chain]] = (
            resid_ref[spans[chain]].astype(jnp.float32) + update.astype(jnp.float32)
        ).astype(rows.dtype)
        view = rows.at[me, spans[chain]]
        pending[chain] = ring_copy(1, chain, 0, view, view)
        pending[chain].start()

    for step in range(1, n - 1):
        for chain in range(len(chains)):
            pending[chain].wait()
            way = chains[chain][0]
            chunk = lax.rem(me + (n - step if way == 0 else step), n)
            view = rows.at[chunk, spans[chain]]
            pending[chain] = ring_copy(1, chain, step, view, view)
            pending[chain].start()
    for chain in range(len(chains)):
        pending[chain].wait()

    own_vocab.wait()
    for copy in vocab_sent:
        copy.wait_send()
    for h in holders:
        pltpu.make_async_remote_copy(
            src_ref=vocab_in,
            dst_ref=vocab_ref.at[h],
            send_sem=vocab_sems.at[0, h],
            recv_sem=vocab_sems.at[1, h],
            device_id=(h, me),
            device_id_type=mesh_id,
        ).wait_recv()

    scores = jnp.zeros((rows.shape[1], vocab_ref.shape[0] * vocab_ref.shape[2]), jnp.float32)
    for j in range(n):
        block = vocab_ref[:, j].reshape(scores.shape[1], rows.shape[2])
        scores = scores + lax.dot_general(
            rows[j], block, (((1,), (1,)), ((), ())),
            preferred_element_type=jnp.float32,
        )
    for p in range(n):
        piece = jnp.max(scores[p * block_rows : (p + 1) * block_rows], axis=1, keepdims=True)
        tops[p] = jnp.broadcast_to(piece, tops.shape[1:])

    sent = []
    for p in peers:
        copy = pltpu.make_async_remote_copy(
            src_ref=tops.at[p],
            dst_ref=got.at[me],
            send_sem=top_sems.at[0, p],
            recv_sem=top_sems.at[1, me],
            device_id=(grp, p),
            device_id_type=mesh_id,
        )
        copy.start()
        sent.append(copy)
    for copy in sent:
        copy.wait_send()
    for q in peers:
        pltpu.make_async_remote_copy(
            src_ref=tops.at[q],
            dst_ref=got.at[q],
            send_sem=top_sems.at[0, q],
            recv_sem=top_sems.at[1, q],
            device_id=(grp, q),
            device_id_type=mesh_id,
        ).wait_recv()
    best = tops[me]
    for q in peers:
        best = jnp.maximum(best, got[q])
    best_ref[...] = best


def mp_exchange(attended, low_rank, out_blocks, up_blocks, residual, vocab_blocks, groups):
    n, _, width = out_blocks.shape
    rows_here = attended.shape[0]
    block_rows = rows_here // n
    chains = 8
    vmem = pl.BlockSpec(memory_space=pltpu.VMEM)
    return pl.pallas_call(
        exchange_kernel,
        out_shape=(
            jax.ShapeDtypeStruct((rows_here, width), jnp.bfloat16),
            jax.ShapeDtypeStruct((block_rows, 128), jnp.float32),
        ),
        in_specs=[vmem] * 6,
        out_specs=(vmem, vmem),
        scratch_shapes=[
            pltpu.VMEM((chains, n - 1, rows_here // chains, width), jnp.bfloat16),
            pltpu.VMEM((chains, n - 1, rows_here // chains, width), jnp.bfloat16),
            pltpu.VMEM((n, rows_here, width), jnp.bfloat16),
            pltpu.VMEM((n, block_rows, 128), jnp.float32),
            pltpu.VMEM((n, block_rows, 128), jnp.float32),
            pltpu.VMEM((n, rows_here, width), jnp.bfloat16),
            pltpu.VMEM((groups,) + vocab_blocks.shape, jnp.bfloat16),
            pltpu.SemaphoreType.DMA((2, chains, 2, n - 1)),
            pltpu.SemaphoreType.DMA((2, n)),
            pltpu.SemaphoreType.DMA((3, groups)),
        ],
        compiler_params=pltpu.CompilerParams(collective_id=0, has_side_effects=True),
    )(attended, low_rank, out_blocks, up_blocks, residual, vocab_blocks)


def on_device(
    hidden,
    norm_gain,
    qkv_weight,
    out_weight,
    adapter_down,
    adapter_up,
    vocab_rows,
    segments,
    request_adapter,
    adapter_slot,
    page_table,
):
    groups = lax.axis_size("group")
    own_group = lax.axis_index("group")
    shards = lax.axis_size("mp")
    own_shard = lax.axis_index("mp")
    rows_here = segments.shape[0]
    model_width = hidden.shape[1]
    slice_width = model_width // shards
    table = page_table.reshape(groups, -1)
    per_group = table.shape[1]
    per_peer = per_group // groups
    page_len = rows_here // per_group
    holders = table // per_group
    position = jnp.arange(per_group, dtype=jnp.int32)
    sort_keys = jnp.where(holders == own_group, position[None, :], per_group + position[None, :])
    ranked = jnp.argsort(sort_keys, axis=1)[:, :per_peer]
    picked = jnp.take_along_axis(table, ranked, axis=1) - own_group * per_group
    outgoing = hidden.reshape(per_group, page_len, model_width)[picked]
    normed_pages = rms_normed(outgoing, norm_gain)
    projected_pages = jnp.einsum(
        "abrd,dc->abrc", normed_pages, qkv_weight, preferred_element_type=jnp.float32
    ).astype(jnp.bfloat16)
    lowered_pages = jnp.einsum(
        "abrd,dc->abrc", normed_pages, adapter_down, preferred_element_type=jnp.float32
    ).astype(jnp.bfloat16)
    kept_pages = lax.dynamic_slice_in_dim(outgoing, own_shard * slice_width, slice_width, 3)
    widths = (kept_pages.shape[3], projected_pages.shape[3], lowered_pages.shape[3])
    packed = lax.all_to_all(
        jnp.concatenate([kept_pages, projected_pages, lowered_pages], axis=3),
        "group", split_axis=0, concat_axis=0, tiled=True,
    )
    own_holders = lax.dynamic_index_in_dim(holders, own_group, 0, keepdims=False)
    onehot = (own_holders[:, None] == jnp.arange(groups, dtype=jnp.int32)[None, :]).astype(
        jnp.int32
    )
    earlier = jnp.sum((jnp.cumsum(onehot, axis=0) - onehot) * onehot, axis=1)
    source_rows = own_holders * per_peer + earlier

    def placed(received):
        gathered_rows = received.reshape((groups * per_peer,) + received.shape[2:])[source_rows]
        return gathered_rows.reshape((rows_here,) + received.shape[3:])

    all_rows = placed(packed)
    residual = all_rows[:, : widths[0]]
    projected = all_rows[:, widths[0] : widths[0] + widths[1]]
    lowered = all_rows[:, widths[0] + widths[1] :]
    vocab_blocks = jnp.transpose(
        vocab_rows.reshape(vocab_rows.shape[0], shards, slice_width), (1, 0, 2)
    )
    heads_here = projected.shape[1] // (2 * FEAT + HD)
    split_heads = jnp.transpose(
        projected.reshape(rows_here, heads_here, 2 * FEAT + HD).astype(jnp.float32), (1, 0, 2)
    )
    query_rows = split_heads[..., :FEAT]
    key_rows = split_heads[..., FEAT : 2 * FEAT]
    value_rows = split_heads[..., 2 * FEAT :]
    phi_query = features(query_rows, FEAT)
    phi_key = features(key_rows, FEAT)
    last_seg = segments[-1]
    member = (segments == last_seg).astype(jnp.float32)
    value_ones = jnp.concatenate(
        [value_rows, jnp.ones(value_rows.shape[:-1] + (1,), value_rows.dtype)], axis=-1
    )
    end_both = jnp.einsum(
        "hcp,hce->hpe", phi_key * member[None, :, None], value_ones, precision=PRECISE
    )
    end_both = jnp.pad(end_both, ((0, 0), (0, 1), (0, 0)))
    end_both = end_both.at[0, -1, 0].set((last_seg + 1).astype(jnp.float32))
    handed = from_behind(end_both.astype(jnp.bfloat16), "group", 1).astype(jnp.float32)
    got_state = handed[:, :-1, :-1]
    got_totals = handed[:, :-1, -1]
    got_tag = handed[0, -1, :1]
    initial = (got_state, got_totals, got_tag[0].astype(jnp.int32) - 1)
    block_len = rows_here
    blocks = rows_here // block_len

    def regroup(values):
        return jnp.transpose(
            values.reshape(values.shape[0], blocks, block_len, values.shape[-1]), (1, 0, 2, 3)
        )

    scan_inputs = (
        regroup(phi_query),
        regroup(phi_key),
        regroup(query_rows),
        regroup(key_rows),
        regroup(value_rows),
        segments.reshape(blocks, block_len),
    )

    def scan_step(state_carry, block_inputs):
        return block_step(state_carry, block_inputs, FEAT)

    _, (mixed_out, state_norm) = lax.scan(scan_step, initial, scan_inputs)
    attended = (
        jnp.transpose(mixed_out, (0, 2, 1, 3))
        .reshape(rows_here, heads_here * HD)
        .astype(jnp.bfloat16)
    )
    state_norms = jnp.transpose(state_norm, (1, 0, 2)).reshape(heads_here, rows_here)
    request_ids = jnp.arange(request_adapter.shape[0], dtype=jnp.int32)
    adapter_of = jnp.sum(
        jnp.where(segments[:, None] == request_ids[None, :], request_adapter[None, :], 0), axis=1
    )
    adapter_ids = jnp.arange(adapter_slot.shape[0], dtype=jnp.int32)
    slot_ids = jnp.sum(
        jnp.where(adapter_of[:, None] == adapter_ids[None, :], adapter_slot[None, :], 0), axis=1
    )
    column_slot = jnp.arange(lowered.shape[1], dtype=jnp.int32) // RANK
    local_slot = slot_ids - own_shard * (lowered.shape[1] // RANK)
    low_rank = jnp.where(
        local_slot[:, None] == column_slot[None, :], lowered, jnp.zeros_like(lowered)
    )
    out_blocks = jnp.transpose(
        out_weight.reshape(out_weight.shape[0], shards, slice_width), (1, 0, 2)
    )
    up_blocks = jnp.transpose(
        adapter_up.reshape(adapter_up.shape[0], shards, slice_width), (1, 0, 2)
    )
    summed, best = mp_exchange(
        attended, low_rank, out_blocks, up_blocks, residual, vocab_blocks, groups
    )
    max_logits = best[:, 0]
    return (summed, state_norms, max_logits)


def solution(mesh):
    placed = (
        P("group", None),
        P(),
        P(None, "mp"),
        P("mp", None),
        P(None, "mp"),
        P("mp", None),
        P(("group", "mp"), None),
        P("group"),
        P(),
        P(),
        P(),
    )
    return jax.shard_map(
        on_device,
        mesh=mesh,
        in_specs=placed,
        out_specs=(P("group", "mp"), P("mp", "group"), P(("group", "mp"))),
        check_vma=False,
    )
```

```python
import jax
import jax.numpy as jnp
from jax import lax
from jax.sharding import PartitionSpec as P
from jax.experimental import pallas as pl
from jax.experimental.pallas import tpu as pltpu

FEAT = 16
HD = 112
RANK = 16


EPSILON = 1e-05
PRECISE = lax.Precision.HIGHEST


def from_behind(value, axis, by):
    size = lax.axis_size(axis)
    pairs = [(i, i + by) for i in range(size) if 0 <= i + by < size]
    return lax.ppermute(value, axis, pairs)


def rms_normed(values, norm_gain):
    wide = values.astype(jnp.float32)
    meansq = jnp.mean(wide * wide, axis=-1, keepdims=True)
    return (wide * lax.rsqrt(meansq + EPSILON) * norm_gain).astype(jnp.bfloat16)


def features(vectors, feat_width):
    linear_part = vectors / feat_width**0.25
    outer_part = (vectors[..., :, None] * vectors[..., None, :]).reshape(
        vectors.shape[:-1] + (feat_width * feat_width,)
    )
    outer_part = outer_part / (2.0 * feat_width) ** 0.5
    ones_part = jnp.ones(vectors.shape[:-1] + (1,), jnp.float32)
    return jnp.concatenate([ones_part, linear_part, outer_part], axis=-1)


def block_step(state_carry, block_inputs, feat_width):
    states, totals, owner_seg = state_carry
    phi_query, phi_key, query_rows, key_rows, value_rows, seg_ids = block_inputs
    scaling = feat_width ** (-0.5)
    block_len = seg_ids.shape[0]
    position = jnp.arange(block_len, dtype=jnp.int32)
    allowed = (
        (position[:, None] >= position[None, :]) & (seg_ids[:, None] == seg_ids[None, :])
    ).astype(jnp.float32)
    carried = (seg_ids == owner_seg).astype(jnp.float32)[None, :]
    scores = jnp.einsum("hcf,hdf->hcd", query_rows, key_rows, precision=PRECISE) * scaling
    weights = (1.0 + scores + 0.5 * scores * scores) * allowed[None]
    numerator = jnp.einsum("hcd,hde->hce", weights, value_rows, precision=PRECISE)
    numerator = numerator + carried[..., None] * jnp.einsum(
        "hcp,hpe->hce", phi_query, states, precision=PRECISE
    )
    denominator = jnp.sum(weights, axis=-1) + carried * jnp.einsum(
        "hcp,hp->hc", phi_query, totals, precision=PRECISE
    )
    mixed_out = numerator / denominator[..., None]
    key_scores = jnp.einsum("hcf,hdf->hcd", key_rows, key_rows, precision=PRECISE) * scaling
    value_gram = jnp.einsum("hce,hde->hcd", value_rows, value_rows, precision=PRECISE)
    key_gram = (1.0 + key_scores + 0.5 * key_scores * key_scores) * value_gram
    diagonal = (position[:, None] == position[None, :]).astype(jnp.float32)
    row_terms = jnp.sum(key_gram * (allowed * (2.0 - diagonal))[None], axis=-1)
    local_squares = jnp.einsum("cd,hd->hc", allowed, row_terms, precision=PRECISE)
    along = jnp.sum(
        jnp.einsum("hcp,hpe->hce", phi_key, states, precision=PRECISE) * value_rows, axis=-1
    )
    cross_squares = jnp.einsum("cd,hd->hc", allowed, along, precision=PRECISE)
    state_squares = jnp.sum(states * states, axis=(1, 2))
    squares = carried * (state_squares[:, None] + 2.0 * cross_squares) + local_squares
    counted = carried * totals[:, :1] + jnp.sum(allowed, axis=-1)[None, :]
    state_norm = jnp.sqrt(squares / (counted * (feat_width * value_rows.shape[-1])))
    last_seg = seg_ids[-1]
    member = (seg_ids == last_seg).astype(jnp.float32)
    continues = (owner_seg == last_seg).astype(jnp.float32)
    new_states = continues * states + jnp.einsum(
        "hcp,hce->hpe", phi_key * member[None, :, None], value_rows, precision=PRECISE
    )
    new_totals = continues * totals + jnp.einsum("hcp,c->hp", phi_key, member, precision=PRECISE)
    return ((new_states, new_totals, last_seg), (mixed_out, state_norm))


def best_of(candidates, piece):
    logits = jnp.einsum("rd,vd->rv", candidates, piece, preferred_element_type=jnp.float32)
    return jnp.max(logits, axis=1)


def exchange_kernel(
    att_ref, low_ref, w_ref, u_ref, resid_ref, vocab_in, upd_ref, best_ref,
    land, acc, rows, tops, got, parts, vocab_ref, ring_sems, top_sems, vocab_sems,
):
    n = w_ref.shape[0]
    quarter = att_ref.shape[0] // 8
    block_rows = best_ref.shape[1]
    me = lax.axis_index("mp")
    grp = lax.axis_index("group")
    peers = [lax.rem(me + k, n) for k in range(1, n)]
    mesh_id = pl.DeviceIdType.MESH
    towards = (lax.rem(me + 1, n), lax.rem(me + n - 1, n))
    chains = [(0, 0), (1, 4), (0, 1), (1, 5), (0, 2), (1, 6), (0, 3), (1, 7)]
    spans = [pl.ds(quarter * piece, quarter) for _, piece in chains]

    for c in range(n):
        value = jnp.dot(att_ref[...], w_ref[c], preferred_element_type=jnp.float32)
        value = value + jnp.dot(low_ref[...], u_ref[c], preferred_element_type=jnp.float32)
        parts[c] = value.astype(parts.dtype)

    groups = vocab_ref.shape[0]
    holders = [lax.rem(grp + k, groups) for k in range(1, groups)]
    barrier = pltpu.get_barrier_semaphore()
    for p in peers:
        pl.semaphore_signal(barrier, inc=1, device_id=(grp, p), device_id_type=mesh_id)
    for h in holders:
        pl.semaphore_signal(barrier, inc=1, device_id=(h, me), device_id_type=mesh_id)
    pl.semaphore_wait(barrier, n - 1 + groups - 1)

    own_vocab = pltpu.make_async_copy(vocab_in, vocab_ref.at[grp], vocab_sems.at[2, 0])
    own_vocab.start()
    vocab_sent = []
    for h in holders:
        copy = pltpu.make_async_remote_copy(
            src_ref=vocab_in,
            dst_ref=vocab_ref.at[grp],
            send_sem=vocab_sems.at[0, h],
            recv_sem=vocab_sems.at[1, grp],
            device_id=(h, me),
            device_id_type=mesh_id,
        )
        copy.start()
        vocab_sent.append(copy)

    def ring_copy(phase, chain, step, src, dst):
        return pltpu.make_async_remote_copy(
            src_ref=src,
            dst_ref=dst,
            send_sem=ring_sems.at[phase, chain, 0, step],
            recv_sem=ring_sems.at[phase, chain, 1, step],
            device_id=(grp, towards[chains[chain][0]]),
            device_id_type=mesh_id,
        )

    def rs_chunk(chain, step):
        way = chains[chain][0]
        return lax.rem(me + (n - 1 - step if way == 0 else 1 + step) + n, n)

    def part(chunk, span):
        return parts[chunk, span].astype(jnp.float32)

    pending = [None] * len(chains)
    for step in range(n - 1):
        for chain in range(len(chains)):
            chunk = rs_chunk(chain, step)
            if step == 0:
                acc[chain, step] = part(chunk, spans[chain]).astype(acc.dtype)
            else:
                pending[chain].wait()
                acc[chain, step] = (
                    land[chain, step - 1].astype(jnp.float32) + part(chunk, spans[chain])
                ).astype(acc.dtype)
            src = acc.at[chain, step]
            pending[chain] = ring_copy(0, chain, step, src, land.at[chain, step])
            pending[chain].start()
    for chain in range(len(chains)):
        pending[chain].wait()
        total = land[chain, n - 2].astype(jnp.float32) + part(me, spans[chain])
        update = total.astype(upd_ref.dtype)
        upd_ref[spans[chain]] = update
        rows[me, spans[chain]] = (
            resid_ref[spans[chain]].astype(jnp.float32) + update.astype(jnp.float32)
        ).astype(rows.dtype)
        view = rows.at[me, spans[chain]]
        pending[chain] = ring_copy(1, chain, 0, view, view)
        pending[chain].start()

    for step in range(1, n - 1):
        for chain in range(len(chains)):
            pending[chain].wait()
            way = chains[chain][0]
            chunk = lax.rem(me + (n - step if way == 0 else step), n)
            view = rows.at[chunk, spans[chain]]
            pending[chain] = ring_copy(1, chain, step, view, view)
            pending[chain].start()
    for chain in range(len(chains)):
        pending[chain].wait()

    own_vocab.wait()
    for copy in vocab_sent:
        copy.wait_send()
    for h in holders:
        pltpu.make_async_remote_copy(
            src_ref=vocab_in,
            dst_ref=vocab_ref.at[h],
            send_sem=vocab_sems.at[0, h],
            recv_sem=vocab_sems.at[1, h],
            device_id=(h, me),
            device_id_type=mesh_id,
        ).wait_recv()

    scores = jnp.zeros((vocab_ref.shape[0] * vocab_ref.shape[2], rows.shape[1]), jnp.float32)
    for j in range(n):
        block = vocab_ref[:, j].reshape(scores.shape[0], rows.shape[2])
        scores = scores + lax.dot_general(
            block, rows[j], (((1,), (1,)), ((), ())),
            preferred_element_type=jnp.float32,
        )
    column_best = jnp.max(scores, axis=0, keepdims=True)
    for p in range(n):
        tops[p] = column_best[:, p * block_rows : (p + 1) * block_rows]

    sent = []
    for p in peers:
        copy = pltpu.make_async_remote_copy(
            src_ref=tops.at[p],
            dst_ref=got.at[me],
            send_sem=top_sems.at[0, p],
            recv_sem=top_sems.at[1, me],
            device_id=(grp, p),
            device_id_type=mesh_id,
        )
        copy.start()
        sent.append(copy)
    for copy in sent:
        copy.wait_send()
    for q in peers:
        pltpu.make_async_remote_copy(
            src_ref=tops.at[q],
            dst_ref=got.at[q],
            send_sem=top_sems.at[0, q],
            recv_sem=top_sems.at[1, q],
            device_id=(grp, q),
            device_id_type=mesh_id,
        ).wait_recv()
    best = tops[me]
    for q in peers:
        best = jnp.maximum(best, got[q])
    best_ref[...] = best


def mp_exchange(attended, low_rank, out_blocks, up_blocks, residual, vocab_blocks, groups):
    n, _, width = out_blocks.shape
    rows_here = attended.shape[0]
    block_rows = rows_here // n
    chains = 8
    vmem = pl.BlockSpec(memory_space=pltpu.VMEM)
    return pl.pallas_call(
        exchange_kernel,
        out_shape=(
            jax.ShapeDtypeStruct((rows_here, width), jnp.bfloat16),
            jax.ShapeDtypeStruct((1, block_rows), jnp.float32),
        ),
        in_specs=[vmem] * 6,
        out_specs=(vmem, vmem),
        scratch_shapes=[
            pltpu.VMEM((chains, n - 1, rows_here // chains, width), jnp.bfloat16),
            pltpu.VMEM((chains, n - 1, rows_here // chains, width), jnp.bfloat16),
            pltpu.VMEM((n, rows_here, width), jnp.bfloat16),
            pltpu.VMEM((n, 1, block_rows), jnp.float32),
            pltpu.VMEM((n, 1, block_rows), jnp.float32),
            pltpu.VMEM((n, rows_here, width), jnp.bfloat16),
            pltpu.VMEM((groups,) + vocab_blocks.shape, jnp.bfloat16),
            pltpu.SemaphoreType.DMA((2, chains, 2, n - 1)),
            pltpu.SemaphoreType.DMA((2, n)),
            pltpu.SemaphoreType.DMA((3, groups)),
        ],
        compiler_params=pltpu.CompilerParams(collective_id=0, has_side_effects=True),
    )(attended, low_rank, out_blocks, up_blocks, residual, vocab_blocks)


def on_device(
    hidden,
    norm_gain,
    qkv_weight,
    out_weight,
    adapter_down,
    adapter_up,
    vocab_rows,
    segments,
    request_adapter,
    adapter_slot,
    page_table,
):
    groups = lax.axis_size("group")
    own_group = lax.axis_index("group")
    shards = lax.axis_size("mp")
    own_shard = lax.axis_index("mp")
    rows_here = segments.shape[0]
    model_width = hidden.shape[1]
    slice_width = model_width // shards
    table = page_table.reshape(groups, -1)
    per_group = table.shape[1]
    per_peer = per_group // groups
    page_len = rows_here // per_group
    holders = table // per_group
    position = jnp.arange(per_group, dtype=jnp.int32)
    sort_keys = jnp.where(holders == own_group, position[None, :], per_group + position[None, :])
    ranked = jnp.argsort(sort_keys, axis=1)[:, :per_peer]
    picked = jnp.take_along_axis(table, ranked, axis=1) - own_group * per_group
    outgoing = hidden.reshape(per_group, page_len, model_width)[picked]
    normed_pages = rms_normed(outgoing, norm_gain)
    projected_pages = jnp.einsum(
        "abrd,dc->abrc", normed_pages, qkv_weight, preferred_element_type=jnp.float32
    ).astype(jnp.bfloat16)
    lowered_pages = jnp.einsum(
        "abrd,dc->abrc", normed_pages, adapter_down, preferred_element_type=jnp.float32
    ).astype(jnp.bfloat16)
    kept_pages = lax.dynamic_slice_in_dim(outgoing, own_shard * slice_width, slice_width, 3)
    widths = (kept_pages.shape[3], projected_pages.shape[3], lowered_pages.shape[3])
    packed = lax.all_to_all(
        jnp.concatenate([kept_pages, projected_pages, lowered_pages], axis=3),
        "group", split_axis=0, concat_axis=0, tiled=True,
    )
    own_holders = lax.dynamic_index_in_dim(holders, own_group, 0, keepdims=False)
    onehot = (own_holders[:, None] == jnp.arange(groups, dtype=jnp.int32)[None, :]).astype(
        jnp.int32
    )
    earlier = jnp.sum((jnp.cumsum(onehot, axis=0) - onehot) * onehot, axis=1)
    source_rows = own_holders * per_peer + earlier

    def placed(received):
        gathered_rows = received.reshape((groups * per_peer,) + received.shape[2:])[source_rows]
        return gathered_rows.reshape((rows_here,) + received.shape[3:])

    all_rows = placed(packed)
    residual = all_rows[:, : widths[0]]
    projected = all_rows[:, widths[0] : widths[0] + widths[1]]
    lowered = all_rows[:, widths[0] + widths[1] :]
    vocab_blocks = jnp.transpose(
        vocab_rows.reshape(vocab_rows.shape[0], shards, slice_width), (1, 0, 2)
    )
    heads_here = projected.shape[1] // (2 * FEAT + HD)
    split_heads = jnp.transpose(
        projected.reshape(rows_here, heads_here, 2 * FEAT + HD).astype(jnp.float32), (1, 0, 2)
    )
    query_rows = split_heads[..., :FEAT]
    key_rows = split_heads[..., FEAT : 2 * FEAT]
    value_rows = split_heads[..., 2 * FEAT :]
    phi_query = features(query_rows, FEAT)
    phi_key = features(key_rows, FEAT)
    last_seg = segments[-1]
    member = (segments == last_seg).astype(jnp.float32)
    value_ones = jnp.concatenate(
        [value_rows, jnp.ones(value_rows.shape[:-1] + (1,), value_rows.dtype)], axis=-1
    )
    end_both = jnp.einsum(
        "hcp,hce->hpe", phi_key * member[None, :, None], value_ones, precision=PRECISE
    )
    end_both = jnp.pad(end_both, ((0, 0), (0, 1), (0, 0)))
    end_both = end_both.at[0, -1, 0].set((last_seg + 1).astype(jnp.float32))
    handed = from_behind(end_both.astype(jnp.bfloat16), "group", 1).astype(jnp.float32)
    got_state = handed[:, :-1, :-1]
    got_totals = handed[:, :-1, -1]
    got_tag = handed[0, -1, :1]
    initial = (got_state, got_totals, got_tag[0].astype(jnp.int32) - 1)
    block_len = rows_here
    blocks = rows_here // block_len

    def regroup(values):
        return jnp.transpose(
            values.reshape(values.shape[0], blocks, block_len, values.shape[-1]), (1, 0, 2, 3)
        )

    scan_inputs = (
        regroup(phi_query),
        regroup(phi_key),
        regroup(query_rows),
        regroup(key_rows),
        regroup(value_rows),
        segments.reshape(blocks, block_len),
    )

    def scan_step(state_carry, block_inputs):
        return block_step(state_carry, block_inputs, FEAT)

    _, (mixed_out, state_norm) = lax.scan(scan_step, initial, scan_inputs)
    attended = (
        jnp.transpose(mixed_out, (0, 2, 1, 3))
        .reshape(rows_here, heads_here * HD)
        .astype(jnp.bfloat16)
    )
    state_norms = jnp.transpose(state_norm, (1, 0, 2)).reshape(heads_here, rows_here)
    request_ids = jnp.arange(request_adapter.shape[0], dtype=jnp.int32)
    adapter_of = jnp.sum(
        jnp.where(segments[:, None] == request_ids[None, :], request_adapter[None, :], 0), axis=1
    )
    adapter_ids = jnp.arange(adapter_slot.shape[0], dtype=jnp.int32)
    slot_ids = jnp.sum(
        jnp.where(adapter_of[:, None] == adapter_ids[None, :], adapter_slot[None, :], 0), axis=1
    )
    column_slot = jnp.arange(lowered.shape[1], dtype=jnp.int32) // RANK
    local_slot = slot_ids - own_shard * (lowered.shape[1] // RANK)
    low_rank = jnp.where(
        local_slot[:, None] == column_slot[None, :], lowered, jnp.zeros_like(lowered)
    )
    out_blocks = jnp.transpose(
        out_weight.reshape(out_weight.shape[0], shards, slice_width), (1, 0, 2)
    )
    up_blocks = jnp.transpose(
        adapter_up.reshape(adapter_up.shape[0], shards, slice_width), (1, 0, 2)
    )
    summed, best = mp_exchange(
        attended, low_rank, out_blocks, up_blocks, residual, vocab_blocks, groups
    )
    max_logits = best[0]
    return (summed, state_norms, max_logits)


def solution(mesh):
    placed = (
        P("group", None),
        P(),
        P(None, "mp"),
        P("mp", None),
        P(None, "mp"),
        P("mp", None),
        P(("group", "mp"), None),
        P("group"),
        P(),
        P(),
        P(),
    )
    return jax.shard_map(
        on_device,
        mesh=mesh,
        in_specs=placed,
        out_specs=(P("group", "mp"), P("mp", "group"), P(("group", "mp"))),
        check_vma=False,
    )
```

```python
import jax
import jax.numpy as jnp
from jax import lax
from jax.sharding import PartitionSpec as P
from jax.experimental import pallas as pl
from jax.experimental.pallas import tpu as pltpu

FEAT = 16
HD = 112
RANK = 16


EPSILON = 1e-05
PRECISE = lax.Precision.HIGHEST


def from_behind(value, axis, by):
    size = lax.axis_size(axis)
    pairs = [(i, i + by) for i in range(size) if 0 <= i + by < size]
    return lax.ppermute(value, axis, pairs)


def rms_normed(values, norm_gain):
    wide = values.astype(jnp.float32)
    meansq = jnp.mean(wide * wide, axis=-1, keepdims=True)
    return (wide * lax.rsqrt(meansq + EPSILON) * norm_gain).astype(jnp.bfloat16)


def features(vectors, feat_width):
    linear_part = vectors / feat_width**0.25
    outer_part = (vectors[..., :, None] * vectors[..., None, :]).reshape(
        vectors.shape[:-1] + (feat_width * feat_width,)
    )
    outer_part = outer_part / (2.0 * feat_width) ** 0.5
    ones_part = jnp.ones(vectors.shape[:-1] + (1,), jnp.float32)
    return jnp.concatenate([ones_part, linear_part, outer_part], axis=-1)


def block_step(state_carry, block_inputs, feat_width):
    states, totals, owner_seg = state_carry
    phi_query, phi_key, query_rows, key_rows, value_rows, seg_ids = block_inputs
    scaling = feat_width ** (-0.5)
    block_len = seg_ids.shape[0]
    position = jnp.arange(block_len, dtype=jnp.int32)
    allowed = (
        (position[:, None] >= position[None, :]) & (seg_ids[:, None] == seg_ids[None, :])
    ).astype(jnp.float32)
    carried = (seg_ids == owner_seg).astype(jnp.float32)[None, :]
    scores = jnp.einsum("hcf,hdf->hcd", query_rows, key_rows, precision=PRECISE) * scaling
    weights = (1.0 + scores + 0.5 * scores * scores) * allowed[None]
    numerator = jnp.einsum("hcd,hde->hce", weights, value_rows, precision=PRECISE)
    numerator = numerator + carried[..., None] * jnp.einsum(
        "hcp,hpe->hce", phi_query, states, precision=PRECISE
    )
    denominator = jnp.sum(weights, axis=-1) + carried * jnp.einsum(
        "hcp,hp->hc", phi_query, totals, precision=PRECISE
    )
    mixed_out = numerator / denominator[..., None]
    key_scores = jnp.einsum("hcf,hdf->hcd", key_rows, key_rows, precision=PRECISE) * scaling
    value_gram = jnp.einsum("hce,hde->hcd", value_rows, value_rows, precision=PRECISE)
    key_gram = (1.0 + key_scores + 0.5 * key_scores * key_scores) * value_gram
    diagonal = (position[:, None] == position[None, :]).astype(jnp.float32)
    row_terms = jnp.sum(key_gram * (allowed * (2.0 - diagonal))[None], axis=-1)
    local_squares = jnp.einsum("cd,hd->hc", allowed, row_terms, precision=PRECISE)
    along = jnp.sum(
        jnp.einsum("hcp,hpe->hce", phi_key, states, precision=PRECISE) * value_rows, axis=-1
    )
    cross_squares = jnp.einsum("cd,hd->hc", allowed, along, precision=PRECISE)
    state_squares = jnp.sum(states * states, axis=(1, 2))
    squares = carried * (state_squares[:, None] + 2.0 * cross_squares) + local_squares
    counted = carried * totals[:, :1] + jnp.sum(allowed, axis=-1)[None, :]
    state_norm = jnp.sqrt(squares / (counted * (feat_width * value_rows.shape[-1])))
    last_seg = seg_ids[-1]
    member = (seg_ids == last_seg).astype(jnp.float32)
    continues = (owner_seg == last_seg).astype(jnp.float32)
    new_states = continues * states + jnp.einsum(
        "hcp,hce->hpe", phi_key * member[None, :, None], value_rows, precision=PRECISE
    )
    new_totals = continues * totals + jnp.einsum("hcp,c->hp", phi_key, member, precision=PRECISE)
    return ((new_states, new_totals, last_seg), (mixed_out, state_norm))


def best_of(candidates, piece):
    logits = jnp.einsum("rd,vd->rv", candidates, piece, preferred_element_type=jnp.float32)
    return jnp.max(logits, axis=1)


def exchange_kernel(
    att_ref, low_ref, w_ref, u_ref, resid_ref, vocab_in, upd_ref, best_ref,
    land, acc, rows, tops, got, parts, vocab_ref, ring_sems, top_sems, vocab_sems,
):
    n = rows.shape[0]
    quarter = att_ref.shape[0] // 8
    block_rows = best_ref.shape[1]
    me = lax.axis_index("mp")
    grp = lax.axis_index("group")
    peers = [lax.rem(me + k, n) for k in range(1, n)]
    mesh_id = pl.DeviceIdType.MESH
    towards = (lax.rem(me + 1, n), lax.rem(me + n - 1, n))
    chains = [(0, 0), (1, 4), (0, 1), (1, 5), (0, 2), (1, 6), (0, 3), (1, 7)]
    spans = [pl.ds(quarter * piece, quarter) for _, piece in chains]

    width = parts.shape[2]
    for c in range(n):
        cols = slice(c * width, (c + 1) * width)
        value = jnp.dot(att_ref[...], w_ref[:, cols], preferred_element_type=jnp.float32)
        value = value + jnp.dot(low_ref[...], u_ref[:, cols], preferred_element_type=jnp.float32)
        parts[c] = value.astype(parts.dtype)

    groups = vocab_ref.shape[0]
    holders = [lax.rem(grp + k, groups) for k in range(1, groups)]
    barrier = pltpu.get_barrier_semaphore()
    for p in peers:
        pl.semaphore_signal(barrier, inc=1, device_id=(grp, p), device_id_type=mesh_id)
    for h in holders:
        pl.semaphore_signal(barrier, inc=1, device_id=(h, me), device_id_type=mesh_id)
    pl.semaphore_wait(barrier, n - 1 + groups - 1)

    own_vocab = pltpu.make_async_copy(vocab_in, vocab_ref.at[grp], vocab_sems.at[2, 0])
    own_vocab.start()
    vocab_sent = []
    for h in holders:
        copy = pltpu.make_async_remote_copy(
            src_ref=vocab_in,
            dst_ref=vocab_ref.at[grp],
            send_sem=vocab_sems.at[0, h],
            recv_sem=vocab_sems.at[1, grp],
            device_id=(h, me),
            device_id_type=mesh_id,
        )
        copy.start()
        vocab_sent.append(copy)

    def ring_copy(phase, chain, step, src, dst):
        return pltpu.make_async_remote_copy(
            src_ref=src,
            dst_ref=dst,
            send_sem=ring_sems.at[phase, chain, 0, step],
            recv_sem=ring_sems.at[phase, chain, 1, step],
            device_id=(grp, towards[chains[chain][0]]),
            device_id_type=mesh_id,
        )

    def rs_chunk(chain, step):
        way = chains[chain][0]
        return lax.rem(me + (n - 1 - step if way == 0 else 1 + step) + n, n)

    def part(chunk, span):
        return parts[chunk, span].astype(jnp.float32)

    pending = [None] * len(chains)
    for step in range(n - 1):
        for chain in range(len(chains)):
            chunk = rs_chunk(chain, step)
            if step == 0:
                acc[chain, step] = part(chunk, spans[chain]).astype(acc.dtype)
            else:
                pending[chain].wait()
                acc[chain, step] = (
                    land[chain, step - 1].astype(jnp.float32) + part(chunk, spans[chain])
                ).astype(acc.dtype)
            src = acc.at[chain, step]
            pending[chain] = ring_copy(0, chain, step, src, land.at[chain, step])
            pending[chain].start()
    for chain in range(len(chains)):
        pending[chain].wait()
        total = land[chain, n - 2].astype(jnp.float32) + part(me, spans[chain])
        update = total.astype(upd_ref.dtype)
        upd_ref[spans[chain]] = update
        rows[me, spans[chain]] = (
            resid_ref[spans[chain]].astype(jnp.float32) + update.astype(jnp.float32)
        ).astype(rows.dtype)
        view = rows.at[me, spans[chain]]
        pending[chain] = ring_copy(1, chain, 0, view, view)
        pending[chain].start()

    for step in range(1, n - 1):
        for chain in range(len(chains)):
            pending[chain].wait()
            way = chains[chain][0]
            chunk = lax.rem(me + (n - step if way == 0 else step), n)
            view = rows.at[chunk, spans[chain]]
            pending[chain] = ring_copy(1, chain, step, view, view)
            pending[chain].start()
    for chain in range(len(chains)):
        pending[chain].wait()

    own_vocab.wait()
    for copy in vocab_sent:
        copy.wait_send()
    for h in holders:
        pltpu.make_async_remote_copy(
            src_ref=vocab_in,
            dst_ref=vocab_ref.at[h],
            send_sem=vocab_sems.at[0, h],
            recv_sem=vocab_sems.at[1, h],
            device_id=(h, me),
            device_id_type=mesh_id,
        ).wait_recv()

    scores = jnp.zeros((vocab_ref.shape[0] * vocab_ref.shape[2], rows.shape[1]), jnp.float32)
    for j in range(n):
        block = vocab_ref[:, j].reshape(scores.shape[0], rows.shape[2])
        scores = scores + lax.dot_general(
            block, rows[j], (((1,), (1,)), ((), ())),
            preferred_element_type=jnp.float32,
        )
    column_best = jnp.max(scores, axis=0, keepdims=True)
    for p in range(n):
        tops[p] = column_best[:, p * block_rows : (p + 1) * block_rows]

    sent = []
    for p in peers:
        copy = pltpu.make_async_remote_copy(
            src_ref=tops.at[p],
            dst_ref=got.at[me],
            send_sem=top_sems.at[0, p],
            recv_sem=top_sems.at[1, me],
            device_id=(grp, p),
            device_id_type=mesh_id,
        )
        copy.start()
        sent.append(copy)
    for copy in sent:
        copy.wait_send()
    for q in peers:
        pltpu.make_async_remote_copy(
            src_ref=tops.at[q],
            dst_ref=got.at[q],
            send_sem=top_sems.at[0, q],
            recv_sem=top_sems.at[1, q],
            device_id=(grp, q),
            device_id_type=mesh_id,
        ).wait_recv()
    best = tops[me]
    for q in peers:
        best = jnp.maximum(best, got[q])
    best_ref[...] = best


def mp_exchange(attended, low_rank, out_blocks, up_blocks, residual, vocab_blocks, groups):
    n = vocab_blocks.shape[0]
    width = out_blocks.shape[1] // n
    rows_here = attended.shape[0]
    block_rows = rows_here // n
    chains = 8
    vmem = pl.BlockSpec(memory_space=pltpu.VMEM)
    return pl.pallas_call(
        exchange_kernel,
        out_shape=(
            jax.ShapeDtypeStruct((rows_here, width), jnp.bfloat16),
            jax.ShapeDtypeStruct((1, block_rows), jnp.float32),
        ),
        in_specs=[vmem] * 6,
        out_specs=(vmem, vmem),
        scratch_shapes=[
            pltpu.VMEM((chains, n - 1, rows_here // chains, width), jnp.bfloat16),
            pltpu.VMEM((chains, n - 1, rows_here // chains, width), jnp.bfloat16),
            pltpu.VMEM((n, rows_here, width), jnp.bfloat16),
            pltpu.VMEM((n, 1, block_rows), jnp.float32),
            pltpu.VMEM((n, 1, block_rows), jnp.float32),
            pltpu.VMEM((n, rows_here, width), jnp.bfloat16),
            pltpu.VMEM((groups,) + vocab_blocks.shape, jnp.bfloat16),
            pltpu.SemaphoreType.DMA((2, chains, 2, n - 1)),
            pltpu.SemaphoreType.DMA((2, n)),
            pltpu.SemaphoreType.DMA((3, groups)),
        ],
        compiler_params=pltpu.CompilerParams(collective_id=0, has_side_effects=True),
    )(attended, low_rank, out_blocks, up_blocks, residual, vocab_blocks)


def on_device(
    hidden,
    norm_gain,
    qkv_weight,
    out_weight,
    adapter_down,
    adapter_up,
    vocab_rows,
    segments,
    request_adapter,
    adapter_slot,
    page_table,
):
    groups = lax.axis_size("group")
    own_group = lax.axis_index("group")
    shards = lax.axis_size("mp")
    own_shard = lax.axis_index("mp")
    rows_here = segments.shape[0]
    model_width = hidden.shape[1]
    slice_width = model_width // shards
    table = page_table.reshape(groups, -1)
    per_group = table.shape[1]
    per_peer = per_group // groups
    page_len = rows_here // per_group
    holders = table // per_group
    position = jnp.arange(per_group, dtype=jnp.int32)
    sort_keys = jnp.where(holders == own_group, position[None, :], per_group + position[None, :])
    ranked = jnp.argsort(sort_keys, axis=1)[:, :per_peer]
    picked = jnp.take_along_axis(table, ranked, axis=1) - own_group * per_group
    outgoing = hidden.reshape(per_group, page_len, model_width)[picked]
    normed_pages = rms_normed(outgoing, norm_gain)
    projected_pages = jnp.einsum(
        "abrd,dc->abrc", normed_pages, qkv_weight, preferred_element_type=jnp.float32
    ).astype(jnp.bfloat16)
    lowered_pages = jnp.einsum(
        "abrd,dc->abrc", normed_pages, adapter_down, preferred_element_type=jnp.float32
    ).astype(jnp.bfloat16)
    kept_pages = lax.dynamic_slice_in_dim(outgoing, own_shard * slice_width, slice_width, 3)
    widths = (kept_pages.shape[3], projected_pages.shape[3], lowered_pages.shape[3])
    packed = lax.all_to_all(
        jnp.concatenate([kept_pages, projected_pages, lowered_pages], axis=3),
        "group", split_axis=0, concat_axis=0, tiled=True,
    )
    own_holders = lax.dynamic_index_in_dim(holders, own_group, 0, keepdims=False)
    onehot = (own_holders[:, None] == jnp.arange(groups, dtype=jnp.int32)[None, :]).astype(
        jnp.int32
    )
    earlier = jnp.sum((jnp.cumsum(onehot, axis=0) - onehot) * onehot, axis=1)
    source_rows = own_holders * per_peer + earlier

    def placed(received):
        gathered_rows = received.reshape((groups * per_peer,) + received.shape[2:])[source_rows]
        return gathered_rows.reshape((rows_here,) + received.shape[3:])

    all_rows = placed(packed)
    residual = all_rows[:, : widths[0]]
    projected = all_rows[:, widths[0] : widths[0] + widths[1]]
    lowered = all_rows[:, widths[0] + widths[1] :]
    vocab_blocks = jnp.transpose(
        vocab_rows.reshape(vocab_rows.shape[0], shards, slice_width), (1, 0, 2)
    )
    heads_here = projected.shape[1] // (2 * FEAT + HD)
    split_heads = jnp.transpose(
        projected.reshape(rows_here, heads_here, 2 * FEAT + HD).astype(jnp.float32), (1, 0, 2)
    )
    query_rows = split_heads[..., :FEAT]
    key_rows = split_heads[..., FEAT : 2 * FEAT]
    value_rows = split_heads[..., 2 * FEAT :]
    phi_query = features(query_rows, FEAT)
    phi_key = features(key_rows, FEAT)
    last_seg = segments[-1]
    member = (segments == last_seg).astype(jnp.float32)
    value_ones = jnp.concatenate(
        [value_rows, jnp.ones(value_rows.shape[:-1] + (1,), value_rows.dtype)], axis=-1
    )
    end_both = jnp.einsum(
        "hcp,hce->hpe", phi_key * member[None, :, None], value_ones, precision=PRECISE
    )
    end_both = jnp.pad(end_both, ((0, 0), (0, 1), (0, 0)))
    end_both = end_both.at[0, -1, 0].set((last_seg + 1).astype(jnp.float32))
    handed = from_behind(end_both.astype(jnp.bfloat16), "group", 1).astype(jnp.float32)
    got_state = handed[:, :-1, :-1]
    got_totals = handed[:, :-1, -1]
    got_tag = handed[0, -1, :1]
    initial = (got_state, got_totals, got_tag[0].astype(jnp.int32) - 1)
    block_len = rows_here
    blocks = rows_here // block_len

    def regroup(values):
        return jnp.transpose(
            values.reshape(values.shape[0], blocks, block_len, values.shape[-1]), (1, 0, 2, 3)
        )

    scan_inputs = (
        regroup(phi_query),
        regroup(phi_key),
        regroup(query_rows),
        regroup(key_rows),
        regroup(value_rows),
        segments.reshape(blocks, block_len),
    )

    def scan_step(state_carry, block_inputs):
        return block_step(state_carry, block_inputs, FEAT)

    _, (mixed_out, state_norm) = lax.scan(scan_step, initial, scan_inputs)
    attended = (
        jnp.transpose(mixed_out, (0, 2, 1, 3))
        .reshape(rows_here, heads_here * HD)
        .astype(jnp.bfloat16)
    )
    state_norms = jnp.transpose(state_norm, (1, 0, 2)).reshape(heads_here, rows_here)
    request_ids = jnp.arange(request_adapter.shape[0], dtype=jnp.int32)
    adapter_of = jnp.sum(
        jnp.where(segments[:, None] == request_ids[None, :], request_adapter[None, :], 0), axis=1
    )
    adapter_ids = jnp.arange(adapter_slot.shape[0], dtype=jnp.int32)
    slot_ids = jnp.sum(
        jnp.where(adapter_of[:, None] == adapter_ids[None, :], adapter_slot[None, :], 0), axis=1
    )
    column_slot = jnp.arange(lowered.shape[1], dtype=jnp.int32) // RANK
    local_slot = slot_ids - own_shard * (lowered.shape[1] // RANK)
    low_rank = jnp.where(
        local_slot[:, None] == column_slot[None, :], lowered, jnp.zeros_like(lowered)
    )
    out_blocks, up_blocks = out_weight, adapter_up
    summed, best = mp_exchange(
        attended, low_rank, out_blocks, up_blocks, residual, vocab_blocks, groups
    )
    max_logits = best[0]
    return (summed, state_norms, max_logits)


def solution(mesh):
    placed = (
        P("group", None),
        P(),
        P(None, "mp"),
        P("mp", None),
        P(None, "mp"),
        P("mp", None),
        P(("group", "mp"), None),
        P("group"),
        P(),
        P(),
        P(),
    )
    return jax.shard_map(
        on_device,
        mesh=mesh,
        in_specs=placed,
        out_specs=(P("group", "mp"), P("mp", "group"), P(("group", "mp"))),
        check_vma=False,
    )
```

```python
import jax
import jax.numpy as jnp
from jax import lax
from jax.sharding import PartitionSpec as P
from jax.experimental import pallas as pl
from jax.experimental.pallas import tpu as pltpu

FEAT = 16
HD = 112
RANK = 16


EPSILON = 1e-05
PRECISE = lax.Precision.HIGHEST


def from_behind(value, axis, by):
    size = lax.axis_size(axis)
    pairs = [(i, i + by) for i in range(size) if 0 <= i + by < size]
    return lax.ppermute(value, axis, pairs)


def rms_normed(values, norm_gain):
    wide = values.astype(jnp.float32)
    meansq = jnp.mean(wide * wide, axis=-1, keepdims=True)
    return (wide * lax.rsqrt(meansq + EPSILON) * norm_gain).astype(jnp.bfloat16)


def features(vectors, feat_width):
    linear_part = vectors / feat_width**0.25
    outer_part = (vectors[..., :, None] * vectors[..., None, :]).reshape(
        vectors.shape[:-1] + (feat_width * feat_width,)
    )
    outer_part = outer_part / (2.0 * feat_width) ** 0.5
    ones_part = jnp.ones(vectors.shape[:-1] + (1,), jnp.float32)
    return jnp.concatenate([ones_part, linear_part, outer_part], axis=-1)


def block_step(state_carry, block_inputs, feat_width):
    states, totals, owner_seg = state_carry
    phi_query, phi_key, query_rows, key_rows, value_rows, seg_ids = block_inputs
    scaling = feat_width ** (-0.5)
    block_len = seg_ids.shape[0]
    position = jnp.arange(block_len, dtype=jnp.int32)
    allowed = (
        (position[:, None] >= position[None, :]) & (seg_ids[:, None] == seg_ids[None, :])
    ).astype(jnp.float32)
    carried = (seg_ids == owner_seg).astype(jnp.float32)[None, :]
    scores = jnp.einsum("hcf,hdf->hcd", query_rows, key_rows, precision=PRECISE) * scaling
    weights = (1.0 + scores + 0.5 * scores * scores) * allowed[None]
    numerator = jnp.einsum("hcd,hde->hce", weights, value_rows, precision=PRECISE)
    numerator = numerator + carried[..., None] * jnp.einsum(
        "hcp,hpe->hce", phi_query, states, precision=PRECISE
    )
    denominator = jnp.sum(weights, axis=-1) + carried * jnp.einsum(
        "hcp,hp->hc", phi_query, totals, precision=PRECISE
    )
    mixed_out = numerator / denominator[..., None]
    key_scores = jnp.einsum("hcf,hdf->hcd", key_rows, key_rows, precision=PRECISE) * scaling
    value_gram = jnp.einsum("hce,hde->hcd", value_rows, value_rows, precision=PRECISE)
    key_gram = (1.0 + key_scores + 0.5 * key_scores * key_scores) * value_gram
    diagonal = (position[:, None] == position[None, :]).astype(jnp.float32)
    row_terms = jnp.sum(key_gram * (allowed * (2.0 - diagonal))[None], axis=-1)
    local_squares = jnp.einsum("cd,hd->hc", allowed, row_terms, precision=PRECISE)
    along = jnp.sum(
        jnp.einsum("hcp,hpe->hce", phi_key, states, precision=PRECISE) * value_rows, axis=-1
    )
    cross_squares = jnp.einsum("cd,hd->hc", allowed, along, precision=PRECISE)
    state_squares = jnp.sum(states * states, axis=(1, 2))
    squares = carried * (state_squares[:, None] + 2.0 * cross_squares) + local_squares
    counted = carried * totals[:, :1] + jnp.sum(allowed, axis=-1)[None, :]
    state_norm = jnp.sqrt(squares / (counted * (feat_width * value_rows.shape[-1])))
    last_seg = seg_ids[-1]
    member = (seg_ids == last_seg).astype(jnp.float32)
    continues = (owner_seg == last_seg).astype(jnp.float32)
    new_states = continues * states + jnp.einsum(
        "hcp,hce->hpe", phi_key * member[None, :, None], value_rows, precision=PRECISE
    )
    new_totals = continues * totals + jnp.einsum("hcp,c->hp", phi_key, member, precision=PRECISE)
    return ((new_states, new_totals, last_seg), (mixed_out, state_norm))


def best_of(candidates, piece):
    logits = jnp.einsum("rd,vd->rv", candidates, piece, preferred_element_type=jnp.float32)
    return jnp.max(logits, axis=1)


def exchange_kernel(
    att_ref, low_ref, w_ref, u_ref, resid_ref, vocab_in, upd_ref, best_ref,
    land, acc, rows, tops, got, parts, vocab_ref, ring_sems, top_sems, vocab_sems,
):
    n = rows.shape[0]
    quarter = att_ref.shape[0] // 16
    block_rows = best_ref.shape[1]
    me = lax.axis_index("mp")
    grp = lax.axis_index("group")
    peers = [lax.rem(me + k, n) for k in range(1, n)]
    mesh_id = pl.DeviceIdType.MESH
    towards = (lax.rem(me + 1, n), lax.rem(me + n - 1, n))
    chains = [(way, piece + 8 * way) for piece in range(8) for way in range(2)]
    spans = [pl.ds(quarter * piece, quarter) for _, piece in chains]

    width = parts.shape[2]
    for c in range(n):
        cols = slice(c * width, (c + 1) * width)
        value = jnp.dot(att_ref[...], w_ref[:, cols], preferred_element_type=jnp.float32)
        value = value + jnp.dot(low_ref[...], u_ref[:, cols], preferred_element_type=jnp.float32)
        parts[c] = value.astype(parts.dtype)

    groups = vocab_ref.shape[0]
    holders = [lax.rem(grp + k, groups) for k in range(1, groups)]
    barrier = pltpu.get_barrier_semaphore()
    for p in peers:
        pl.semaphore_signal(barrier, inc=1, device_id=(grp, p), device_id_type=mesh_id)
    for h in holders:
        pl.semaphore_signal(barrier, inc=1, device_id=(h, me), device_id_type=mesh_id)
    pl.semaphore_wait(barrier, n - 1 + groups - 1)

    own_vocab = pltpu.make_async_copy(vocab_in, vocab_ref.at[grp], vocab_sems.at[2, 0])
    own_vocab.start()
    vocab_sent = []
    for h in holders:
        copy = pltpu.make_async_remote_copy(
            src_ref=vocab_in,
            dst_ref=vocab_ref.at[grp],
            send_sem=vocab_sems.at[0, h],
            recv_sem=vocab_sems.at[1, grp],
            device_id=(h, me),
            device_id_type=mesh_id,
        )
        copy.start()
        vocab_sent.append(copy)

    def ring_copy(phase, chain, step, src, dst):
        return pltpu.make_async_remote_copy(
            src_ref=src,
            dst_ref=dst,
            send_sem=ring_sems.at[phase, chain, 0, step],
            recv_sem=ring_sems.at[phase, chain, 1, step],
            device_id=(grp, towards[chains[chain][0]]),
            device_id_type=mesh_id,
        )

    def rs_chunk(chain, step):
        way = chains[chain][0]
        return lax.rem(me + (n - 1 - step if way == 0 else 1 + step) + n, n)

    def part(chunk, span):
        return parts[chunk, span].astype(jnp.float32)

    pending = [None] * len(chains)
    for step in range(n - 1):
        for chain in range(len(chains)):
            chunk = rs_chunk(chain, step)
            if step == 0:
                acc[chain, step] = part(chunk, spans[chain]).astype(acc.dtype)
            else:
                pending[chain].wait()
                acc[chain, step] = (
                    land[chain, step - 1].astype(jnp.float32) + part(chunk, spans[chain])
                ).astype(acc.dtype)
            src = acc.at[chain, step]
            pending[chain] = ring_copy(0, chain, step, src, land.at[chain, step])
            pending[chain].start()
    for chain in range(len(chains)):
        pending[chain].wait()
        total = land[chain, n - 2].astype(jnp.float32) + part(me, spans[chain])
        update = total.astype(upd_ref.dtype)
        upd_ref[spans[chain]] = update
        rows[me, spans[chain]] = (
            resid_ref[spans[chain]].astype(jnp.float32) + update.astype(jnp.float32)
        ).astype(rows.dtype)
        view = rows.at[me, spans[chain]]
        pending[chain] = ring_copy(1, chain, 0, view, view)
        pending[chain].start()

    for step in range(1, n - 1):
        for chain in range(len(chains)):
            pending[chain].wait()
            way = chains[chain][0]
            chunk = lax.rem(me + (n - step if way == 0 else step), n)
            view = rows.at[chunk, spans[chain]]
            pending[chain] = ring_copy(1, chain, step, view, view)
            pending[chain].start()
    for chain in range(len(chains)):
        pending[chain].wait()

    own_vocab.wait()
    for copy in vocab_sent:
        copy.wait_send()
    for h in holders:
        pltpu.make_async_remote_copy(
            src_ref=vocab_in,
            dst_ref=vocab_ref.at[h],
            send_sem=vocab_sems.at[0, h],
            recv_sem=vocab_sems.at[1, h],
            device_id=(h, me),
            device_id_type=mesh_id,
        ).wait_recv()

    scores = jnp.zeros((vocab_ref.shape[0] * vocab_ref.shape[2], rows.shape[1]), jnp.float32)
    for j in range(n):
        block = vocab_ref[:, j].reshape(scores.shape[0], rows.shape[2])
        scores = scores + lax.dot_general(
            block, rows[j], (((1,), (1,)), ((), ())),
            preferred_element_type=jnp.float32,
        )
    column_best = jnp.max(scores, axis=0, keepdims=True)
    for p in range(n):
        tops[p] = column_best[:, p * block_rows : (p + 1) * block_rows]

    sent = []
    for p in peers:
        copy = pltpu.make_async_remote_copy(
            src_ref=tops.at[p],
            dst_ref=got.at[me],
            send_sem=top_sems.at[0, p],
            recv_sem=top_sems.at[1, me],
            device_id=(grp, p),
            device_id_type=mesh_id,
        )
        copy.start()
        sent.append(copy)
    for copy in sent:
        copy.wait_send()
    for q in peers:
        pltpu.make_async_remote_copy(
            src_ref=tops.at[q],
            dst_ref=got.at[q],
            send_sem=top_sems.at[0, q],
            recv_sem=top_sems.at[1, q],
            device_id=(grp, q),
            device_id_type=mesh_id,
        ).wait_recv()
    best = tops[me]
    for q in peers:
        best = jnp.maximum(best, got[q])
    best_ref[...] = best


def mp_exchange(attended, low_rank, out_blocks, up_blocks, residual, vocab_blocks, groups):
    n = vocab_blocks.shape[0]
    width = out_blocks.shape[1] // n
    rows_here = attended.shape[0]
    block_rows = rows_here // n
    chains = 16
    vmem = pl.BlockSpec(memory_space=pltpu.VMEM)
    return pl.pallas_call(
        exchange_kernel,
        out_shape=(
            jax.ShapeDtypeStruct((rows_here, width), jnp.bfloat16),
            jax.ShapeDtypeStruct((1, block_rows), jnp.float32),
        ),
        in_specs=[vmem] * 6,
        out_specs=(vmem, vmem),
        scratch_shapes=[
            pltpu.VMEM((chains, n - 1, rows_here // chains, width), jnp.bfloat16),
            pltpu.VMEM((chains, n - 1, rows_here // chains, width), jnp.bfloat16),
            pltpu.VMEM((n, rows_here, width), jnp.bfloat16),
            pltpu.VMEM((n, 1, block_rows), jnp.float32),
            pltpu.VMEM((n, 1, block_rows), jnp.float32),
            pltpu.VMEM((n, rows_here, width), jnp.bfloat16),
            pltpu.VMEM((groups,) + vocab_blocks.shape, jnp.bfloat16),
            pltpu.SemaphoreType.DMA((2, chains, 2, n - 1)),
            pltpu.SemaphoreType.DMA((2, n)),
            pltpu.SemaphoreType.DMA((3, groups)),
        ],
        compiler_params=pltpu.CompilerParams(collective_id=0, has_side_effects=True),
    )(attended, low_rank, out_blocks, up_blocks, residual, vocab_blocks)


def on_device(
    hidden,
    norm_gain,
    qkv_weight,
    out_weight,
    adapter_down,
    adapter_up,
    vocab_rows,
    segments,
    request_adapter,
    adapter_slot,
    page_table,
):
    groups = lax.axis_size("group")
    own_group = lax.axis_index("group")
    shards = lax.axis_size("mp")
    own_shard = lax.axis_index("mp")
    rows_here = segments.shape[0]
    model_width = hidden.shape[1]
    slice_width = model_width // shards
    table = page_table.reshape(groups, -1)
    per_group = table.shape[1]
    per_peer = per_group // groups
    page_len = rows_here // per_group
    holders = table // per_group
    position = jnp.arange(per_group, dtype=jnp.int32)
    sort_keys = jnp.where(holders == own_group, position[None, :], per_group + position[None, :])
    ranked = jnp.argsort(sort_keys, axis=1)[:, :per_peer]
    picked = jnp.take_along_axis(table, ranked, axis=1) - own_group * per_group
    outgoing = hidden.reshape(per_group, page_len, model_width)[picked]
    normed_pages = rms_normed(outgoing, norm_gain)
    projected_pages = jnp.einsum(
        "abrd,dc->abrc", normed_pages, qkv_weight, preferred_element_type=jnp.float32
    ).astype(jnp.bfloat16)
    lowered_pages = jnp.einsum(
        "abrd,dc->abrc", normed_pages, adapter_down, preferred_element_type=jnp.float32
    ).astype(jnp.bfloat16)
    kept_pages = lax.dynamic_slice_in_dim(outgoing, own_shard * slice_width, slice_width, 3)
    widths = (kept_pages.shape[3], projected_pages.shape[3], lowered_pages.shape[3])
    packed = lax.all_to_all(
        jnp.concatenate([kept_pages, projected_pages, lowered_pages], axis=3),
        "group", split_axis=0, concat_axis=0, tiled=True,
    )
    own_holders = lax.dynamic_index_in_dim(holders, own_group, 0, keepdims=False)
    onehot = (own_holders[:, None] == jnp.arange(groups, dtype=jnp.int32)[None, :]).astype(
        jnp.int32
    )
    earlier = jnp.sum((jnp.cumsum(onehot, axis=0) - onehot) * onehot, axis=1)
    source_rows = own_holders * per_peer + earlier

    def placed(received):
        gathered_rows = received.reshape((groups * per_peer,) + received.shape[2:])[source_rows]
        return gathered_rows.reshape((rows_here,) + received.shape[3:])

    all_rows = placed(packed)
    residual = all_rows[:, : widths[0]]
    projected = all_rows[:, widths[0] : widths[0] + widths[1]]
    lowered = all_rows[:, widths[0] + widths[1] :]
    vocab_blocks = jnp.transpose(
        vocab_rows.reshape(vocab_rows.shape[0], shards, slice_width), (1, 0, 2)
    )
    heads_here = projected.shape[1] // (2 * FEAT + HD)
    split_heads = jnp.transpose(
        projected.reshape(rows_here, heads_here, 2 * FEAT + HD).astype(jnp.float32), (1, 0, 2)
    )
    query_rows = split_heads[..., :FEAT]
    key_rows = split_heads[..., FEAT : 2 * FEAT]
    value_rows = split_heads[..., 2 * FEAT :]
    phi_query = features(query_rows, FEAT)
    phi_key = features(key_rows, FEAT)
    last_seg = segments[-1]
    member = (segments == last_seg).astype(jnp.float32)
    value_ones = jnp.concatenate(
        [value_rows, jnp.ones(value_rows.shape[:-1] + (1,), value_rows.dtype)], axis=-1
    )
    end_both = jnp.einsum(
        "hcp,hce->hpe", phi_key * member[None, :, None], value_ones, precision=PRECISE
    )
    end_both = jnp.pad(end_both, ((0, 0), (0, 1), (0, 0)))
    end_both = end_both.at[0, -1, 0].set((last_seg + 1).astype(jnp.float32))
    handed = from_behind(end_both.astype(jnp.bfloat16), "group", 1).astype(jnp.float32)
    got_state = handed[:, :-1, :-1]
    got_totals = handed[:, :-1, -1]
    got_tag = handed[0, -1, :1]
    initial = (got_state, got_totals, got_tag[0].astype(jnp.int32) - 1)
    block_len = rows_here
    blocks = rows_here // block_len

    def regroup(values):
        return jnp.transpose(
            values.reshape(values.shape[0], blocks, block_len, values.shape[-1]), (1, 0, 2, 3)
        )

    scan_inputs = (
        regroup(phi_query),
        regroup(phi_key),
        regroup(query_rows),
        regroup(key_rows),
        regroup(value_rows),
        segments.reshape(blocks, block_len),
    )

    def scan_step(state_carry, block_inputs):
        return block_step(state_carry, block_inputs, FEAT)

    _, (mixed_out, state_norm) = lax.scan(scan_step, initial, scan_inputs)
    attended = (
        jnp.transpose(mixed_out, (0, 2, 1, 3))
        .reshape(rows_here, heads_here * HD)
        .astype(jnp.bfloat16)
    )
    state_norms = jnp.transpose(state_norm, (1, 0, 2)).reshape(heads_here, rows_here)
    request_ids = jnp.arange(request_adapter.shape[0], dtype=jnp.int32)
    adapter_of = jnp.sum(
        jnp.where(segments[:, None] == request_ids[None, :], request_adapter[None, :], 0), axis=1
    )
    adapter_ids = jnp.arange(adapter_slot.shape[0], dtype=jnp.int32)
    slot_ids = jnp.sum(
        jnp.where(adapter_of[:, None] == adapter_ids[None, :], adapter_slot[None, :], 0), axis=1
    )
    column_slot = jnp.arange(lowered.shape[1], dtype=jnp.int32) // RANK
    local_slot = slot_ids - own_shard * (lowered.shape[1] // RANK)
    low_rank = jnp.where(
        local_slot[:, None] == column_slot[None, :], lowered, jnp.zeros_like(lowered)
    )
    out_blocks, up_blocks = out_weight, adapter_up
    summed, best = mp_exchange(
        attended, low_rank, out_blocks, up_blocks, residual, vocab_blocks, groups
    )
    max_logits = best[0]
    return (summed, state_norms, max_logits)


def solution(mesh):
    placed = (
        P("group", None),
        P(),
        P(None, "mp"),
        P("mp", None),
        P(None, "mp"),
        P("mp", None),
        P(("group", "mp"), None),
        P("group"),
        P(),
        P(),
        P(),
    )
    return jax.shard_map(
        on_device,
        mesh=mesh,
        in_specs=placed,
        out_specs=(P("group", "mp"), P("mp", "group"), P(("group", "mp"))),
        check_vma=False,
    )
```

```python
import jax
import jax.numpy as jnp
from jax import lax
from jax.sharding import PartitionSpec as P
from jax.experimental import pallas as pl
from jax.experimental.pallas import tpu as pltpu

FEAT = 16
HD = 112
RANK = 16


EPSILON = 1e-05
PRECISE = lax.Precision.HIGHEST


def from_behind(value, axis, by):
    size = lax.axis_size(axis)
    pairs = [(i, i + by) for i in range(size) if 0 <= i + by < size]
    return lax.ppermute(value, axis, pairs)


def rms_normed(values, norm_gain):
    wide = values.astype(jnp.float32)
    meansq = jnp.mean(wide * wide, axis=-1, keepdims=True)
    return (wide * lax.rsqrt(meansq + EPSILON) * norm_gain).astype(jnp.bfloat16)


def features(vectors, feat_width):
    linear_part = vectors / feat_width**0.25
    outer_part = (vectors[..., :, None] * vectors[..., None, :]).reshape(
        vectors.shape[:-1] + (feat_width * feat_width,)
    )
    outer_part = outer_part / (2.0 * feat_width) ** 0.5
    ones_part = jnp.ones(vectors.shape[:-1] + (1,), jnp.float32)
    return jnp.concatenate([ones_part, linear_part, outer_part], axis=-1)


def block_step(state_carry, block_inputs, feat_width):
    states, totals, owner_seg = state_carry
    phi_query, phi_key, query_rows, key_rows, value_rows, seg_ids = block_inputs
    scaling = feat_width ** (-0.5)
    block_len = seg_ids.shape[0]
    position = jnp.arange(block_len, dtype=jnp.int32)
    allowed = (
        (position[:, None] >= position[None, :]) & (seg_ids[:, None] == seg_ids[None, :])
    ).astype(jnp.float32)
    carried = (seg_ids == owner_seg).astype(jnp.float32)[None, :]
    narrow = lambda values: values.astype(jnp.bfloat16)
    scores = jnp.einsum(
        "hcf,hdf->hcd", narrow(query_rows), narrow(key_rows), preferred_element_type=jnp.float32
    ) * scaling
    weights = (1.0 + scores + 0.5 * scores * scores) * allowed[None]
    numerator = jnp.einsum("hcd,hde->hce", weights, value_rows, precision=PRECISE)
    numerator = numerator + carried[..., None] * jnp.einsum(
        "hcp,hpe->hce", phi_query, states, precision=PRECISE
    )
    denominator = jnp.sum(weights, axis=-1) + carried * jnp.einsum(
        "hcp,hp->hc", phi_query, totals, precision=PRECISE
    )
    mixed_out = numerator / denominator[..., None]
    key_scores = jnp.einsum(
        "hcf,hdf->hcd", narrow(key_rows), narrow(key_rows), preferred_element_type=jnp.float32
    ) * scaling
    value_gram = jnp.einsum(
        "hce,hde->hcd", narrow(value_rows), narrow(value_rows), preferred_element_type=jnp.float32
    )
    key_gram = (1.0 + key_scores + 0.5 * key_scores * key_scores) * value_gram
    diagonal = (position[:, None] == position[None, :]).astype(jnp.float32)
    row_terms = jnp.sum(key_gram * (allowed * (2.0 - diagonal))[None], axis=-1)
    local_squares = jnp.einsum("cd,hd->hc", allowed, row_terms, precision=PRECISE)
    along = jnp.sum(
        jnp.einsum("hcp,hpe->hce", phi_key, states, precision=PRECISE) * value_rows, axis=-1
    )
    cross_squares = jnp.einsum("cd,hd->hc", allowed, along, precision=PRECISE)
    state_squares = jnp.sum(states * states, axis=(1, 2))
    squares = carried * (state_squares[:, None] + 2.0 * cross_squares) + local_squares
    counted = carried * totals[:, :1] + jnp.sum(allowed, axis=-1)[None, :]
    state_norm = jnp.sqrt(squares / (counted * (feat_width * value_rows.shape[-1])))
    last_seg = seg_ids[-1]
    member = (seg_ids == last_seg).astype(jnp.float32)
    continues = (owner_seg == last_seg).astype(jnp.float32)
    new_states = continues * states + jnp.einsum(
        "hcp,hce->hpe", phi_key * member[None, :, None], value_rows, precision=PRECISE
    )
    new_totals = continues * totals + jnp.einsum("hcp,c->hp", phi_key, member, precision=PRECISE)
    return ((new_states, new_totals, last_seg), (mixed_out, state_norm))


def best_of(candidates, piece):
    logits = jnp.einsum("rd,vd->rv", candidates, piece, preferred_element_type=jnp.float32)
    return jnp.max(logits, axis=1)


def exchange_kernel(
    att_ref, low_ref, w_ref, u_ref, resid_ref, vocab_in, upd_ref, best_ref,
    land, acc, rows, tops, got, parts, vocab_ref, ring_sems, top_sems, vocab_sems,
):
    n = rows.shape[0]
    quarter = att_ref.shape[0] // 8
    block_rows = best_ref.shape[1]
    me = lax.axis_index("mp")
    grp = lax.axis_index("group")
    peers = [lax.rem(me + k, n) for k in range(1, n)]
    mesh_id = pl.DeviceIdType.MESH
    towards = (lax.rem(me + 1, n), lax.rem(me + n - 1, n))
    chains = [(0, 0), (1, 4), (0, 1), (1, 5), (0, 2), (1, 6), (0, 3), (1, 7)]
    spans = [pl.ds(quarter * piece, quarter) for _, piece in chains]

    width = parts.shape[2]
    for c in range(n):
        cols = slice(c * width, (c + 1) * width)
        value = jnp.dot(att_ref[...], w_ref[:, cols], preferred_element_type=jnp.float32)
        value = value + jnp.dot(low_ref[...], u_ref[:, cols], preferred_element_type=jnp.float32)
        parts[c] = value.astype(parts.dtype)

    groups = vocab_ref.shape[0]
    holders = [lax.rem(grp + k, groups) for k in range(1, groups)]
    barrier = pltpu.get_barrier_semaphore()
    for p in peers:
        pl.semaphore_signal(barrier, inc=1, device_id=(grp, p), device_id_type=mesh_id)
    for h in holders:
        pl.semaphore_signal(barrier, inc=1, device_id=(h, me), device_id_type=mesh_id)
    pl.semaphore_wait(barrier, n - 1 + groups - 1)

    own_vocab = pltpu.make_async_copy(vocab_in, vocab_ref.at[grp], vocab_sems.at[2, 0])
    own_vocab.start()
    vocab_sent = []
    for h in holders:
        copy = pltpu.make_async_remote_copy(
            src_ref=vocab_in,
            dst_ref=vocab_ref.at[grp],
            send_sem=vocab_sems.at[0, h],
            recv_sem=vocab_sems.at[1, grp],
            device_id=(h, me),
            device_id_type=mesh_id,
        )
        copy.start()
        vocab_sent.append(copy)

    def ring_copy(phase, chain, step, src, dst):
        return pltpu.make_async_remote_copy(
            src_ref=src,
            dst_ref=dst,
            send_sem=ring_sems.at[phase, chain, 0, step],
            recv_sem=ring_sems.at[phase, chain, 1, step],
            device_id=(grp, towards[chains[chain][0]]),
            device_id_type=mesh_id,
        )

    def rs_chunk(chain, step):
        way = chains[chain][0]
        return lax.rem(me + (n - 1 - step if way == 0 else 1 + step) + n, n)

    def part(chunk, span):
        return parts[chunk, span].astype(jnp.float32)

    pending = [None] * len(chains)
    for step in range(n - 1):
        for chain in range(len(chains)):
            chunk = rs_chunk(chain, step)
            if step == 0:
                acc[chain, step] = part(chunk, spans[chain]).astype(acc.dtype)
            else:
                pending[chain].wait()
                acc[chain, step] = (
                    land[chain, step - 1].astype(jnp.float32) + part(chunk, spans[chain])
                ).astype(acc.dtype)
            src = acc.at[chain, step]
            pending[chain] = ring_copy(0, chain, step, src, land.at[chain, step])
            pending[chain].start()
    for chain in range(len(chains)):
        pending[chain].wait()
        total = land[chain, n - 2].astype(jnp.float32) + part(me, spans[chain])
        update = total.astype(upd_ref.dtype)
        upd_ref[spans[chain]] = update
        rows[me, spans[chain]] = (
            resid_ref[spans[chain]].astype(jnp.float32) + update.astype(jnp.float32)
        ).astype(rows.dtype)
        view = rows.at[me, spans[chain]]
        pending[chain] = ring_copy(1, chain, 0, view, view)
        pending[chain].start()

    for step in range(1, n - 1):
        for chain in range(len(chains)):
            pending[chain].wait()
            way = chains[chain][0]
            chunk = lax.rem(me + (n - step if way == 0 else step), n)
            view = rows.at[chunk, spans[chain]]
            pending[chain] = ring_copy(1, chain, step, view, view)
            pending[chain].start()
    for chain in range(len(chains)):
        pending[chain].wait()

    own_vocab.wait()
    for copy in vocab_sent:
        copy.wait_send()
    for h in holders:
        pltpu.make_async_remote_copy(
            src_ref=vocab_in,
            dst_ref=vocab_ref.at[h],
            send_sem=vocab_sems.at[0, h],
            recv_sem=vocab_sems.at[1, h],
            device_id=(h, me),
            device_id_type=mesh_id,
        ).wait_recv()

    scores = jnp.zeros((vocab_ref.shape[0] * vocab_ref.shape[2], rows.shape[1]), jnp.float32)
    for j in range(n):
        block = vocab_ref[:, j].reshape(scores.shape[0], rows.shape[2])
        scores = scores + lax.dot_general(
            block, rows[j], (((1,), (1,)), ((), ())),
            preferred_element_type=jnp.float32,
        )
    column_best = jnp.max(scores, axis=0, keepdims=True)
    for p in range(n):
        tops[p] = column_best[:, p * block_rows : (p + 1) * block_rows]

    sent = []
    for p in peers:
        copy = pltpu.make_async_remote_copy(
            src_ref=tops.at[p],
            dst_ref=got.at[me],
            send_sem=top_sems.at[0, p],
            recv_sem=top_sems.at[1, me],
            device_id=(grp, p),
            device_id_type=mesh_id,
        )
        copy.start()
        sent.append(copy)
    for copy in sent:
        copy.wait_send()
    for q in peers:
        pltpu.make_async_remote_copy(
            src_ref=tops.at[q],
            dst_ref=got.at[q],
            send_sem=top_sems.at[0, q],
            recv_sem=top_sems.at[1, q],
            device_id=(grp, q),
            device_id_type=mesh_id,
        ).wait_recv()
    best = tops[me]
    for q in peers:
        best = jnp.maximum(best, got[q])
    best_ref[...] = best


def mp_exchange(attended, low_rank, out_blocks, up_blocks, residual, vocab_blocks, groups):
    n = vocab_blocks.shape[0]
    width = out_blocks.shape[1] // n
    rows_here = attended.shape[0]
    block_rows = rows_here // n
    chains = 8
    vmem = pl.BlockSpec(memory_space=pltpu.VMEM)
    return pl.pallas_call(
        exchange_kernel,
        out_shape=(
            jax.ShapeDtypeStruct((rows_here, width), jnp.bfloat16),
            jax.ShapeDtypeStruct((1, block_rows), jnp.float32),
        ),
        in_specs=[vmem] * 6,
        out_specs=(vmem, vmem),
        scratch_shapes=[
            pltpu.VMEM((chains, n - 1, rows_here // chains, width), jnp.bfloat16),
            pltpu.VMEM((chains, n - 1, rows_here // chains, width), jnp.bfloat16),
            pltpu.VMEM((n, rows_here, width), jnp.bfloat16),
            pltpu.VMEM((n, 1, block_rows), jnp.float32),
            pltpu.VMEM((n, 1, block_rows), jnp.float32),
            pltpu.VMEM((n, rows_here, width), jnp.bfloat16),
            pltpu.VMEM((groups,) + vocab_blocks.shape, jnp.bfloat16),
            pltpu.SemaphoreType.DMA((2, chains, 2, n - 1)),
            pltpu.SemaphoreType.DMA((2, n)),
            pltpu.SemaphoreType.DMA((3, groups)),
        ],
        compiler_params=pltpu.CompilerParams(collective_id=0, has_side_effects=True),
    )(attended, low_rank, out_blocks, up_blocks, residual, vocab_blocks)


def on_device(
    hidden,
    norm_gain,
    qkv_weight,
    out_weight,
    adapter_down,
    adapter_up,
    vocab_rows,
    segments,
    request_adapter,
    adapter_slot,
    page_table,
):
    groups = lax.axis_size("group")
    own_group = lax.axis_index("group")
    shards = lax.axis_size("mp")
    own_shard = lax.axis_index("mp")
    rows_here = segments.shape[0]
    model_width = hidden.shape[1]
    slice_width = model_width // shards
    table = page_table.reshape(groups, -1)
    per_group = table.shape[1]
    per_peer = per_group // groups
    page_len = rows_here // per_group
    holders = table // per_group
    position = jnp.arange(per_group, dtype=jnp.int32)
    sort_keys = jnp.where(holders == own_group, position[None, :], per_group + position[None, :])
    ranked = jnp.argsort(sort_keys, axis=1)[:, :per_peer]
    picked = jnp.take_along_axis(table, ranked, axis=1) - own_group * per_group
    outgoing = hidden.reshape(per_group, page_len, model_width)[picked]
    normed_pages = rms_normed(outgoing, norm_gain)
    projected_pages = jnp.einsum(
        "abrd,dc->abrc", normed_pages, qkv_weight, preferred_element_type=jnp.float32
    ).astype(jnp.bfloat16)
    lowered_pages = jnp.einsum(
        "abrd,dc->abrc", normed_pages, adapter_down, preferred_element_type=jnp.float32
    ).astype(jnp.bfloat16)
    kept_pages = lax.dynamic_slice_in_dim(outgoing, own_shard * slice_width, slice_width, 3)
    widths = (kept_pages.shape[3], projected_pages.shape[3], lowered_pages.shape[3])
    packed = lax.all_to_all(
        jnp.concatenate([kept_pages, projected_pages, lowered_pages], axis=3),
        "group", split_axis=0, concat_axis=0, tiled=True,
    )
    own_holders = lax.dynamic_index_in_dim(holders, own_group, 0, keepdims=False)
    onehot = (own_holders[:, None] == jnp.arange(groups, dtype=jnp.int32)[None, :]).astype(
        jnp.int32
    )
    earlier = jnp.sum((jnp.cumsum(onehot, axis=0) - onehot) * onehot, axis=1)
    source_rows = own_holders * per_peer + earlier

    def placed(received):
        gathered_rows = received.reshape((groups * per_peer,) + received.shape[2:])[source_rows]
        return gathered_rows.reshape((rows_here,) + received.shape[3:])

    all_rows = placed(packed)
    residual = all_rows[:, : widths[0]]
    projected = all_rows[:, widths[0] : widths[0] + widths[1]]
    lowered = all_rows[:, widths[0] + widths[1] :]
    vocab_blocks = jnp.transpose(
        vocab_rows.reshape(vocab_rows.shape[0], shards, slice_width), (1, 0, 2)
    )
    heads_here = projected.shape[1] // (2 * FEAT + HD)
    split_heads = jnp.transpose(
        projected.reshape(rows_here, heads_here, 2 * FEAT + HD).astype(jnp.float32), (1, 0, 2)
    )
    query_rows = split_heads[..., :FEAT]
    key_rows = split_heads[..., FEAT : 2 * FEAT]
    value_rows = split_heads[..., 2 * FEAT :]
    phi_query = features(query_rows, FEAT)
    phi_key = features(key_rows, FEAT)
    last_seg = segments[-1]
    member = (segments == last_seg).astype(jnp.float32)
    value_ones = jnp.concatenate(
        [value_rows, jnp.ones(value_rows.shape[:-1] + (1,), value_rows.dtype)], axis=-1
    )
    end_both = jnp.einsum(
        "hcp,hce->hpe", phi_key * member[None, :, None], value_ones, precision=PRECISE
    )
    end_both = jnp.pad(end_both, ((0, 0), (0, 1), (0, 0)))
    end_both = end_both.at[0, -1, 0].set((last_seg + 1).astype(jnp.float32))
    handed = from_behind(end_both.astype(jnp.bfloat16), "group", 1).astype(jnp.float32)
    got_state = handed[:, :-1, :-1]
    got_totals = handed[:, :-1, -1]
    got_tag = handed[0, -1, :1]
    initial = (got_state, got_totals, got_tag[0].astype(jnp.int32) - 1)
    block_len = rows_here
    blocks = rows_here // block_len

    def regroup(values):
        return jnp.transpose(
            values.reshape(values.shape[0], blocks, block_len, values.shape[-1]), (1, 0, 2, 3)
        )

    scan_inputs = (
        regroup(phi_query),
        regroup(phi_key),
        regroup(query_rows),
        regroup(key_rows),
        regroup(value_rows),
        segments.reshape(blocks, block_len),
    )

    def scan_step(state_carry, block_inputs):
        return block_step(state_carry, block_inputs, FEAT)

    _, (mixed_out, state_norm) = lax.scan(scan_step, initial, scan_inputs)
    attended = (
        jnp.transpose(mixed_out, (0, 2, 1, 3))
        .reshape(rows_here, heads_here * HD)
        .astype(jnp.bfloat16)
    )
    state_norms = jnp.transpose(state_norm, (1, 0, 2)).reshape(heads_here, rows_here)
    request_ids = jnp.arange(request_adapter.shape[0], dtype=jnp.int32)
    adapter_of = jnp.sum(
        jnp.where(segments[:, None] == request_ids[None, :], request_adapter[None, :], 0), axis=1
    )
    adapter_ids = jnp.arange(adapter_slot.shape[0], dtype=jnp.int32)
    slot_ids = jnp.sum(
        jnp.where(adapter_of[:, None] == adapter_ids[None, :], adapter_slot[None, :], 0), axis=1
    )
    column_slot = jnp.arange(lowered.shape[1], dtype=jnp.int32) // RANK
    local_slot = slot_ids - own_shard * (lowered.shape[1] // RANK)
    low_rank = jnp.where(
        local_slot[:, None] == column_slot[None, :], lowered, jnp.zeros_like(lowered)
    )
    out_blocks, up_blocks = out_weight, adapter_up
    summed, best = mp_exchange(
        attended, low_rank, out_blocks, up_blocks, residual, vocab_blocks, groups
    )
    max_logits = best[0]
    return (summed, state_norms, max_logits)


def solution(mesh):
    placed = (
        P("group", None),
        P(),
        P(None, "mp"),
        P("mp", None),
        P(None, "mp"),
        P("mp", None),
        P(("group", "mp"), None),
        P("group"),
        P(),
        P(),
        P(),
    )
    return jax.shard_map(
        on_device,
        mesh=mesh,
        in_specs=placed,
        out_specs=(P("group", "mp"), P("mp", "group"), P(("group", "mp"))),
        check_vma=False,
    )
```

```python
import jax
import jax.numpy as jnp
from jax import lax
from jax.sharding import PartitionSpec as P
from jax.experimental import pallas as pl
from jax.experimental.pallas import tpu as pltpu

FEAT = 16
HD = 112
RANK = 16


EPSILON = 1e-05
PRECISE = lax.Precision.HIGHEST


def from_behind(value, axis, by):
    size = lax.axis_size(axis)
    pairs = [(i, i + by) for i in range(size) if 0 <= i + by < size]
    return lax.ppermute(value, axis, pairs)


def rms_normed(values, norm_gain):
    wide = values.astype(jnp.float32)
    meansq = jnp.mean(wide * wide, axis=-1, keepdims=True)
    return (wide * lax.rsqrt(meansq + EPSILON) * norm_gain).astype(jnp.bfloat16)


def features(vectors, feat_width):
    linear_part = vectors / feat_width**0.25
    outer_part = (vectors[..., :, None] * vectors[..., None, :]).reshape(
        vectors.shape[:-1] + (feat_width * feat_width,)
    )
    outer_part = outer_part / (2.0 * feat_width) ** 0.5
    ones_part = jnp.ones(vectors.shape[:-1] + (1,), jnp.float32)
    return jnp.concatenate([ones_part, linear_part, outer_part], axis=-1)


def block_step(state_carry, block_inputs, feat_width):
    states, totals, owner_seg = state_carry
    phi_query, phi_key, query_rows, key_rows, value_rows, seg_ids = block_inputs
    scaling = feat_width ** (-0.5)
    block_len = seg_ids.shape[0]
    position = jnp.arange(block_len, dtype=jnp.int32)
    allowed = (
        (position[:, None] >= position[None, :]) & (seg_ids[:, None] == seg_ids[None, :])
    ).astype(jnp.float32)
    carried = (seg_ids == owner_seg).astype(jnp.float32)[None, :]
    scores = jnp.einsum("hcf,hdf->hcd", query_rows, key_rows, precision=PRECISE) * scaling
    weights = (1.0 + scores + 0.5 * scores * scores) * allowed[None]
    numerator = jnp.einsum("hcd,hde->hce", weights, value_rows, precision=PRECISE)
    numerator = numerator + carried[..., None] * jnp.einsum(
        "hcp,hpe->hce", phi_query, states, precision=PRECISE
    )
    denominator = jnp.sum(weights, axis=-1) + carried * jnp.einsum(
        "hcp,hp->hc", phi_query, totals, precision=PRECISE
    )
    mixed_out = numerator / denominator[..., None]
    key_scores = jnp.einsum("hcf,hdf->hcd", key_rows, key_rows, precision=PRECISE) * scaling
    value_gram = jnp.einsum("hce,hde->hcd", value_rows, value_rows, precision=PRECISE)
    key_gram = (1.0 + key_scores + 0.5 * key_scores * key_scores) * value_gram
    diagonal = (position[:, None] == position[None, :]).astype(jnp.float32)
    row_terms = jnp.sum(key_gram * (allowed * (2.0 - diagonal))[None], axis=-1)
    local_squares = jnp.einsum("cd,hd->hc", allowed, row_terms, precision=PRECISE)
    along = jnp.sum(
        jnp.einsum("hcp,hpe->hce", phi_key, states, precision=PRECISE) * value_rows, axis=-1
    )
    cross_squares = jnp.einsum("cd,hd->hc", allowed, along, precision=PRECISE)
    state_squares = jnp.sum(states * states, axis=(1, 2))
    squares = carried * (state_squares[:, None] + 2.0 * cross_squares) + local_squares
    counted = carried * totals[:, :1] + jnp.sum(allowed, axis=-1)[None, :]
    state_norm = jnp.sqrt(squares / (counted * (feat_width * value_rows.shape[-1])))
    last_seg = seg_ids[-1]
    member = (seg_ids == last_seg).astype(jnp.float32)
    continues = (owner_seg == last_seg).astype(jnp.float32)
    new_states = continues * states + jnp.einsum(
        "hcp,hce->hpe", phi_key * member[None, :, None], value_rows, precision=PRECISE
    )
    new_totals = continues * totals + jnp.einsum("hcp,c->hp", phi_key, member, precision=PRECISE)
    return ((new_states, new_totals, last_seg), (mixed_out, state_norm))


def best_of(candidates, piece):
    logits = jnp.einsum("rd,vd->rv", candidates, piece, preferred_element_type=jnp.float32)
    return jnp.max(logits, axis=1)


def exchange_kernel(
    att_ref, low_ref, w_ref, u_ref, resid_ref, vocab_in, upd_ref, best_ref,
    land, acc, rows, tops, got, parts, vocab_ref, ring_sems, top_sems, vocab_sems,
):
    n = rows.shape[0]
    quarter = att_ref.shape[0] // 8
    block_rows = best_ref.shape[1]
    me = lax.axis_index("mp")
    grp = lax.axis_index("group")
    peers = [lax.rem(me + k, n) for k in range(1, n)]
    mesh_id = pl.DeviceIdType.MESH
    towards = (lax.rem(me + 1, n), lax.rem(me + n - 1, n))
    chains = [(0, 0), (1, 4), (0, 1), (1, 5), (0, 2), (1, 6), (0, 3), (1, 7)]
    spans = [pl.ds(quarter * piece, quarter) for _, piece in chains]

    width = parts.shape[2]
    for c in range(n):
        cols = slice(c * width, (c + 1) * width)
        value = jnp.dot(att_ref[...], w_ref[:, cols], preferred_element_type=jnp.float32)
        value = value + jnp.dot(low_ref[...], u_ref[:, cols], preferred_element_type=jnp.float32)
        parts[c] = value.astype(parts.dtype)

    groups = vocab_ref.shape[0]
    holders = [lax.rem(grp + k, groups) for k in range(1, groups)]
    barrier = pltpu.get_barrier_semaphore()
    for p in peers:
        pl.semaphore_signal(barrier, inc=1, device_id=(grp, p), device_id_type=mesh_id)
    for h in holders:
        pl.semaphore_signal(barrier, inc=1, device_id=(h, me), device_id_type=mesh_id)
    pl.semaphore_wait(barrier, n - 1 + groups - 1)

    own_vocab = pltpu.make_async_copy(vocab_in, vocab_ref.at[grp], vocab_sems.at[2, 0])
    own_vocab.start()
    vocab_sent = []
    for h in holders:
        copy = pltpu.make_async_remote_copy(
            src_ref=vocab_in,
            dst_ref=vocab_ref.at[grp],
            send_sem=vocab_sems.at[0, h],
            recv_sem=vocab_sems.at[1, grp],
            device_id=(h, me),
            device_id_type=mesh_id,
        )
        copy.start()
        vocab_sent.append(copy)

    def ring_copy(phase, chain, step, src, dst):
        return pltpu.make_async_remote_copy(
            src_ref=src,
            dst_ref=dst,
            send_sem=ring_sems.at[phase, chain, 0, step],
            recv_sem=ring_sems.at[phase, chain, 1, step],
            device_id=(grp, towards[chains[chain][0]]),
            device_id_type=mesh_id,
        )

    def rs_chunk(chain, step):
        way = chains[chain][0]
        return lax.rem(me + (n - 1 - step if way == 0 else 1 + step) + n, n)

    def part(chunk, span):
        return parts[chunk, span].astype(jnp.float32)

    pending = [None] * len(chains)
    for step in range(n - 1):
        for chain in range(len(chains)):
            chunk = rs_chunk(chain, step)
            if step == 0:
                acc[chain, step] = part(chunk, spans[chain]).astype(acc.dtype)
            else:
                pending[chain].wait()
                acc[chain, step] = (
                    land[chain, step - 1].astype(jnp.float32) + part(chunk, spans[chain])
                ).astype(acc.dtype)
            src = acc.at[chain, step]
            pending[chain] = ring_copy(0, chain, step, src, land.at[chain, step])
            pending[chain].start()
    for chain in range(len(chains)):
        pending[chain].wait()
        total = land[chain, n - 2].astype(jnp.float32) + part(me, spans[chain])
        update = total.astype(upd_ref.dtype)
        upd_ref[spans[chain]] = update
        rows[me, spans[chain]] = (
            resid_ref[spans[chain]].astype(jnp.float32) + update.astype(jnp.float32)
        ).astype(rows.dtype)
        view = rows.at[me, spans[chain]]
        pending[chain] = ring_copy(1, chain, 0, view, view)
        pending[chain].start()

    for step in range(1, n - 1):
        for chain in range(len(chains)):
            pending[chain].wait()
            way = chains[chain][0]
            chunk = lax.rem(me + (n - step if way == 0 else step), n)
            view = rows.at[chunk, spans[chain]]
            pending[chain] = ring_copy(1, chain, step, view, view)
            pending[chain].start()
    for chain in range(len(chains)):
        pending[chain].wait()

    own_vocab.wait()
    for copy in vocab_sent:
        copy.wait_send()
    for h in holders:
        pltpu.make_async_remote_copy(
            src_ref=vocab_in,
            dst_ref=vocab_ref.at[h],
            send_sem=vocab_sems.at[0, h],
            recv_sem=vocab_sems.at[1, h],
            device_id=(h, me),
            device_id_type=mesh_id,
        ).wait_recv()

    scores = jnp.zeros((vocab_ref.shape[0] * vocab_ref.shape[1], rows.shape[1]), jnp.float32)
    for j in range(n):
        cut = slice(j * rows.shape[2], (j + 1) * rows.shape[2])
        block = vocab_ref[:, :, cut].reshape(scores.shape[0], rows.shape[2])
        scores = scores + lax.dot_general(
            block, rows[j], (((1,), (1,)), ((), ())),
            preferred_element_type=jnp.float32,
        )
    column_best = jnp.max(scores, axis=0, keepdims=True)
    for p in range(n):
        tops[p] = column_best[:, p * block_rows : (p + 1) * block_rows]

    sent = []
    for p in peers:
        copy = pltpu.make_async_remote_copy(
            src_ref=tops.at[p],
            dst_ref=got.at[me],
            send_sem=top_sems.at[0, p],
            recv_sem=top_sems.at[1, me],
            device_id=(grp, p),
            device_id_type=mesh_id,
        )
        copy.start()
        sent.append(copy)
    for copy in sent:
        copy.wait_send()
    for q in peers:
        pltpu.make_async_remote_copy(
            src_ref=tops.at[q],
            dst_ref=got.at[q],
            send_sem=top_sems.at[0, q],
            recv_sem=top_sems.at[1, q],
            device_id=(grp, q),
            device_id_type=mesh_id,
        ).wait_recv()
    best = tops[me]
    for q in peers:
        best = jnp.maximum(best, got[q])
    best_ref[...] = best


def mp_exchange(attended, low_rank, out_blocks, up_blocks, residual, vocab_blocks, groups):
    width = residual.shape[1]
    n = out_blocks.shape[1] // width
    rows_here = attended.shape[0]
    block_rows = rows_here // n
    chains = 8
    vmem = pl.BlockSpec(memory_space=pltpu.VMEM)
    return pl.pallas_call(
        exchange_kernel,
        out_shape=(
            jax.ShapeDtypeStruct((rows_here, width), jnp.bfloat16),
            jax.ShapeDtypeStruct((1, block_rows), jnp.float32),
        ),
        in_specs=[vmem] * 6,
        out_specs=(vmem, vmem),
        scratch_shapes=[
            pltpu.VMEM((chains, n - 1, rows_here // chains, width), jnp.bfloat16),
            pltpu.VMEM((chains, n - 1, rows_here // chains, width), jnp.bfloat16),
            pltpu.VMEM((n, rows_here, width), jnp.bfloat16),
            pltpu.VMEM((n, 1, block_rows), jnp.float32),
            pltpu.VMEM((n, 1, block_rows), jnp.float32),
            pltpu.VMEM((n, rows_here, width), jnp.bfloat16),
            pltpu.VMEM((groups,) + vocab_blocks.shape, jnp.bfloat16),
            pltpu.SemaphoreType.DMA((2, chains, 2, n - 1)),
            pltpu.SemaphoreType.DMA((2, n)),
            pltpu.SemaphoreType.DMA((3, groups)),
        ],
        compiler_params=pltpu.CompilerParams(collective_id=0, has_side_effects=True),
    )(attended, low_rank, out_blocks, up_blocks, residual, vocab_blocks)


def on_device(
    hidden,
    norm_gain,
    qkv_weight,
    out_weight,
    adapter_down,
    adapter_up,
    vocab_rows,
    segments,
    request_adapter,
    adapter_slot,
    page_table,
):
    groups = lax.axis_size("group")
    own_group = lax.axis_index("group")
    shards = lax.axis_size("mp")
    own_shard = lax.axis_index("mp")
    rows_here = segments.shape[0]
    model_width = hidden.shape[1]
    slice_width = model_width // shards
    table = page_table.reshape(groups, -1)
    per_group = table.shape[1]
    per_peer = per_group // groups
    page_len = rows_here // per_group
    holders = table // per_group
    position = jnp.arange(per_group, dtype=jnp.int32)
    sort_keys = jnp.where(holders == own_group, position[None, :], per_group + position[None, :])
    ranked = jnp.argsort(sort_keys, axis=1)[:, :per_peer]
    picked = jnp.take_along_axis(table, ranked, axis=1) - own_group * per_group
    outgoing = hidden.reshape(per_group, page_len, model_width)[picked]
    normed_pages = rms_normed(outgoing, norm_gain)
    projected_pages = jnp.einsum(
        "abrd,dc->abrc", normed_pages, qkv_weight, preferred_element_type=jnp.float32
    ).astype(jnp.bfloat16)
    lowered_pages = jnp.einsum(
        "abrd,dc->abrc", normed_pages, adapter_down, preferred_element_type=jnp.float32
    ).astype(jnp.bfloat16)
    kept_pages = lax.dynamic_slice_in_dim(outgoing, own_shard * slice_width, slice_width, 3)
    widths = (kept_pages.shape[3], projected_pages.shape[3], lowered_pages.shape[3])
    packed = lax.all_to_all(
        jnp.concatenate([kept_pages, projected_pages, lowered_pages], axis=3),
        "group", split_axis=0, concat_axis=0, tiled=True,
    )
    own_holders = lax.dynamic_index_in_dim(holders, own_group, 0, keepdims=False)
    onehot = (own_holders[:, None] == jnp.arange(groups, dtype=jnp.int32)[None, :]).astype(
        jnp.int32
    )
    earlier = jnp.sum((jnp.cumsum(onehot, axis=0) - onehot) * onehot, axis=1)
    source_rows = own_holders * per_peer + earlier

    def placed(received):
        gathered_rows = received.reshape((groups * per_peer,) + received.shape[2:])[source_rows]
        return gathered_rows.reshape((rows_here,) + received.shape[3:])

    all_rows = placed(packed)
    residual = all_rows[:, : widths[0]]
    projected = all_rows[:, widths[0] : widths[0] + widths[1]]
    lowered = all_rows[:, widths[0] + widths[1] :]
    vocab_blocks = vocab_rows
    heads_here = projected.shape[1] // (2 * FEAT + HD)
    split_heads = jnp.transpose(
        projected.reshape(rows_here, heads_here, 2 * FEAT + HD).astype(jnp.float32), (1, 0, 2)
    )
    query_rows = split_heads[..., :FEAT]
    key_rows = split_heads[..., FEAT : 2 * FEAT]
    value_rows = split_heads[..., 2 * FEAT :]
    phi_query = features(query_rows, FEAT)
    phi_key = features(key_rows, FEAT)
    last_seg = segments[-1]
    member = (segments == last_seg).astype(jnp.float32)
    value_ones = jnp.concatenate(
        [value_rows, jnp.ones(value_rows.shape[:-1] + (1,), value_rows.dtype)], axis=-1
    )
    end_both = jnp.einsum(
        "hcp,hce->hpe", phi_key * member[None, :, None], value_ones, precision=PRECISE
    )
    end_both = jnp.pad(end_both, ((0, 0), (0, 1), (0, 0)))
    end_both = end_both.at[0, -1, 0].set((last_seg + 1).astype(jnp.float32))
    handed = from_behind(end_both.astype(jnp.bfloat16), "group", 1).astype(jnp.float32)
    got_state = handed[:, :-1, :-1]
    got_totals = handed[:, :-1, -1]
    got_tag = handed[0, -1, :1]
    initial = (got_state, got_totals, got_tag[0].astype(jnp.int32) - 1)
    block_len = rows_here
    blocks = rows_here // block_len

    def regroup(values):
        return jnp.transpose(
            values.reshape(values.shape[0], blocks, block_len, values.shape[-1]), (1, 0, 2, 3)
        )

    scan_inputs = (
        regroup(phi_query),
        regroup(phi_key),
        regroup(query_rows),
        regroup(key_rows),
        regroup(value_rows),
        segments.reshape(blocks, block_len),
    )

    def scan_step(state_carry, block_inputs):
        return block_step(state_carry, block_inputs, FEAT)

    _, (mixed_out, state_norm) = lax.scan(scan_step, initial, scan_inputs)
    attended = (
        jnp.transpose(mixed_out, (0, 2, 1, 3))
        .reshape(rows_here, heads_here * HD)
        .astype(jnp.bfloat16)
    )
    state_norms = jnp.transpose(state_norm, (1, 0, 2)).reshape(heads_here, rows_here)
    request_ids = jnp.arange(request_adapter.shape[0], dtype=jnp.int32)
    adapter_of = jnp.sum(
        jnp.where(segments[:, None] == request_ids[None, :], request_adapter[None, :], 0), axis=1
    )
    adapter_ids = jnp.arange(adapter_slot.shape[0], dtype=jnp.int32)
    slot_ids = jnp.sum(
        jnp.where(adapter_of[:, None] == adapter_ids[None, :], adapter_slot[None, :], 0), axis=1
    )
    column_slot = jnp.arange(lowered.shape[1], dtype=jnp.int32) // RANK
    local_slot = slot_ids - own_shard * (lowered.shape[1] // RANK)
    low_rank = jnp.where(
        local_slot[:, None] == column_slot[None, :], lowered, jnp.zeros_like(lowered)
    )
    out_blocks, up_blocks = out_weight, adapter_up
    summed, best = mp_exchange(
        attended, low_rank, out_blocks, up_blocks, residual, vocab_blocks, groups
    )
    max_logits = best[0]
    return (summed, state_norms, max_logits)


def solution(mesh):
    placed = (
        P("group", None),
        P(),
        P(None, "mp"),
        P("mp", None),
        P(None, "mp"),
        P("mp", None),
        P(("group", "mp"), None),
        P("group"),
        P(),
        P(),
        P(),
    )
    return jax.shard_map(
        on_device,
        mesh=mesh,
        in_specs=placed,
        out_specs=(P("group", "mp"), P("mp", "group"), P(("group", "mp"))),
        check_vma=False,
    )
```

```python
import jax
import jax.numpy as jnp
from jax import lax
from jax.sharding import PartitionSpec as P
from jax.experimental import pallas as pl
from jax.experimental.pallas import tpu as pltpu

FEAT = 16
HD = 112
RANK = 16


EPSILON = 1e-05
PRECISE = lax.Precision.HIGHEST


def from_behind(value, axis, by):
    size = lax.axis_size(axis)
    pairs = [(i, i + by) for i in range(size) if 0 <= i + by < size]
    return lax.ppermute(value, axis, pairs)


def rms_normed(values, norm_gain):
    wide = values.astype(jnp.float32)
    meansq = jnp.mean(wide * wide, axis=-1, keepdims=True)
    return (wide * lax.rsqrt(meansq + EPSILON) * norm_gain).astype(jnp.bfloat16)


def features(vectors, feat_width):
    linear_part = vectors / feat_width**0.25
    outer_part = (vectors[..., :, None] * vectors[..., None, :]).reshape(
        vectors.shape[:-1] + (feat_width * feat_width,)
    )
    outer_part = outer_part / (2.0 * feat_width) ** 0.5
    ones_part = jnp.ones(vectors.shape[:-1] + (1,), jnp.float32)
    return jnp.concatenate([ones_part, linear_part, outer_part], axis=-1)


def block_step(state_carry, block_inputs, feat_width):
    states, totals, owner_seg = state_carry
    phi_query, phi_key, query_rows, key_rows, value_rows, seg_ids = block_inputs
    scaling = feat_width ** (-0.5)
    block_len = seg_ids.shape[0]
    position = jnp.arange(block_len, dtype=jnp.int32)
    allowed = (
        (position[:, None] >= position[None, :]) & (seg_ids[:, None] == seg_ids[None, :])
    ).astype(jnp.float32)
    carried = (seg_ids == owner_seg).astype(jnp.float32)[None, :]
    scores = jnp.einsum("hcf,hdf->hcd", query_rows, key_rows, precision=PRECISE) * scaling
    weights = (1.0 + scores + 0.5 * scores * scores) * allowed[None]
    numerator = jnp.einsum("hcd,hde->hce", weights, value_rows, precision=PRECISE)
    numerator = numerator + carried[..., None] * jnp.einsum(
        "hcp,hpe->hce", phi_query, states, precision=PRECISE
    )
    denominator = jnp.sum(weights, axis=-1) + carried * jnp.einsum(
        "hcp,hp->hc", phi_query, totals, precision=PRECISE
    )
    mixed_out = numerator / denominator[..., None]
    key_scores = jnp.einsum("hcf,hdf->hcd", key_rows, key_rows, precision=PRECISE) * scaling
    value_gram = jnp.einsum("hce,hde->hcd", value_rows, value_rows, precision=PRECISE)
    key_gram = (1.0 + key_scores + 0.5 * key_scores * key_scores) * value_gram
    diagonal = (position[:, None] == position[None, :]).astype(jnp.float32)
    row_terms = jnp.sum(key_gram * (allowed * (2.0 - diagonal))[None], axis=-1)
    local_squares = jnp.einsum("cd,hd->hc", allowed, row_terms, precision=PRECISE)
    along = jnp.sum(
        jnp.einsum("hcp,hpe->hce", phi_key, states, precision=PRECISE) * value_rows, axis=-1
    )
    cross_squares = jnp.einsum("cd,hd->hc", allowed, along, precision=PRECISE)
    state_squares = jnp.sum(states * states, axis=(1, 2))
    squares = carried * (state_squares[:, None] + 2.0 * cross_squares) + local_squares
    counted = carried * totals[:, :1] + jnp.sum(allowed, axis=-1)[None, :]
    state_norm = jnp.sqrt(squares / (counted * (feat_width * value_rows.shape[-1])))
    last_seg = seg_ids[-1]
    member = (seg_ids == last_seg).astype(jnp.float32)
    continues = (owner_seg == last_seg).astype(jnp.float32)
    new_states = continues * states + jnp.einsum(
        "hcp,hce->hpe", phi_key * member[None, :, None], value_rows, precision=PRECISE
    )
    new_totals = continues * totals + jnp.einsum("hcp,c->hp", phi_key, member, precision=PRECISE)
    return ((new_states, new_totals, last_seg), (mixed_out, state_norm))


def best_of(candidates, piece):
    logits = jnp.einsum("rd,vd->rv", candidates, piece, preferred_element_type=jnp.float32)
    return jnp.max(logits, axis=1)


def exchange_kernel(
    att_ref, low_ref, w_ref, u_ref, resid_ref, vocab_in, upd_ref, best_ref,
    land, acc, rows, tops, got, parts, vocab_ref, ring_sems, top_sems, vocab_sems,
):
    n = rows.shape[0]
    quarter = att_ref.shape[0] // 8
    block_rows = best_ref.shape[1]
    me = lax.axis_index("mp")
    grp = lax.axis_index("group")
    peers = [lax.rem(me + k, n) for k in range(1, n)]
    mesh_id = pl.DeviceIdType.MESH
    towards = (lax.rem(me + 1, n), lax.rem(me + n - 1, n))
    chains = [(0, 0), (1, 4), (0, 1), (1, 5), (0, 2), (1, 6), (0, 3), (1, 7)]
    spans = [pl.ds(quarter * piece, quarter) for _, piece in chains]

    width = parts.shape[2]
    for c in range(n):
        cols = slice(c * width, (c + 1) * width)
        value = jnp.dot(att_ref[...], w_ref[:, cols], preferred_element_type=jnp.float32)
        value = value + jnp.dot(low_ref[...], u_ref[:, cols], preferred_element_type=jnp.float32)
        parts[c] = value.astype(parts.dtype)

    groups = vocab_ref.shape[0]
    holders = [lax.rem(grp + k, groups) for k in range(1, groups)]
    barrier = pltpu.get_barrier_semaphore()
    for p in peers:
        pl.semaphore_signal(barrier, inc=1, device_id=(grp, p), device_id_type=mesh_id)
    for h in holders:
        pl.semaphore_signal(barrier, inc=1, device_id=(h, me), device_id_type=mesh_id)
    pl.semaphore_wait(barrier, n - 1 + groups - 1)

    own_vocab = pltpu.make_async_copy(vocab_in, vocab_ref.at[grp], vocab_sems.at[2, 0])
    own_vocab.start()
    vocab_sent = []
    for h in holders:
        copy = pltpu.make_async_remote_copy(
            src_ref=vocab_in,
            dst_ref=vocab_ref.at[grp],
            send_sem=vocab_sems.at[0, h],
            recv_sem=vocab_sems.at[1, grp],
            device_id=(h, me),
            device_id_type=mesh_id,
        )
        copy.start()
        vocab_sent.append(copy)

    def ring_copy(phase, chain, step, src, dst):
        return pltpu.make_async_remote_copy(
            src_ref=src,
            dst_ref=dst,
            send_sem=ring_sems.at[phase, chain, 0, step],
            recv_sem=ring_sems.at[phase, chain, 1, step],
            device_id=(grp, towards[chains[chain][0]]),
            device_id_type=mesh_id,
        )

    def rs_chunk(chain, step):
        way = chains[chain][0]
        return lax.rem(me + (n - 1 - step if way == 0 else 1 + step) + n, n)

    def part(chunk, span):
        return parts[chunk, span].astype(jnp.float32)

    pending = [None] * len(chains)
    issued = []
    for step in range(n - 1):
        for chain in range(len(chains)):
            chunk = rs_chunk(chain, step)
            if step == 0:
                acc[chain, step] = part(chunk, spans[chain]).astype(acc.dtype)
            else:
                pending[chain].wait_recv()
                acc[chain, step] = (
                    land[chain, step - 1].astype(jnp.float32) + part(chunk, spans[chain])
                ).astype(acc.dtype)
            src = acc.at[chain, step]
            pending[chain] = ring_copy(0, chain, step, src, land.at[chain, step])
            pending[chain].start()
            issued.append(pending[chain])
    for chain in range(len(chains)):
        pending[chain].wait_recv()
        total = land[chain, n - 2].astype(jnp.float32) + part(me, spans[chain])
        update = total.astype(upd_ref.dtype)
        upd_ref[spans[chain]] = update
        rows[me, spans[chain]] = (
            resid_ref[spans[chain]].astype(jnp.float32) + update.astype(jnp.float32)
        ).astype(rows.dtype)
        view = rows.at[me, spans[chain]]
        pending[chain] = ring_copy(1, chain, 0, view, view)
        pending[chain].start()
        issued.append(pending[chain])

    for step in range(1, n - 1):
        for chain in range(len(chains)):
            pending[chain].wait_recv()
            way = chains[chain][0]
            chunk = lax.rem(me + (n - step if way == 0 else step), n)
            view = rows.at[chunk, spans[chain]]
            pending[chain] = ring_copy(1, chain, step, view, view)
            pending[chain].start()
            issued.append(pending[chain])
    for chain in range(len(chains)):
        pending[chain].wait_recv()
    for copy in issued:
        copy.wait_send()

    own_vocab.wait()
    for copy in vocab_sent:
        copy.wait_send()
    for h in holders:
        pltpu.make_async_remote_copy(
            src_ref=vocab_in,
            dst_ref=vocab_ref.at[h],
            send_sem=vocab_sems.at[0, h],
            recv_sem=vocab_sems.at[1, h],
            device_id=(h, me),
            device_id_type=mesh_id,
        ).wait_recv()

    scores = jnp.zeros((vocab_ref.shape[0] * vocab_ref.shape[2], rows.shape[1]), jnp.float32)
    for j in range(n):
        block = vocab_ref[:, j].reshape(scores.shape[0], rows.shape[2])
        scores = scores + lax.dot_general(
            block, rows[j], (((1,), (1,)), ((), ())),
            preferred_element_type=jnp.float32,
        )
    column_best = jnp.max(scores, axis=0, keepdims=True)
    for p in range(n):
        tops[p] = column_best[:, p * block_rows : (p + 1) * block_rows]

    sent = []
    for p in peers:
        copy = pltpu.make_async_remote_copy(
            src_ref=tops.at[p],
            dst_ref=got.at[me],
            send_sem=top_sems.at[0, p],
            recv_sem=top_sems.at[1, me],
            device_id=(grp, p),
            device_id_type=mesh_id,
        )
        copy.start()
        sent.append(copy)
    for copy in sent:
        copy.wait_send()
    for q in peers:
        pltpu.make_async_remote_copy(
            src_ref=tops.at[q],
            dst_ref=got.at[q],
            send_sem=top_sems.at[0, q],
            recv_sem=top_sems.at[1, q],
            device_id=(grp, q),
            device_id_type=mesh_id,
        ).wait_recv()
    best = tops[me]
    for q in peers:
        best = jnp.maximum(best, got[q])
    best_ref[...] = best


def mp_exchange(attended, low_rank, out_blocks, up_blocks, residual, vocab_blocks, groups):
    n = vocab_blocks.shape[0]
    width = out_blocks.shape[1] // n
    rows_here = attended.shape[0]
    block_rows = rows_here // n
    chains = 8
    vmem = pl.BlockSpec(memory_space=pltpu.VMEM)
    return pl.pallas_call(
        exchange_kernel,
        out_shape=(
            jax.ShapeDtypeStruct((rows_here, width), jnp.bfloat16),
            jax.ShapeDtypeStruct((1, block_rows), jnp.float32),
        ),
        in_specs=[vmem] * 6,
        out_specs=(vmem, vmem),
        scratch_shapes=[
            pltpu.VMEM((chains, n - 1, rows_here // chains, width), jnp.bfloat16),
            pltpu.VMEM((chains, n - 1, rows_here // chains, width), jnp.bfloat16),
            pltpu.VMEM((n, rows_here, width), jnp.bfloat16),
            pltpu.VMEM((n, 1, block_rows), jnp.float32),
            pltpu.VMEM((n, 1, block_rows), jnp.float32),
            pltpu.VMEM((n, rows_here, width), jnp.bfloat16),
            pltpu.VMEM((groups,) + vocab_blocks.shape, jnp.bfloat16),
            pltpu.SemaphoreType.DMA((2, chains, 2, n - 1)),
            pltpu.SemaphoreType.DMA((2, n)),
            pltpu.SemaphoreType.DMA((3, groups)),
        ],
        compiler_params=pltpu.CompilerParams(collective_id=0, has_side_effects=True),
    )(attended, low_rank, out_blocks, up_blocks, residual, vocab_blocks)


def on_device(
    hidden,
    norm_gain,
    qkv_weight,
    out_weight,
    adapter_down,
    adapter_up,
    vocab_rows,
    segments,
    request_adapter,
    adapter_slot,
    page_table,
):
    groups = lax.axis_size("group")
    own_group = lax.axis_index("group")
    shards = lax.axis_size("mp")
    own_shard = lax.axis_index("mp")
    rows_here = segments.shape[0]
    model_width = hidden.shape[1]
    slice_width = model_width // shards
    table = page_table.reshape(groups, -1)
    per_group = table.shape[1]
    per_peer = per_group // groups
    page_len = rows_here // per_group
    holders = table // per_group
    position = jnp.arange(per_group, dtype=jnp.int32)
    sort_keys = jnp.where(holders == own_group, position[None, :], per_group + position[None, :])
    ranked = jnp.argsort(sort_keys, axis=1)[:, :per_peer]
    picked = jnp.take_along_axis(table, ranked, axis=1) - own_group * per_group
    outgoing = hidden.reshape(per_group, page_len, model_width)[picked]
    normed_pages = rms_normed(outgoing, norm_gain)
    projected_pages = jnp.einsum(
        "abrd,dc->abrc", normed_pages, qkv_weight, preferred_element_type=jnp.float32
    ).astype(jnp.bfloat16)
    lowered_pages = jnp.einsum(
        "abrd,dc->abrc", normed_pages, adapter_down, preferred_element_type=jnp.float32
    ).astype(jnp.bfloat16)
    kept_pages = lax.dynamic_slice_in_dim(outgoing, own_shard * slice_width, slice_width, 3)
    widths = (kept_pages.shape[3], projected_pages.shape[3], lowered_pages.shape[3])
    packed = lax.all_to_all(
        jnp.concatenate([kept_pages, projected_pages, lowered_pages], axis=3),
        "group", split_axis=0, concat_axis=0, tiled=True,
    )
    own_holders = lax.dynamic_index_in_dim(holders, own_group, 0, keepdims=False)
    onehot = (own_holders[:, None] == jnp.arange(groups, dtype=jnp.int32)[None, :]).astype(
        jnp.int32
    )
    earlier = jnp.sum((jnp.cumsum(onehot, axis=0) - onehot) * onehot, axis=1)
    source_rows = own_holders * per_peer + earlier

    def placed(received):
        gathered_rows = received.reshape((groups * per_peer,) + received.shape[2:])[source_rows]
        return gathered_rows.reshape((rows_here,) + received.shape[3:])

    all_rows = placed(packed)
    residual = all_rows[:, : widths[0]]
    projected = all_rows[:, widths[0] : widths[0] + widths[1]]
    lowered = all_rows[:, widths[0] + widths[1] :]
    vocab_blocks = jnp.transpose(
        vocab_rows.reshape(vocab_rows.shape[0], shards, slice_width), (1, 0, 2)
    )
    heads_here = projected.shape[1] // (2 * FEAT + HD)
    split_heads = jnp.transpose(
        projected.reshape(rows_here, heads_here, 2 * FEAT + HD).astype(jnp.float32), (1, 0, 2)
    )
    query_rows = split_heads[..., :FEAT]
    key_rows = split_heads[..., FEAT : 2 * FEAT]
    value_rows = split_heads[..., 2 * FEAT :]
    phi_query = features(query_rows, FEAT)
    phi_key = features(key_rows, FEAT)
    last_seg = segments[-1]
    member = (segments == last_seg).astype(jnp.float32)
    value_ones = jnp.concatenate(
        [value_rows, jnp.ones(value_rows.shape[:-1] + (1,), value_rows.dtype)], axis=-1
    )
    end_both = jnp.einsum(
        "hcp,hce->hpe", phi_key * member[None, :, None], value_ones, precision=PRECISE
    )
    end_both = jnp.pad(end_both, ((0, 0), (0, 1), (0, 0)))
    end_both = end_both.at[0, -1, 0].set((last_seg + 1).astype(jnp.float32))
    handed = from_behind(end_both.astype(jnp.bfloat16), "group", 1).astype(jnp.float32)
    got_state = handed[:, :-1, :-1]
    got_totals = handed[:, :-1, -1]
    got_tag = handed[0, -1, :1]
    initial = (got_state, got_totals, got_tag[0].astype(jnp.int32) - 1)
    block_len = rows_here
    blocks = rows_here // block_len

    def regroup(values):
        return jnp.transpose(
            values.reshape(values.shape[0], blocks, block_len, values.shape[-1]), (1, 0, 2, 3)
        )

    scan_inputs = (
        regroup(phi_query),
        regroup(phi_key),
        regroup(query_rows),
        regroup(key_rows),
        regroup(value_rows),
        segments.reshape(blocks, block_len),
    )

    def scan_step(state_carry, block_inputs):
        return block_step(state_carry, block_inputs, FEAT)

    _, (mixed_out, state_norm) = lax.scan(scan_step, initial, scan_inputs)
    attended = (
        jnp.transpose(mixed_out, (0, 2, 1, 3))
        .reshape(rows_here, heads_here * HD)
        .astype(jnp.bfloat16)
    )
    state_norms = jnp.transpose(state_norm, (1, 0, 2)).reshape(heads_here, rows_here)
    request_ids = jnp.arange(request_adapter.shape[0], dtype=jnp.int32)
    adapter_of = jnp.sum(
        jnp.where(segments[:, None] == request_ids[None, :], request_adapter[None, :], 0), axis=1
    )
    adapter_ids = jnp.arange(adapter_slot.shape[0], dtype=jnp.int32)
    slot_ids = jnp.sum(
        jnp.where(adapter_of[:, None] == adapter_ids[None, :], adapter_slot[None, :], 0), axis=1
    )
    column_slot = jnp.arange(lowered.shape[1], dtype=jnp.int32) // RANK
    local_slot = slot_ids - own_shard * (lowered.shape[1] // RANK)
    low_rank = jnp.where(
        local_slot[:, None] == column_slot[None, :], lowered, jnp.zeros_like(lowered)
    )
    out_blocks, up_blocks = out_weight, adapter_up
    summed, best = mp_exchange(
        attended, low_rank, out_blocks, up_blocks, residual, vocab_blocks, groups
    )
    max_logits = best[0]
    return (summed, state_norms, max_logits)


def solution(mesh):
    placed = (
        P("group", None),
        P(),
        P(None, "mp"),
        P("mp", None),
        P(None, "mp"),
        P("mp", None),
        P(("group", "mp"), None),
        P("group"),
        P(),
        P(),
        P(),
    )
    return jax.shard_map(
        on_device,
        mesh=mesh,
        in_specs=placed,
        out_specs=(P("group", "mp"), P("mp", "group"), P(("group", "mp"))),
        check_vma=False,
    )
```
